32 devices in a mesh: region: 2 (over y), tx: 4 (over z), ty: 2 (over x), band: 2 (over core).
Axes of the slice: x: 2, y: 2, z: 4, core: 2. Of those that a mesh axis runs over, the one named last changes fastest.
Arguments:
- scenes: bfloat16 [4, 256, 12, 256], P(('region', 'ty'), 'tx', 'band'), parts along dimension 0, may hold values from -6 to 6
- cloud: bfloat16 [4, 256, 256], P(('region', 'ty'), 'tx'), parts along dimension 0, may hold values from 0.049804688 to 1
- destination: int32 [4, 256], P(('region', 'ty'), 'tx'), parts along dimension 0, may hold values from 0 to 3, as said below
- offset: int32 [4, 256], P(('region', 'ty'), 'tx'), parts along dimension 0, may hold values from 0 to 63
- counts: int32 [4, 4], P(('region', 'ty'), 'tx'), parts along dimension 0, may hold values from 32 to 64
Outputs:
- composite: bfloat16 [12, 4, 128, 512], P('band', ('region', 'ty'), 'tx'), parts along dimension 1
The draws below stay inside these ranges and needn't reach their ends.
There are 2 independent parts, one for each index of `region`. The reference program is written for one: setup_inputs(seed, part) draws one part's arguments, and reference() takes and returns one part's arrays. A program takes and returns all parts, laid end to end along the dimension named above; each array names one. Nothing has to cross between parts.
Inputs may be any that keep to these rules, and one draw needn't show every extreme that they name: `destination`: among the 64 blocks of one device no tile row is named more than 32 times, and the first 32 blocks of every device in one column of tiles name one common tile row. `offset`: slots are numbered row by row, 8 slots to a row. A device's first counts blocks are live; its other blocks add nothing.
All inputs are finite; a program needn't handle non-finite values.
Results may differ from the reference program's by a relative error of at most 0.0025.
Values may be sent and summed in bfloat16 or wider, within the bound.
No kernel may reach another device: no remote copies, remote signals or barrier semaphores. Data moves between devices by JAX's collectives and lax.ppermute only.
A program may use at most 64 MiB of HBM per device.

```python
import math
import jax
import jax.numpy as jnp
from jax import lax

BANDS = 12
TS = 128
BS = 16
S_DEV = 64
LEVELS = 4
CAP = 32
SLOTS = 64
NR = 512
NC = 256
N_TX = 4
N_TY = 2


def draw_destination(key, part):
    folded = jax.random.fold_in(key, 7)
    key_star, key_rest = jax.random.split(folded)
    hot_rows = jax.random.randint(key_star, (N_TY,), 0, N_TX)
    hot_each = jnp.repeat(hot_rows, N_TX)
    subkeys = jax.random.split(key_rest, N_TY * N_TX)

    def one_device(subkey, hot_row):
        others = jnp.arange((N_TX - 1) * CAP, dtype=jnp.int32) // CAP
        others = others + (others >= hot_row).astype(jnp.int32)
        mixed = jax.random.permutation(subkey, others)
        leading = jnp.full((CAP,), hot_row, jnp.int32)
        return jnp.concatenate([leading, mixed[:S_DEV - CAP]])
    table = jax.vmap(one_device)(subkeys, hot_each)
    return table.reshape(N_TY, N_TX * S_DEV).astype(jnp.int32)


def plant(array, key, least, high):
    index_at = [jax.random.randint(jax.random.fold_in(key, axis), (), 0, length) for axis, length in enumerate(array.shape)]
    longest = array.shape.index(max(array.shape))
    beside = index_at[:longest] + [(index_at[longest] + 1) % array.shape[longest]] + index_at[longest + 1:]
    return array.at[tuple(index_at)].set(least).at[tuple(beside)].set(high)


def shard_levels(stream_key, shape, cuts, least, largest):
    loudness, own = 1.0, jax.random.fold_in(stream_key, 6)
    for axis_at, blocks in cuts:
        steps = jnp.exp(jax.random.uniform(jax.random.fold_in(own, axis_at), (blocks,), jnp.float32, least / len(cuts), largest / len(cuts)))
        loudness = loudness * jnp.repeat(steps, shape[axis_at] // blocks).reshape([-1 if axis == axis_at else 1 for axis in range(len(shape))])
    return loudness


def normal_values(rng, shape, scale, bound, cuts=(), held_as=jnp.bfloat16):
    array = scale * jax.random.normal(rng, shape, jnp.float32)
    if cuts:
        array = array * shard_levels(rng, shape, cuts, -0.22, 0.18)
    return jnp.clip(array, -bound, bound).astype(held_as)


def setup_inputs(seed: int = 0, part: int = 0) -> dict:
    seeds = jax.random.split(jax.random.key(seed), 6)
    own_keys = jax.random.split(jax.random.fold_in(seeds[5], part), 6)
    return {
        "scenes": normal_values(own_keys[0], (N_TY, N_TX * S_DEV, BANDS, BS * BS), 1.0, 6.0, ((0, 2), (1, 4), (2, 2))),
        "cloud": jnp.clip(jnp.exp(math.log(1.0) - 2.9996462 * jax.random.uniform(own_keys[1], (N_TY, N_TX * S_DEV, BS * BS), jnp.float32) ** shard_levels(own_keys[1], (N_TY, N_TX * S_DEV, BS * BS), ((0, 2), (1, 4)), -0.2, 0.2)), 0.049804688, 1.0).astype(jnp.bfloat16),
        "destination": draw_destination(jax.random.fold_in(jax.random.fold_in(seeds[5], part), 71), part),
        "offset": plant(jax.random.randint(own_keys[3], (N_TY, N_TX * S_DEV), 0, SLOTS), jax.random.fold_in(own_keys[3], 1), 0, SLOTS - 1).astype(jnp.int32),
        "counts": plant(jax.random.randint(own_keys[4], (N_TY, N_TX), CAP, S_DEV + 1), jax.random.fold_in(own_keys[4], 1), CAP, S_DEV).astype(jnp.int32),
    }


BINOMIAL = (0.0625, 0.25, 0.375, 0.25, 0.0625)
BACKGROUND = 0.25


def shrink_axis(field, along, rim_in, rim_out):
    length = field.shape[along]
    extent = length - 2 * rim_in
    outputs = extent // 2 + 2 * rim_out
    first_index = rim_in - 2 - 2 * rim_out
    running = None
    for tap_index, tap_weight in enumerate(BINOMIAL):
        begin = first_index + tap_index
        piece = lax.slice_in_dim(field, begin, begin + 2 * (outputs - 1) + 1, 2, along)
        running = tap_weight * piece if running is None else running + tap_weight * piece
    return running


def shrink(field, rim_in, rim_out):
    rows_done = shrink_axis(field, field.ndim - 2, rim_in, rim_out)
    return shrink_axis(rows_done, field.ndim - 1, rim_in, rim_out)


def grow_axis(field, along, rim_in, rim_out):
    length = field.shape[along]
    before = lax.slice_in_dim(field, 0, length - 2, 1, along)
    middle = lax.slice_in_dim(field, 1, length - 1, 1, along)
    behind = lax.slice_in_dim(field, 2, length, 1, along)
    at_even = (before + 6.0 * middle + behind) * 0.125
    at_odd = (middle + behind) * 0.5
    paired = jnp.stack([at_even, at_odd], axis=along + 1)
    new_shape = list(middle.shape)
    new_shape[along] = new_shape[along] * 2
    paired = paired.reshape(new_shape)
    excess = 2 * rim_in - 2 - rim_out
    return lax.slice_in_dim(paired, excess, new_shape[along] - excess, 1, along)


def grow(field, rim_in, rim_out):
    rows_done = grow_axis(field, field.ndim - 2, rim_in, rim_out)
    return grow_axis(rows_done, field.ndim - 1, rim_in, rim_out)


def pad_edges(field, depth):
    widths = [(0, 0)] * (field.ndim - 2) + [(depth, depth), (depth, depth)]
    return jnp.pad(field, widths)


def reference(scenes, cloud, destination, offset, counts):
    per_row = TS // BS
    blocks_all = N_TX * S_DEV
    living = (jnp.arange(S_DEV, dtype=jnp.int32)[None, None, :] < counts[:, :, None]).reshape(N_TY, blocks_all)
    coverage = cloud.astype(jnp.float32) * living[:, :, None].astype(jnp.float32)
    weighted = scenes.astype(jnp.float32) * coverage[:, :, None, :]
    top_row = destination * TS + (offset // per_row) * BS
    left_col = jnp.arange(N_TY, dtype=jnp.int32)[:, None] * TS + (offset % per_row) * BS
    offsets_in = jnp.arange(BS, dtype=jnp.int32)
    rows = top_row[:, :, None, None] + offsets_in[None, None, :, None]
    cols = left_col[:, :, None, None] + offsets_in[None, None, None, :]
    rows = jnp.broadcast_to(rows, (N_TY, blocks_all, BS, BS))
    cols = jnp.broadcast_to(cols, (N_TY, blocks_all, BS, BS))
    values = weighted.reshape(N_TY, blocks_all, BANDS, BS, BS).transpose(2, 0, 1, 3, 4)
    total = jnp.zeros((BANDS, NR, NC), jnp.float32).at[:, rows, cols].add(values)
    weight_sum = jnp.zeros((NR, NC), jnp.float32).at[rows, cols].add(coverage.reshape(N_TY, blocks_all, BS, BS))
    stacked = jnp.concatenate([total, weight_sum[None]], axis=0)
    pyramid = [stacked]
    for tier_index in range(1, LEVELS):
        pyramid.append(shrink(pad_edges(pyramid[-1], 2), 2, 0))
    summit = pyramid[-1]
    collapsed = summit[:BANDS] / (BACKGROUND + summit[BANDS])
    for tier_index in range(LEVELS - 2, -1, -1):
        current = pyramid[tier_index]
        coarser = pyramid[tier_index + 1]
        detail = current[:BANDS] - grow(pad_edges(coarser[:BANDS], 1), 1, 0)
        band_part = detail / (BACKGROUND + current[BANDS])
        collapsed = band_part + grow(pad_edges(collapsed, 1), 1, 0)
    blended = collapsed.astype(jnp.bfloat16)
    return blended.reshape(BANDS, NR, N_TY, TS).transpose(0, 2, 3, 1)
```

```python
import functools

import jax
import jax.numpy as jnp
import numpy as np
from jax import lax
from jax.experimental import pallas as pl
from jax.experimental.pallas import tpu as pltpu
from jax.sharding import PartitionSpec as P

TS = 128
BS = 16
S_DEV = 64
MARGIN = 32
LEVELS = 4
SLOTS = 64


BINOMIAL = (0.0625, 0.25, 0.375, 0.25, 0.0625)
BACKGROUND = 0.25


def with_halo(shard, sides, width):
    for axis, dim in sides:
        devices, length = (lax.axis_size(axis), shard.shape[dim])
        up = [(i, (i + 1) % devices) for i in range(devices - 1)]
        down = [(j, i) for i, j in up]
        last = lax.slice_in_dim(shard, length - width, length, axis=dim)
        leading = lax.slice_in_dim(shard, 0, width, axis=dim)
        before = lax.ppermute(last, axis, up)
        after = lax.ppermute(leading, axis, down)
        shard = jnp.concatenate([before, shard, after], axis=dim)
    return shard


def shrink_table(length, rim_in, rim_out):
    extent = length - 2 * rim_in
    outputs = extent // 2 + 2 * rim_out
    first_index = rim_in - 2 - 2 * rim_out
    out_pos = jnp.arange(outputs, dtype=jnp.int32)[:, None]
    in_pos = jnp.arange(length, dtype=jnp.int32)[None, :]
    spacing = in_pos - first_index - 2 * out_pos
    table = jnp.zeros((outputs, length), jnp.float32)
    for tap_index, tap_weight in enumerate(BINOMIAL):
        table = table + tap_weight * (spacing == tap_index).astype(jnp.float32)
    return table


def grow_table(length, rim_in, rim_out):
    excess = 2 * rim_in - 2 - rim_out
    outputs = 2 * (length - 2) - 2 * excess
    paired = jnp.arange(outputs, dtype=jnp.int32)[:, None] + excess
    source = paired // 2
    parity = paired % 2
    spacing = jnp.arange(length, dtype=jnp.int32)[None, :] - source
    even_part = (
        0.125 * (spacing == 0).astype(jnp.float32)
        + 0.75 * (spacing == 1).astype(jnp.float32)
        + 0.125 * (spacing == 2).astype(jnp.float32)
    )
    odd_part = 0.5 * (spacing == 1).astype(jnp.float32) + 0.5 * (spacing == 2).astype(jnp.float32)
    return jnp.where(parity == 0, even_part, odd_part)


def apply_both(field, row_table, col_table):
    rows_done = jnp.einsum("ki,bic->bkc", row_table, field, precision=lax.Precision.HIGHEST)
    return jnp.einsum("bkc,mc->bkm", rows_done, col_table, precision=lax.Precision.HIGHEST)


def shrink(field, rim_in, rim_out):
    row_table = shrink_table(field.shape[-2], rim_in, rim_out)
    col_table = shrink_table(field.shape[-1], rim_in, rim_out)
    return apply_both(field, row_table, col_table)


def grow(field, rim_in, rim_out):
    row_table = grow_table(field.shape[-2], rim_in, rim_out)
    col_table = grow_table(field.shape[-1], rim_in, rim_out)
    return apply_both(field, row_table, col_table)


def trim(field, rim_have, rim_want):
    excess = rim_have - rim_want
    return field[..., excess : field.shape[-2] - excess, excess : field.shape[-1] - excess]


def border(extent, rim, begin, whole):
    position = begin - rim + jnp.arange(extent + 2 * rim, dtype=jnp.int32)
    return ((position >= 0) & (position < whole)).astype(jnp.float32)


def local(scenes, cloud, destination, offset, counts):
    row_tiles = lax.axis_size("tx")
    col_tiles = lax.axis_size("ty")
    row_tile = lax.axis_index("tx")
    col_tile = lax.axis_index("ty")
    spread = max(2, 2 * S_DEV // row_tiles)
    blocks = scenes[0]
    weights = cloud[0]
    target_row = destination[0]
    placed = offset[0]
    live_count = counts[0, 0]
    own_bands = blocks.shape[1]
    living = jnp.arange(S_DEV, dtype=jnp.int32) < live_count
    matches = (target_row[:, None] == jnp.arange(row_tiles, dtype=jnp.int32)[None, :]) & living[
        :, None
    ]
    ordinal = jnp.cumsum(matches.astype(jnp.int32), axis=0) - 1
    ranking = jnp.sum(jnp.where(matches, ordinal, 0), axis=1)
    target = target_row * spread + ranking
    chooser = (
        (jnp.arange(row_tiles * spread, dtype=jnp.int32)[:, None] == target[None, :])
        & living[None, :]
    ).astype(jnp.bfloat16)
    merged = jnp.concatenate([blocks, weights[:, None, :]], axis=1).reshape(
        S_DEV, (own_bands + 1) * BS * BS
    )
    packed = jnp.dot(chooser, merged, preferred_element_type=jnp.float32).astype(jnp.bfloat16)
    packed = packed.reshape(row_tiles, spread, own_bands + 1, BS * BS)
    slot_ids = jnp.arange(SLOTS, dtype=jnp.int32)
    tag_send = jnp.dot(
        chooser, (placed + 1).astype(jnp.bfloat16)[:, None], preferred_element_type=jnp.float32
    )
    tag_send = tag_send.astype(jnp.bfloat16).reshape(row_tiles, spread)
    arrived, tag_back = (
        lax.all_to_all(packed, "tx", split_axis=0, concat_axis=0, tiled=True),
        lax.all_to_all(tag_send, "tx", split_axis=0, concat_axis=0, tiled=True),
    )
    landing = (slot_ids + 1).astype(jnp.float32)[:, None] == tag_back.reshape(-1).astype(
        jnp.float32
    )[None, :]
    arrived = arrived.reshape(row_tiles * spread, own_bands + 1, BS * BS)
    coverage = arrived[:, own_bands:].astype(jnp.float32)
    payload = jnp.concatenate(
        [arrived[:, :own_bands].astype(jnp.float32) * coverage, coverage], axis=1
    )
    payload = payload.reshape(row_tiles * spread, (own_bands + 1) * BS * BS)
    slot_sums = jnp.dot(landing.astype(jnp.float32), payload, precision=lax.Precision.HIGHEST)
    per_row = TS // BS
    tile_field = slot_sums.reshape(per_row, per_row, own_bands + 1, BS, BS).transpose(2, 0, 3, 1, 4)
    tile_field = tile_field.reshape(own_bands + 1, TS, TS)

    def masked(field, extent, rim):
        row_mask = border(extent, rim, row_tile * extent, extent * row_tiles)
        col_mask = border(extent, rim, col_tile * extent, extent * col_tiles)
        return field * row_mask[:, None] * col_mask[None, :]

    def enlarge(field, rim_in, rim_out):
        return grow(field, rim_in, rim_out)

    ground = with_halo(tile_field, (("tx", 1), ("ty", 2)), MARGIN)
    margin = MARGIN
    needed = [0]
    for tier_index in range(1, LEVELS):
        needed.append((needed[-1] + 3) // 2)
    pyramid = [(ground, margin)]
    extent = TS
    for tier_index in range(1, LEVELS):
        source, rim_in = pyramid[-1]
        rim_out = (rim_in - 2) // 2
        extent = extent // 2
        reduced = masked(shrink(source, rim_in, rim_out), extent, rim_out)
        pyramid.append((reduced, rim_out))
    deepest = LEVELS - 1
    summit, rim_top = pyramid[-1]
    summit = trim(summit, rim_top, needed[deepest])
    collapsed = summit[:own_bands] / (BACKGROUND + summit[own_bands])
    for tier_index in range(LEVELS - 2, -1, -1):
        current, rim_here = pyramid[tier_index]
        coarser, rim_below = pyramid[tier_index + 1]
        current = trim(current, rim_here, needed[tier_index])
        detail = current[:own_bands] - enlarge(coarser[:own_bands], rim_below, needed[tier_index])
        band_part = detail / (BACKGROUND + current[own_bands])
        collapsed = band_part + enlarge(collapsed, needed[tier_index + 1], needed[tier_index])
        collapsed = masked(collapsed, TS >> tier_index, needed[tier_index])
    blended = collapsed.astype(jnp.bfloat16)
    flipped = jnp.swapaxes(blended, 1, 2)
    strips = lax.all_to_all(flipped, "tx", split_axis=1, concat_axis=2, tiled=True)
    return strips[:, None]


BF = jnp.bfloat16
F32 = jnp.float32
EDGE = 3


def up8(v):
    return -(-v // 8) * 8


def shrink_grid(length):
    table = np.zeros((length // 2, length))
    for i in range(length // 2):
        for tap, weight in enumerate(BINOMIAL):
            k = 2 * i + tap - 2
            if 0 <= k < length:
                table[i, k] += weight
    return table


def grow_grid(length):
    table = np.zeros((2 * length, length))
    for i in range(length):
        for k, weight in ((i - 1, 0.125), (i, 0.75), (i + 1, 0.125)):
            if 0 <= k < length:
                table[2 * i, k] += weight
        for k in (i, i + 1):
            if k < length:
                table[2 * i + 1, k] += 0.5
    return table


def split_table(table):
    high = table.astype(BF)
    return high, (table - high.astype(np.float64)).astype(BF)


def row_shrinks(rows):
    tables, current = [], np.eye(rows)
    for level in range(1, LEVELS):
        current = shrink_grid(rows >> (level - 1)) @ current
        tables.append(current)
    return tables


class Plan:
    def __init__(self, n, m, bands):
        self.n, self.m, self.bands = n, m, bands
        self.rows = n * TS
        self.strip = TS // n
        self.slots = n * SLOTS
        self.slot_rows = n * (TS // BS)
        w = self.strip
        self.held = [w, w // 2 + 2, w // 4 + 3, w // 8 + 3]
        self.size = [w] + [up8(h) for h in self.held[1:]]
        self.first = [0, -1, -1, -1]
        self.at = [0]
        for size in self.size:
            self.at.append(self.at[-1] + size)
        self.edge_at = [None] + [self.at[LEVELS] + 8 * k for k in range(LEVELS - 1)]
        self.main = self.at[LEVELS] + 8 * (LEVELS - 1)
        self.low_at = self.main
        self.low_edge_at = self.main + self.size[3]
        self.total = self.main + self.size[3] + 8

    def column_tables(self):
        n, m, w = self.n, self.m, self.strip
        width = m * TS
        grids = [np.eye(width)] + row_shrinks(width)
        tables = np.zeros((n, m, self.total, TS))
        for t in range(n):
            for j in range(m):
                for level in range(LEVELS):
                    base = ((j * TS + t * w) >> level) + self.first[level]
                    for k in range(self.held[level]):
                        o = base + k
                        if 0 <= o < width >> level:
                            tables[t, j, self.at[level] + k] = grids[level][o, j * TS : (j + 1) * TS]
                    if level == 0:
                        continue
                    if 2 * t < n:
                        base = ((j + 1) * TS >> level) - 1
                    else:
                        base = (j * TS >> level) - 1
                    for k in range(EDGE):
                        o = base + k
                        if 0 <= o < width >> level:
                            tables[t, j, self.edge_at[level] + k] = grids[level][o, j * TS : (j + 1) * TS]
        high, low = split_table(tables)
        high[:, :, self.low_at : self.low_at + self.size[3]] = low[:, :, self.at[3] : self.at[4]]
        edge = self.edge_at[3]
        high[:, :, self.low_edge_at : self.low_edge_at + 8] = low[:, :, edge : edge + 8]
        return np.concatenate([high, high], axis=-1).reshape(n * m, self.total, 2 * TS)


def halves(value):
    high = value.astype(BF)
    return high, (value - high.astype(F32)).astype(BF)


def dot2(value, table):
    high, low = halves(value)
    return jnp.dot(high, table, preferred_element_type=F32) + jnp.dot(
        low, table, preferred_element_type=F32
    )


def note_kernel(plan, count_ref, cloud_ref, dest_ref, offset_ref, out_ref):
    out_ref[:S_DEV, :] = cloud_ref[...]
    per_row = TS // BS
    offset = offset_ref[...]
    code = (offset % per_row) * plan.slot_rows + dest_ref[...] * per_row + offset // per_row
    live = lax.broadcasted_iota(jnp.int32, (1, S_DEV), 1) < count_ref[0, 0]
    code = jnp.where(live, code, -1).astype(F32)
    tail = out_ref.shape[0] - S_DEV
    out_ref[S_DEV:, :] = jnp.full((tail, BS * BS), -1.0, BF)
    out_ref[S_DEV:, :S_DEV] = jnp.broadcast_to(code, (tail, S_DEV)).astype(BF)


def place_kernel(plan, *refs):
    n, bands = plan.n, plan.bands
    scenes, notes = refs[:n], refs[n : 2 * n]
    column_ref, row1_ref, row2_ref, row3_ref, a0_ref, a1_ref, a2_ref, a3_ref, edge_ref = refs[
        2 * n : 2 * n + 9
    ]
    prod_ref, tile_ref, z1_ref, z2_ref, z3_ref = refs[2 * n + 9 :]
    blocks = n * S_DEV
    area = BS * BS
    codes = notes[0][S_DEV : S_DEV + 16, :].astype(F32)
    for p in range(1, n):
        codes = jnp.maximum(
            codes, pltpu.roll(notes[p][S_DEV : S_DEV + 16, :].astype(F32), S_DEV * p, 1)
        )
    codes = codes[:1, :blocks]
    slot = lax.broadcasted_iota(jnp.int32, (plan.slots, blocks), 0).astype(F32)
    landing = jnp.where(slot == codes, 1.0, 0.0).astype(BF)
    landing2 = jnp.concatenate([landing, landing], axis=1)
    group = lax.broadcasted_iota(jnp.int32, (plan.slot_rows, TS), 1) // BS
    per_row = TS // BS
    column = column_ref[...]
    e1 = plan.size[1]
    for f in range(bands + 1):
        for p in range(n):
            weight = notes[p][:S_DEV, :]
            at = pl.ds(p * S_DEV, S_DEV)
            if f == bands:
                prod_ref[at, :] = weight
            else:
                value = scenes[p][f].astype(F32) * weight.astype(F32)
                high, low = halves(value)
                prod_ref[at, :] = high
                prod_ref[pl.ds(blocks + p * S_DEV, S_DEV), :] = low
        if f == bands:
            sums = jnp.dot(landing, prod_ref[:blocks, :], preferred_element_type=F32)
        else:
            sums = jnp.dot(landing2, prod_ref[...], preferred_element_type=F32)
        for half in range(area // TS):
            part = [
                sums[b * plan.slot_rows : (b + 1) * plan.slot_rows, half * TS : (half + 1) * TS]
                for b in range(per_row)
            ]
            step = per_row // 2
            while step:
                odd = (group & step) != 0
                for i in range(per_row):
                    if i & step:
                        continue
                    a, b = part[i], part[i + step]
                    part[i] = jnp.where(odd, pltpu.roll(b, step * BS, 1), a)
                    part[i + step] = jnp.where(odd, b, pltpu.roll(a, TS - step * BS, 1))
                step //= 2
            for r in range(per_row):
                tile_ref[pl.ds(half * per_row + r, plan.slot_rows, stride=BS), :] = part[r]
        high, low = halves(tile_ref[...])
        tile = jnp.concatenate([high, low], axis=1)
        cols = lax.dot_general(
            column, tile, (((1,), (1,)), ((), ())), preferred_element_type=F32
        )
        at, size, edge = plan.at, plan.size, plan.edge_at
        a0_ref[f] = cols[at[0] : at[1]]
        z1_ref[f, : size[1]] = cols[at[1] : at[2]]
        z1_ref[f, size[1] :] = cols[edge[1] : edge[1] + 8]
        z2_ref[f, : size[2]] = cols[at[2] : at[3]]
        z2_ref[f, size[2] :] = cols[edge[2] : edge[2] + 8]
        z3_ref[f, : size[3]] = (
            cols[at[3] : at[4]] + cols[plan.low_at : plan.low_at + size[3]]
        )
        z3_ref[f, size[3] :] = (
            cols[edge[3] : edge[3] + 8] + cols[plan.low_edge_at : plan.low_edge_at + 8]
        )
    planes = bands + 1
    rows = plan.rows
    z1 = dot2(z1_ref[...].reshape(planes * (size[1] + 8), rows), row1_ref[...])
    z2 = dot2(z2_ref[...].reshape(planes * (size[2] + 8), rows), row2_ref[...])
    z3 = z3_ref[...].reshape(planes * (size[3] + 8), rows)
    z3 = dot2(z3, row3_ref[0]) + jnp.dot(
        z3.astype(BF), row3_ref[1], preferred_element_type=F32
    )
    start = 0
    edge_ref[...] = jnp.zeros(edge_ref.shape, F32)
    for z, out_ref, level in ((z1, a1_ref, 1), (z2, a2_ref, 2), (z3, a3_ref, 3)):
        lanes = z.shape[-1]
        z = z.reshape(planes, size[level] + 8, lanes)
        out_ref[...] = z[:, : size[level]]
        for f in range(planes):
            edge_ref[pl.ds(EDGE * f, EDGE), start : start + lanes] = z[
                f, size[level] : size[level] + EDGE
            ]
        start += lanes


def grow_columns(value, outputs):
    half = outputs // 2
    a, b, c = value[:, :half], value[:, 1 : half + 1], value[:, 2 : half + 2]
    return (a + b) * 0.5, (a + 6.0 * b + c) * 0.125


def weave(even, odd, ref, size):
    k, half, lanes = even.shape
    if 2 * half < size:
        ref[...] = jnp.zeros(ref.shape, F32)
    for q in range(k):
        for chunk in range(lanes // TS):
            part = slice(chunk * TS, (chunk + 1) * TS)
            ref[q, chunk, pl.ds(0, half, stride=2), :] = even[q][:, part]
            ref[q, chunk, pl.ds(1, half, stride=2), :] = odd[q][:, part]
    return jnp.concatenate([ref[:, chunk] for chunk in range(lanes // TS)], axis=-1)


def blend_kernel(plan, flag_ref, a0_ref, a1_ref, a2_ref, a3_ref, edge_ref, grow1_ref, grow2_ref, grow3_ref,
                 out_ref, g1_ref, g2_ref, g3_ref, e2_ref, e1_ref, e0_ref):
    bands = plan.bands
    planes = bands + 1
    w = plan.strip
    left, right = flag_ref[0], flag_ref[1]
    start = 0
    for level, (src, dst) in enumerate(((a1_ref, g1_ref), (a2_ref, g2_ref), (a3_ref, g3_ref)), 1):
        lanes = src.shape[-1]
        dst[...] = src[...]
        for f in range(planes):
            edge = edge_ref[pl.ds(EDGE * f, EDGE), start : start + lanes]
            far = w >> level
            dst[f, :EDGE] += jnp.where(left > 0, edge, 0.0)
            dst[f, far : far + EDGE] += jnp.where(right > 0, edge, 0.0)
        start += lanes
    first = flag_ref[2]
    last = flag_ref[3]

    def inside(level, columns):
        column = lax.broadcasted_iota(jnp.int32, (columns, 1), 0) - 1
        keep = ((column >= 0) | (first == 0)) & ((column < (w >> level)) | (last == 0))
        return keep.astype(F32)

    top = g3_ref[...]
    blend = top[:bands] / (BACKGROUND + top[bands:])
    for level, cur_ref, below_ref, grow_ref, up_ref in (
        (2, g2_ref, g3_ref, grow3_ref, e2_ref),
        (1, g1_ref, g2_ref, grow2_ref, e1_ref),
    ):
        stacked = jnp.concatenate([below_ref[:bands], blend], axis=0)
        k, c, r = stacked.shape
        wide = dot2(stacked.reshape(k * c, r), grow_ref[...])
        wide = wide.reshape(k, c, wide.shape[-1])
        pairs = up8(plan.held[level]) // 2
        pairs = min(pairs, c - 2)
        even, odd = grow_columns(wide, 2 * pairs)
        size = cur_ref.shape[1]
        up = weave(even, odd, up_ref, size)
        current = cur_ref[...]
        inverse = 1.0 / (BACKGROUND + current[bands])
        blend = (current[:bands] - up[:bands]) * inverse + up[bands:]
        blend = blend * inside(level, blend.shape[1])
    stacked = jnp.concatenate([g1_ref[:bands], blend], axis=0)
    k, c, r = stacked.shape
    wide = dot2(stacked.reshape(k * c, r), grow1_ref[...]).reshape(k, c, plan.rows)
    half = w // 2
    a, b, c = wide[:, :half], wide[:, 1 : half + 1], wide[:, 2 : half + 2]
    even, odd = (a + 6.0 * b + c) * 0.125, (b + c) * 0.5
    up = weave(even, odd, e0_ref, w)
    inverse = 1.0 / (BACKGROUND + a0_ref[bands])
    for f in range(bands):
        value = (a0_ref[f] - up[f]) * inverse + up[bands + f]
        out_ref[f] = value.astype(BF)


def strip_local(scenes, cloud, destination, offset, counts):
    n, m = lax.axis_size("tx"), lax.axis_size("ty")
    row_tile, col_tile = lax.axis_index("tx"), lax.axis_index("ty")
    bands = scenes.shape[2]
    plan = Plan(n, m, bands)
    planes = bands + 1
    area = BS * BS
    vmem = pl.BlockSpec(memory_space=pltpu.VMEM)
    smem = pl.BlockSpec(memory_space=pltpu.SMEM)
    blocks = jnp.swapaxes(scenes[0], 0, 1)
    note = pl.pallas_call(
        functools.partial(note_kernel, plan),
        out_shape=jax.ShapeDtypeStruct((S_DEV + 16, area), BF),
        in_specs=[smem, vmem, vmem, vmem],
        out_specs=vmem,
        name="note",
    )(counts, cloud[0], destination, offset)

    def swap(value, mask):
        return lax.ppermute(value, "tx", [(i, i ^ mask) for i in range(n)])

    gathered = [(blocks, note)]
    mask = 1
    masks = []
    while mask < n:
        masks.append(2 * mask - 1)
        mask *= 2
    for mask in masks:
        gathered = gathered + [(swap(b, mask), swap(s, mask)) for b, s in gathered]

    column = lax.dynamic_index_in_dim(
        jnp.asarray(plan.column_tables()), row_tile * m + col_tile, keepdims=False
    )
    shrinks = row_shrinks(plan.rows)
    row1 = jnp.asarray(shrinks[0].T.astype(BF))
    row2 = jnp.asarray(shrinks[1].T.astype(BF))
    top = plan.rows >> 3
    wide_top = max(top, 128)
    padded = np.zeros((plan.rows, wide_top))
    padded[:, :top] = shrinks[2].T
    row3 = jnp.asarray(np.stack(split_table(padded)))
    size = plan.size
    shapes = [
        (planes, size[0], plan.rows),
        (planes, size[1], plan.rows >> 1),
        (planes, size[2], plan.rows >> 2),
        (planes, size[3], wide_top),
    ]
    edge_lanes = sum(s[-1] for s in shapes[1:])
    edge_shape = (up8(EDGE * planes), edge_lanes)
    a0, a1, a2, a3, edge = pl.pallas_call(
        functools.partial(place_kernel, plan),
        out_shape=[jax.ShapeDtypeStruct(s, F32) for s in shapes + [edge_shape]],
        in_specs=[vmem] * (2 * n + 4),
        out_specs=[vmem] * 5,
        scratch_shapes=[
            pltpu.VMEM((2 * n * S_DEV, area), BF),
            pltpu.VMEM((plan.rows, TS), F32),
            pltpu.VMEM((planes, size[1] + 8, plan.rows), F32),
            pltpu.VMEM((planes, size[2] + 8, plan.rows), F32),
            pltpu.VMEM((planes, size[3] + 8, plan.rows), F32),
        ],
        name="place",
    )(*[b for b, _ in gathered], *[s for _, s in gathered], column, row1, row2, row3)

    pairs = []
    for t in range(n):
        for j in range(m):
            other = (j + 1) % m if 2 * t < n else (j - 1) % m
            pairs.append((t * m + j, t * m + other))
    edge = lax.ppermute(edge, ("tx", "ty"), pairs)

    first, last = row_tile == 0, row_tile == n - 1
    flags = jnp.stack(
        [first & (col_tile > 0), last & (col_tile < m - 1), first & (col_tile == 0), last & (col_tile == m - 1)]
    ).astype(jnp.int32)
    grow3 = np.zeros((wide_top, plan.rows >> 2))
    grow3[:top] = grow_grid(top).T
    grow2 = grow_grid(plan.rows >> 2).T
    grow1 = grow_grid(plan.rows >> 1).T
    out = pl.pallas_call(
        functools.partial(blend_kernel, plan),
        out_shape=jax.ShapeDtypeStruct((bands, size[0], plan.rows), BF),
        in_specs=[smem] + [vmem] * 8,
        out_specs=vmem,
        scratch_shapes=[
            pltpu.VMEM(shapes[1], F32),
            pltpu.VMEM(shapes[2], F32),
            pltpu.VMEM(shapes[3], F32),
            pltpu.VMEM((2 * bands, (plan.rows >> 2) // TS, size[2], TS), F32),
            pltpu.VMEM((2 * bands, (plan.rows >> 1) // TS, size[1], TS), F32),
            pltpu.VMEM((2 * bands, plan.rows // TS, size[0], TS), F32),
        ],
        name="blend",
    )(
        flags, a0, a1, a2, a3, edge,
        jnp.asarray(grow1.astype(BF)), jnp.asarray(grow2.astype(BF)), jnp.asarray(grow3.astype(BF)),
    )
    return out[:, None]


def use_strips(n, m):
    power = n & (n - 1) == 0
    spread = max(2, 2 * S_DEV // n)
    return power and 2 <= n and TS // n >= 32 and m >= 2 and S_DEV <= 2 * spread


def solution(mesh):
    placed = (
        P(("region", "ty"), "tx", "band", None),
        P(("region", "ty"), "tx", None),
        P(("region", "ty"), "tx"),
        P(("region", "ty"), "tx"),
        P(("region", "ty"), "tx"),
    )
    body = strip_local if use_strips(mesh.shape["tx"], mesh.shape["ty"]) else local
    return jax.shard_map(
        body,
        mesh=mesh,
        in_specs=placed,
        out_specs=P("band", ("region", "ty"), "tx", None),
        check_vma=False,
    )
```

```python
import functools

import jax
import jax.numpy as jnp
import numpy as np
from jax import lax
from jax.experimental import pallas as pl
from jax.experimental.pallas import tpu as pltpu
from jax.sharding import PartitionSpec as P


TS = 128
BS = 16
S_DEV = 64
MARGIN = 32
LEVELS = 4
SLOTS = 64


BINOMIAL = (0.0625, 0.25, 0.375, 0.25, 0.0625)
BACKGROUND = 0.25


def with_halo(shard, sides, width):
    for axis, dim in sides:
        devices, length = (lax.axis_size(axis), shard.shape[dim])
        up = [(i, (i + 1) % devices) for i in range(devices - 1)]
        down = [(j, i) for i, j in up]
        last = lax.slice_in_dim(shard, length - width, length, axis=dim)
        leading = lax.slice_in_dim(shard, 0, width, axis=dim)
        before = lax.ppermute(last, axis, up)
        after = lax.ppermute(leading, axis, down)
        shard = jnp.concatenate([before, shard, after], axis=dim)
    return shard


def shrink_table(length, rim_in, rim_out):
    extent = length - 2 * rim_in
    outputs = extent // 2 + 2 * rim_out
    first_index = rim_in - 2 - 2 * rim_out
    out_pos = jnp.arange(outputs, dtype=jnp.int32)[:, None]
    in_pos = jnp.arange(length, dtype=jnp.int32)[None, :]
    spacing = in_pos - first_index - 2 * out_pos
    table = jnp.zeros((outputs, length), jnp.float32)
    for tap_index, tap_weight in enumerate(BINOMIAL):
        table = table + tap_weight * (spacing == tap_index).astype(jnp.float32)
    return table


def grow_table(length, rim_in, rim_out):
    excess = 2 * rim_in - 2 - rim_out
    outputs = 2 * (length - 2) - 2 * excess
    paired = jnp.arange(outputs, dtype=jnp.int32)[:, None] + excess
    source = paired // 2
    parity = paired % 2
    spacing = jnp.arange(length, dtype=jnp.int32)[None, :] - source
    even_part = (
        0.125 * (spacing == 0).astype(jnp.float32)
        + 0.75 * (spacing == 1).astype(jnp.float32)
        + 0.125 * (spacing == 2).astype(jnp.float32)
    )
    odd_part = 0.5 * (spacing == 1).astype(jnp.float32) + 0.5 * (spacing == 2).astype(jnp.float32)
    return jnp.where(parity == 0, even_part, odd_part)


def apply_both(field, row_table, col_table):
    rows_done = jnp.einsum("ki,bic->bkc", row_table, field, precision=lax.Precision.HIGHEST)
    return jnp.einsum("bkc,mc->bkm", rows_done, col_table, precision=lax.Precision.HIGHEST)


def shrink(field, rim_in, rim_out):
    row_table = shrink_table(field.shape[-2], rim_in, rim_out)
    col_table = shrink_table(field.shape[-1], rim_in, rim_out)
    return apply_both(field, row_table, col_table)


def grow(field, rim_in, rim_out):
    row_table = grow_table(field.shape[-2], rim_in, rim_out)
    col_table = grow_table(field.shape[-1], rim_in, rim_out)
    return apply_both(field, row_table, col_table)


def trim(field, rim_have, rim_want):
    excess = rim_have - rim_want
    return field[..., excess : field.shape[-2] - excess, excess : field.shape[-1] - excess]


def border(extent, rim, begin, whole):
    position = begin - rim + jnp.arange(extent + 2 * rim, dtype=jnp.int32)
    return ((position >= 0) & (position < whole)).astype(jnp.float32)


def local(scenes, cloud, destination, offset, counts):
    row_tiles = lax.axis_size("tx")
    col_tiles = lax.axis_size("ty")
    row_tile = lax.axis_index("tx")
    col_tile = lax.axis_index("ty")
    spread = max(2, 2 * S_DEV // row_tiles)
    blocks = scenes[0]
    weights = cloud[0]
    target_row = destination[0]
    placed = offset[0]
    live_count = counts[0, 0]
    own_bands = blocks.shape[1]
    living = jnp.arange(S_DEV, dtype=jnp.int32) < live_count
    matches = (target_row[:, None] == jnp.arange(row_tiles, dtype=jnp.int32)[None, :]) & living[
        :, None
    ]
    ordinal = jnp.cumsum(matches.astype(jnp.int32), axis=0) - 1
    ranking = jnp.sum(jnp.where(matches, ordinal, 0), axis=1)
    target = target_row * spread + ranking
    chooser = (
        (jnp.arange(row_tiles * spread, dtype=jnp.int32)[:, None] == target[None, :])
        & living[None, :]
    ).astype(jnp.bfloat16)
    merged = jnp.concatenate([blocks, weights[:, None, :]], axis=1).reshape(
        S_DEV, (own_bands + 1) * BS * BS
    )
    packed = jnp.dot(chooser, merged, preferred_element_type=jnp.float32).astype(jnp.bfloat16)
    packed = packed.reshape(row_tiles, spread, own_bands + 1, BS * BS)
    slot_ids = jnp.arange(SLOTS, dtype=jnp.int32)
    tag_send = jnp.dot(
        chooser, (placed + 1).astype(jnp.bfloat16)[:, None], preferred_element_type=jnp.float32
    )
    tag_send = tag_send.astype(jnp.bfloat16).reshape(row_tiles, spread)
    arrived, tag_back = (
        lax.all_to_all(packed, "tx", split_axis=0, concat_axis=0, tiled=True),
        lax.all_to_all(tag_send, "tx", split_axis=0, concat_axis=0, tiled=True),
    )
    landing = (slot_ids + 1).astype(jnp.float32)[:, None] == tag_back.reshape(-1).astype(
        jnp.float32
    )[None, :]
    arrived = arrived.reshape(row_tiles * spread, own_bands + 1, BS * BS)
    coverage = arrived[:, own_bands:].astype(jnp.float32)
    payload = jnp.concatenate(
        [arrived[:, :own_bands].astype(jnp.float32) * coverage, coverage], axis=1
    )
    payload = payload.reshape(row_tiles * spread, (own_bands + 1) * BS * BS)
    slot_sums = jnp.dot(landing.astype(jnp.float32), payload, precision=lax.Precision.HIGHEST)
    per_row = TS // BS
    tile_field = slot_sums.reshape(per_row, per_row, own_bands + 1, BS, BS).transpose(2, 0, 3, 1, 4)
    tile_field = tile_field.reshape(own_bands + 1, TS, TS)

    def masked(field, extent, rim):
        row_mask = border(extent, rim, row_tile * extent, extent * row_tiles)
        col_mask = border(extent, rim, col_tile * extent, extent * col_tiles)
        return field * row_mask[:, None] * col_mask[None, :]

    def enlarge(field, rim_in, rim_out):
        return grow(field, rim_in, rim_out)

    ground = with_halo(tile_field, (("tx", 1), ("ty", 2)), MARGIN)
    margin = MARGIN
    needed = [0]
    for _ in range(1, LEVELS):
        needed.append((needed[-1] + 3) // 2)
    pyramid = [(ground, margin)]
    extent = TS
    for _ in range(1, LEVELS):
        source, rim_in = pyramid[-1]
        rim_out = (rim_in - 2) // 2
        extent = extent // 2
        reduced = masked(shrink(source, rim_in, rim_out), extent, rim_out)
        pyramid.append((reduced, rim_out))
    deepest = LEVELS - 1
    summit, rim_top = pyramid[-1]
    summit = trim(summit, rim_top, needed[deepest])
    collapsed = summit[:own_bands] / (BACKGROUND + summit[own_bands])
    for tier_index in range(LEVELS - 2, -1, -1):
        current, rim_here = pyramid[tier_index]
        coarser, rim_below = pyramid[tier_index + 1]
        current = trim(current, rim_here, needed[tier_index])
        detail = current[:own_bands] - enlarge(coarser[:own_bands], rim_below, needed[tier_index])
        band_part = detail / (BACKGROUND + current[own_bands])
        collapsed = band_part + enlarge(collapsed, needed[tier_index + 1], needed[tier_index])
        collapsed = masked(collapsed, TS >> tier_index, needed[tier_index])
    blended = collapsed.astype(jnp.bfloat16)
    flipped = jnp.swapaxes(blended, 1, 2)
    strips = lax.all_to_all(flipped, "tx", split_axis=1, concat_axis=2, tiled=True)
    return strips[:, None]


BF = jnp.bfloat16
F32 = jnp.float32
EDGE = 3
CODE_ROWS = 8


def up8(v):
    return -(-v // 8) * 8


def shrink_grid(length):
    table = np.zeros((length // 2, length))
    for i in range(length // 2):
        for tap, weight in enumerate(BINOMIAL):
            k = 2 * i + tap - 2
            if 0 <= k < length:
                table[i, k] += weight
    return table


def grow_grid(length):
    table = np.zeros((2 * length, length))
    for i in range(length):
        for k, weight in ((i - 1, 0.125), (i, 0.75), (i + 1, 0.125)):
            if 0 <= k < length:
                table[2 * i, k] += weight
        for k in (i, i + 1):
            if k < length:
                table[2 * i + 1, k] += 0.5
    return table


def split_table(table):
    high = table.astype(BF)
    return high, (table - high.astype(np.float64)).astype(BF)


def row_shrinks(rows):
    tables, current = [], np.eye(rows)
    for level in range(1, LEVELS):
        current = shrink_grid(rows >> (level - 1)) @ current
        tables.append(current)
    return tables


class Plan:
    def __init__(self, n, m, bands):
        self.n, self.m, self.bands = n, m, bands
        self.rows = n * TS
        self.strip = TS // n
        self.slots = n * SLOTS
        self.slot_rows = n * (TS // BS)
        w = self.strip
        self.held = [w, w // 2 + 2, w // 4 + 3, w // 8 + 3]
        self.size = [w] + [up8(h) for h in self.held[1:]]
        self.first = [0, -1, -1, -1]
        self.at = [0]
        for size in self.size:
            self.at.append(self.at[-1] + size)
        self.edge_at = [None] + [self.at[LEVELS] + 8 * k for k in range(LEVELS - 1)]
        self.main = self.at[LEVELS] + 8 * (LEVELS - 1)
        self.low_at = self.main
        self.low_edge_at = self.main + self.size[3]
        self.total = self.main + self.size[3] + 8

    def column_tables(self):
        n, m, w = self.n, self.m, self.strip
        width = m * TS
        grids = [np.eye(width)] + row_shrinks(width)
        tables = np.zeros((n, m, self.total, TS))
        for t in range(n):
            for j in range(m):
                for level in range(LEVELS):
                    base = ((j * TS + t * w) >> level) + self.first[level]
                    for k in range(self.held[level]):
                        o = base + k
                        if 0 <= o < width >> level:
                            tables[t, j, self.at[level] + k] = grids[level][o, j * TS : (j + 1) * TS]
                    if level == 0:
                        continue
                    if 2 * t < n:
                        base = ((j + 1) * TS >> level) - 1
                    else:
                        base = (j * TS >> level) - 1
                    for k in range(EDGE):
                        o = base + k
                        if 0 <= o < width >> level:
                            tables[t, j, self.edge_at[level] + k] = grids[level][o, j * TS : (j + 1) * TS]
        high, low = split_table(tables)
        high[:, :, self.low_at : self.low_at + self.size[3]] = low[:, :, self.at[3] : self.at[4]]
        edge = self.edge_at[3]
        high[:, :, self.low_edge_at : self.low_edge_at + 8] = low[:, :, edge : edge + 8]
        return np.concatenate([high, high], axis=-1).reshape(n * m, self.total, 2 * TS)


def halves(value):
    high = value.astype(BF)
    return high, (value - high.astype(F32)).astype(BF)


def dot2(value, table):
    high, low = halves(value)
    return jnp.dot(high, table, preferred_element_type=F32) + jnp.dot(
        low, table, preferred_element_type=F32
    )


def pack_kernel(plan, count_ref, scenes_ref, cloud_ref, dest_ref, offset_ref, out_ref, dest, offset, sems):
    rows = plan.bands * S_DEV
    copies = [
        pltpu.make_async_copy(source, target, sems.at[k])
        for k, (source, target) in enumerate(
            (
                (dest_ref, dest),
                (offset_ref, offset),
                (cloud_ref, out_ref.at[pl.ds(rows, S_DEV)]),
                (scenes_ref, out_ref.at[pl.ds(0, rows)]),
            )
        )
    ]
    for copy in copies:
        copy.start()
    for copy in copies[:2]:
        copy.wait()
    per_row = TS // BS
    slot = offset[...]
    code = (slot % per_row) * plan.slot_rows + dest[...] * per_row + slot // per_row
    live = lax.broadcasted_iota(jnp.int32, (1, S_DEV), 1) < count_ref[0, 0]
    code = jnp.where(live, code, -1).astype(F32)
    rows += S_DEV
    tail = out_ref.shape[0] - rows
    out_ref[rows:, :] = jnp.full((tail, BS * BS), -1.0, BF)
    out_ref[rows:, :S_DEV] = jnp.broadcast_to(code, (tail, S_DEV)).astype(BF)
    for copy in copies[2:]:
        copy.wait()


def landing_of(plan, packs):
    tail = slice((plan.bands + 1) * S_DEV, (plan.bands + 1) * S_DEV + CODE_ROWS)
    codes = packs[0][tail, :].astype(F32)
    for p in range(1, len(packs)):
        codes = jnp.maximum(codes, pltpu.roll(packs[p][tail, :].astype(F32), S_DEV * p, 1))
    blocks = len(packs) * S_DEV
    slot = lax.broadcasted_iota(jnp.int32, (plan.slots, blocks), 0).astype(F32)
    landing = jnp.where(slot == codes[:1, :blocks], 1.0, 0.0).astype(BF)
    return jnp.concatenate([landing, landing], axis=1)


def slot_sums(plan, packs, landing2, prod_ref, f):
    blocks = len(packs) * S_DEV
    weights = pl.ds(plan.bands * S_DEV, S_DEV)
    for p, pack in enumerate(packs):
        weight = pack[weights, :]
        if f == plan.bands:
            prod_ref[pl.ds(p * S_DEV, S_DEV), :] = weight
            continue
        value = pack[f * S_DEV : (f + 1) * S_DEV, :].astype(F32) * weight.astype(F32)
        high, low = halves(value)
        prod_ref[pl.ds(p * S_DEV, S_DEV), :] = high
        prod_ref[pl.ds(blocks + p * S_DEV, S_DEV), :] = low
    used = blocks if f == plan.bands else 2 * blocks
    return jnp.dot(landing2[:, :used], prod_ref[:used, :], preferred_element_type=F32)


def sum_kernel(plan, count, *refs):
    packs, rest = refs[:count], refs[count:]
    before_ref = rest[0] if len(rest) == 3 else None
    out_ref, prod_ref = rest[-2:]
    landing2 = landing_of(plan, packs)
    for f in range(plan.bands + 1):
        sums = slot_sums(plan, packs, landing2, prod_ref, f)
        out_ref[f] = sums if before_ref is None else before_ref[f] + sums


def place_kernel(plan, count, *refs):
    bands = plan.bands
    packs = refs[:count]
    before_ref, column_ref, row1_ref, row2_ref, row3_ref = refs[count : count + 5]
    a0_ref, a1_ref, a2_ref, a3_ref, edge_ref = refs[count + 5 : count + 10]
    prod_ref, sums_ref, tile_ref, z1_ref, z2_ref, z3_ref = refs[count + 10 :]
    area = BS * BS
    landing2 = landing_of(plan, packs)
    group = lax.broadcasted_iota(jnp.int32, (plan.slot_rows, TS), 1) // BS
    per_row = TS // BS
    column = column_ref[...]
    for f in range(bands + 1):
        sums_ref[f] = before_ref[f] + slot_sums(plan, packs, landing2, prod_ref, f)
    for f in range(bands + 1):
        sums = sums_ref[f]
        for half in range(area // TS):
            part = [
                sums[b * plan.slot_rows : (b + 1) * plan.slot_rows, half * TS : (half + 1) * TS]
                for b in range(per_row)
            ]
            step = per_row // 2
            while step:
                odd = (group & step) != 0
                for i in range(per_row):
                    if i & step:
                        continue
                    a, b = part[i], part[i + step]
                    part[i] = jnp.where(odd, pltpu.roll(b, step * BS, 1), a)
                    part[i + step] = jnp.where(odd, b, pltpu.roll(a, TS - step * BS, 1))
                step //= 2
            for r in range(per_row):
                tile_ref[pl.ds(half * per_row + r, plan.slot_rows, stride=BS), :] = part[r]
        high, low = halves(tile_ref[...])
        tile = jnp.concatenate([high, low], axis=1)
        cols = lax.dot_general(
            column, tile, (((1,), (1,)), ((), ())), preferred_element_type=F32
        )
        at, size, edge = plan.at, plan.size, plan.edge_at
        a0_ref[f] = cols[at[0] : at[1]]
        z1_ref[f, : size[1]] = cols[at[1] : at[2]]
        z1_ref[f, size[1] :] = cols[edge[1] : edge[1] + 8]
        z2_ref[f, : size[2]] = cols[at[2] : at[3]]
        z2_ref[f, size[2] :] = cols[edge[2] : edge[2] + 8]
        z3_ref[f, : size[3]] = (
            cols[at[3] : at[4]] + cols[plan.low_at : plan.low_at + size[3]]
        )
        z3_ref[f, size[3] :] = (
            cols[edge[3] : edge[3] + 8] + cols[plan.low_edge_at : plan.low_edge_at + 8]
        )
    planes = bands + 1
    rows = plan.rows
    z1 = dot2(z1_ref[...].reshape(planes * (size[1] + 8), rows), row1_ref[...])
    z2 = dot2(z2_ref[...].reshape(planes * (size[2] + 8), rows), row2_ref[...])
    z3 = z3_ref[...].reshape(planes * (size[3] + 8), rows)
    z3 = dot2(z3, row3_ref[0]) + jnp.dot(
        z3.astype(BF), row3_ref[1], preferred_element_type=F32
    )
    start = 0
    edge_ref[...] = jnp.zeros(edge_ref.shape, F32)
    for z, out_ref, level in ((z1, a1_ref, 1), (z2, a2_ref, 2), (z3, a3_ref, 3)):
        lanes = z.shape[-1]
        z = z.reshape(planes, size[level] + 8, lanes)
        out_ref[...] = z[:, : size[level]]
        for f in range(planes):
            edge_ref[pl.ds(EDGE * f, EDGE), start : start + lanes] = z[
                f, size[level] : size[level] + EDGE
            ]
        start += lanes


def grow_columns(value, outputs):
    half = outputs // 2
    a, b, c = value[:, :half], value[:, 1 : half + 1], value[:, 2 : half + 2]
    return (a + b) * 0.5, (a + 6.0 * b + c) * 0.125


def weave(even, odd, ref, size):
    k, half, lanes = even.shape
    if 2 * half < size:
        ref[...] = jnp.zeros(ref.shape, F32)
    for q in range(k):
        for chunk in range(lanes // TS):
            part = slice(chunk * TS, (chunk + 1) * TS)
            ref[q, chunk, pl.ds(0, half, stride=2), :] = even[q][:, part]
            ref[q, chunk, pl.ds(1, half, stride=2), :] = odd[q][:, part]
    return jnp.concatenate([ref[:, chunk] for chunk in range(lanes // TS)], axis=-1)


def blend_kernel(plan, flag_ref, a0_ref, a1_ref, a2_ref, a3_ref, edge_ref, grow1_ref, grow2_ref, grow3_ref,
                 out_ref, g1_ref, g2_ref, g3_ref, e2_ref, e1_ref, e0_ref):
    bands = plan.bands
    planes = bands + 1
    w = plan.strip
    left, right = flag_ref[0], flag_ref[1]
    start = 0
    for level, (src, dst) in enumerate(((a1_ref, g1_ref), (a2_ref, g2_ref), (a3_ref, g3_ref)), 1):
        lanes = src.shape[-1]
        dst[...] = src[...]
        for f in range(planes):
            edge = edge_ref[pl.ds(EDGE * f, EDGE), start : start + lanes]
            far = w >> level
            dst[f, :EDGE] += jnp.where(left > 0, edge, 0.0)
            dst[f, far : far + EDGE] += jnp.where(right > 0, edge, 0.0)
        start += lanes
    first = flag_ref[2]
    last = flag_ref[3]

    def inside(level, columns):
        column = lax.broadcasted_iota(jnp.int32, (columns, 1), 0) - 1
        keep = ((column >= 0) | (first == 0)) & ((column < (w >> level)) | (last == 0))
        return keep.astype(F32)

    top = g3_ref[...]
    blend = top[:bands] / (BACKGROUND + top[bands:])
    for level, cur_ref, below_ref, grow_ref, up_ref in (
        (2, g2_ref, g3_ref, grow3_ref, e2_ref),
        (1, g1_ref, g2_ref, grow2_ref, e1_ref),
    ):
        stacked = jnp.concatenate([below_ref[:bands], blend], axis=0)
        k, c, r = stacked.shape
        wide = dot2(stacked.reshape(k * c, r), grow_ref[...])
        wide = wide.reshape(k, c, wide.shape[-1])
        pairs = up8(plan.held[level]) // 2
        pairs = min(pairs, c - 2)
        even, odd = grow_columns(wide, 2 * pairs)
        size = cur_ref.shape[1]
        up = weave(even, odd, up_ref, size)
        current = cur_ref[...]
        inverse = 1.0 / (BACKGROUND + current[bands])
        blend = (current[:bands] - up[:bands]) * inverse + up[bands:]
        blend = blend * inside(level, blend.shape[1])
    stacked = jnp.concatenate([g1_ref[:bands], blend], axis=0)
    k, c, r = stacked.shape
    wide = dot2(stacked.reshape(k * c, r), grow1_ref[...]).reshape(k, c, plan.rows)
    half = w // 2
    a, b, c = wide[:, :half], wide[:, 1 : half + 1], wide[:, 2 : half + 2]
    even, odd = (a + 6.0 * b + c) * 0.125, (b + c) * 0.5
    up = weave(even, odd, e0_ref, w)
    inverse = 1.0 / (BACKGROUND + a0_ref[bands])
    for f in range(bands):
        value = (a0_ref[f] - up[f]) * inverse + up[bands + f]
        out_ref[f] = value.astype(BF)


def on_chip(value):
    return pltpu.with_memory_space_constraint(value, pltpu.VMEM)


def off_chip(value):
    return pltpu.with_memory_space_constraint(value, pltpu.HBM)


def strip_local(scenes, cloud, destination, offset, counts):
    n, m = lax.axis_size("tx"), lax.axis_size("ty")
    row_tile, col_tile = lax.axis_index("tx"), lax.axis_index("ty")
    bands = scenes.shape[2]
    plan = Plan(n, m, bands)
    planes = bands + 1
    area = BS * BS
    vmem = pl.BlockSpec(memory_space=pltpu.VMEM)
    smem = pl.BlockSpec(memory_space=pltpu.SMEM)
    hbm = pl.BlockSpec(memory_space=pl.ANY)
    blocks = jnp.swapaxes(scenes[0], 0, 1).reshape(bands * S_DEV, area)
    pack = pl.pallas_call(
        functools.partial(pack_kernel, plan),
        out_shape=pltpu.VMEM((planes * S_DEV + CODE_ROWS, area), BF),
        in_specs=[smem] + [hbm] * 4,
        out_specs=vmem,
        scratch_shapes=[
            pltpu.VMEM(destination.shape, jnp.int32),
            pltpu.VMEM(offset.shape, jnp.int32),
            pltpu.SemaphoreType.DMA((4,)),
        ],
        compiler_params=pltpu.CompilerParams(vmem_limit_bytes=4 << 20),
        name="pack",
    )(counts, *[off_chip(v) for v in (blocks, cloud[0], destination, offset)])

    def swap(value, mask):
        return lax.ppermute(value, "tx", [(i, i ^ mask) for i in range(n)])

    def sum_blocks(packs, before):
        count = len(packs)
        operands = [on_chip(v) for v in packs + before]
        return pl.pallas_call(
            functools.partial(sum_kernel, plan, count),
            out_shape=pltpu.VMEM((planes, plan.slots, area), F32),
            in_specs=[vmem] * len(operands),
            out_specs=vmem,
            scratch_shapes=[pltpu.VMEM((2 * count * S_DEV, area), BF)],
            input_output_aliases={count: 0} if before else {},
            compiler_params=pltpu.CompilerParams(vmem_limit_bytes=4 << 20),
            cost_estimate=pl.CostEstimate(
                flops=4 * planes * plan.slots * area * count * S_DEV,
                bytes_accessed=planes * plan.slots * area * 4,
                transcendentals=0,
            ),
        )(*operands)

    gathered = [pack]
    sums = [sum_blocks([pack], [])]
    mask = n - 1
    while mask:
        arrived = [swap(g, mask) for g in gathered]
        if mask == 1:
            early, late = gathered[1:] + arrived[:-1], arrived[-1:]
            if early:
                sums = [sum_blocks(early, sums)]
        gathered = gathered + arrived
        mask //= 2

    column = lax.dynamic_index_in_dim(
        jnp.asarray(plan.column_tables()), row_tile * m + col_tile, keepdims=False
    )
    shrinks = row_shrinks(plan.rows)
    row1 = jnp.asarray(shrinks[0].T.astype(BF))
    row2 = jnp.asarray(shrinks[1].T.astype(BF))
    top = plan.rows >> 3
    wide_top = max(top, 128)
    padded = np.zeros((plan.rows, wide_top))
    padded[:, :top] = shrinks[2].T
    row3 = jnp.asarray(np.stack(split_table(padded)))
    size = plan.size
    shapes = [
        (planes, size[0], plan.rows),
        (planes, size[1], plan.rows >> 1),
        (planes, size[2], plan.rows >> 2),
        (planes, size[3], wide_top),
    ]
    edge_lanes = sum(s[-1] for s in shapes[1:])
    edge_shape = (up8(EDGE * planes), edge_lanes)
    a0, a1, a2, a3, edge = pl.pallas_call(
        functools.partial(place_kernel, plan, len(late)),
        out_shape=[pltpu.VMEM(s, F32) for s in shapes + [edge_shape]],
        in_specs=[vmem] * (len(late) + 5),
        compiler_params=pltpu.CompilerParams(vmem_limit_bytes=16 << 20),
        out_specs=[vmem] * 5,
        scratch_shapes=[
            pltpu.VMEM((2 * len(late) * S_DEV, area), BF),
            pltpu.VMEM((planes, plan.slots, area), F32),
            pltpu.VMEM((plan.rows, TS), F32),
            pltpu.VMEM((planes, size[1] + 8, plan.rows), F32),
            pltpu.VMEM((planes, size[2] + 8, plan.rows), F32),
            pltpu.VMEM((planes, size[3] + 8, plan.rows), F32),
        ],
        name="place",
    )(*[on_chip(v) for v in late + sums], column, row1, row2, row3)

    pairs = []
    for t in range(n):
        for j in range(m):
            other = (j + 1) % m if 2 * t < n else (j - 1) % m
            pairs.append((t * m + j, t * m + other))
    edge = lax.ppermute(edge, ("tx", "ty"), pairs)

    first, last = row_tile == 0, row_tile == n - 1
    flags = jnp.stack(
        [first & (col_tile > 0), last & (col_tile < m - 1), first & (col_tile == 0), last & (col_tile == m - 1)]
    ).astype(jnp.int32)
    grow3 = np.zeros((wide_top, plan.rows >> 2))
    grow3[:top] = grow_grid(top).T
    grow2 = grow_grid(plan.rows >> 2).T
    grow1 = grow_grid(plan.rows >> 1).T
    out = pl.pallas_call(
        functools.partial(blend_kernel, plan),
        out_shape=jax.ShapeDtypeStruct((bands, size[0], plan.rows), BF),
        in_specs=[smem] + [vmem] * 8,
        out_specs=vmem,
        scratch_shapes=[
            pltpu.VMEM(shapes[1], F32),
            pltpu.VMEM(shapes[2], F32),
            pltpu.VMEM(shapes[3], F32),
            pltpu.VMEM((2 * bands, (plan.rows >> 2) // TS, size[2], TS), F32),
            pltpu.VMEM((2 * bands, (plan.rows >> 1) // TS, size[1], TS), F32),
            pltpu.VMEM((2 * bands, plan.rows // TS, size[0], TS), F32),
        ],
        compiler_params=pltpu.CompilerParams(vmem_limit_bytes=16 << 20),
        name="blend",
    )(
        flags, *[on_chip(v) for v in (a0, a1, a2, a3, edge)],
        jnp.asarray(grow1.astype(BF)), jnp.asarray(grow2.astype(BF)), jnp.asarray(grow3.astype(BF)),
    )
    return out[:, None]


def strip_step(*arguments):
    return strip_local(*arguments)


def use_strips(n, m):
    power = n & (n - 1) == 0
    spread = max(2, 2 * S_DEV // n)
    return power and 2 <= n and TS // n >= 32 and m >= 2 and S_DEV <= 2 * spread


def solution(mesh):
    placed = (
        P(("region", "ty"), "tx", "band", None),
        P(("region", "ty"), "tx", None),
        P(("region", "ty"), "tx"),
        P(("region", "ty"), "tx"),
        P(("region", "ty"), "tx"),
    )
    strips = use_strips(mesh.shape["tx"], mesh.shape["ty"])
    return jax.shard_map(
        strip_step if strips else local,
        mesh=mesh,
        in_specs=placed,
        out_specs=P("band", ("region", "ty"), "tx", None),
        check_vma=False,
    )
```

```python
import functools

import jax
import jax.numpy as jnp
import numpy as np
from jax import lax
from jax.experimental import pallas as pl
from jax.experimental.pallas import tpu as pltpu
from jax.sharding import PartitionSpec as P


TS = 128
BS = 16
S_DEV = 64
MARGIN = 32
LEVELS = 4
SLOTS = 64


BINOMIAL = (0.0625, 0.25, 0.375, 0.25, 0.0625)
BACKGROUND = 0.25


def with_halo(shard, sides, width):
    for axis, dim in sides:
        devices, length = (lax.axis_size(axis), shard.shape[dim])
        up = [(i, (i + 1) % devices) for i in range(devices - 1)]
        down = [(j, i) for i, j in up]
        last = lax.slice_in_dim(shard, length - width, length, axis=dim)
        leading = lax.slice_in_dim(shard, 0, width, axis=dim)
        before = lax.ppermute(last, axis, up)
        after = lax.ppermute(leading, axis, down)
        shard = jnp.concatenate([before, shard, after], axis=dim)
    return shard


def shrink_table(length, rim_in, rim_out):
    extent = length - 2 * rim_in
    outputs = extent // 2 + 2 * rim_out
    first_index = rim_in - 2 - 2 * rim_out
    out_pos = jnp.arange(outputs, dtype=jnp.int32)[:, None]
    in_pos = jnp.arange(length, dtype=jnp.int32)[None, :]
    spacing = in_pos - first_index - 2 * out_pos
    table = jnp.zeros((outputs, length), jnp.float32)
    for tap_index, tap_weight in enumerate(BINOMIAL):
        table = table + tap_weight * (spacing == tap_index).astype(jnp.float32)
    return table


def grow_table(length, rim_in, rim_out):
    excess = 2 * rim_in - 2 - rim_out
    outputs = 2 * (length - 2) - 2 * excess
    paired = jnp.arange(outputs, dtype=jnp.int32)[:, None] + excess
    source = paired // 2
    parity = paired % 2
    spacing = jnp.arange(length, dtype=jnp.int32)[None, :] - source
    even_part = (
        0.125 * (spacing == 0).astype(jnp.float32)
        + 0.75 * (spacing == 1).astype(jnp.float32)
        + 0.125 * (spacing == 2).astype(jnp.float32)
    )
    odd_part = 0.5 * (spacing == 1).astype(jnp.float32) + 0.5 * (spacing == 2).astype(jnp.float32)
    return jnp.where(parity == 0, even_part, odd_part)


def apply_both(field, row_table, col_table):
    rows_done = jnp.einsum("ki,bic->bkc", row_table, field, precision=lax.Precision.HIGHEST)
    return jnp.einsum("bkc,mc->bkm", rows_done, col_table, precision=lax.Precision.HIGHEST)


def shrink(field, rim_in, rim_out):
    row_table = shrink_table(field.shape[-2], rim_in, rim_out)
    col_table = shrink_table(field.shape[-1], rim_in, rim_out)
    return apply_both(field, row_table, col_table)


def grow(field, rim_in, rim_out):
    row_table = grow_table(field.shape[-2], rim_in, rim_out)
    col_table = grow_table(field.shape[-1], rim_in, rim_out)
    return apply_both(field, row_table, col_table)


def trim(field, rim_have, rim_want):
    excess = rim_have - rim_want
    return field[..., excess : field.shape[-2] - excess, excess : field.shape[-1] - excess]


def border(extent, rim, begin, whole):
    position = begin - rim + jnp.arange(extent + 2 * rim, dtype=jnp.int32)
    return ((position >= 0) & (position < whole)).astype(jnp.float32)


def local(scenes, cloud, destination, offset, counts):
    row_tiles = lax.axis_size("tx")
    col_tiles = lax.axis_size("ty")
    row_tile = lax.axis_index("tx")
    col_tile = lax.axis_index("ty")
    spread = max(2, 2 * S_DEV // row_tiles)
    blocks = scenes[0]
    weights = cloud[0]
    target_row = destination[0]
    placed = offset[0]
    live_count = counts[0, 0]
    own_bands = blocks.shape[1]
    living = jnp.arange(S_DEV, dtype=jnp.int32) < live_count
    matches = (target_row[:, None] == jnp.arange(row_tiles, dtype=jnp.int32)[None, :]) & living[
        :, None
    ]
    ordinal = jnp.cumsum(matches.astype(jnp.int32), axis=0) - 1
    ranking = jnp.sum(jnp.where(matches, ordinal, 0), axis=1)
    target = target_row * spread + ranking
    chooser = (
        (jnp.arange(row_tiles * spread, dtype=jnp.int32)[:, None] == target[None, :])
        & living[None, :]
    ).astype(jnp.bfloat16)
    merged = jnp.concatenate([blocks, weights[:, None, :]], axis=1).reshape(
        S_DEV, (own_bands + 1) * BS * BS
    )
    packed = jnp.dot(chooser, merged, preferred_element_type=jnp.float32).astype(jnp.bfloat16)
    packed = packed.reshape(row_tiles, spread, own_bands + 1, BS * BS)
    slot_ids = jnp.arange(SLOTS, dtype=jnp.int32)
    tag_send = jnp.dot(
        chooser, (placed + 1).astype(jnp.bfloat16)[:, None], preferred_element_type=jnp.float32
    )
    tag_send = tag_send.astype(jnp.bfloat16).reshape(row_tiles, spread)
    arrived, tag_back = (
        lax.all_to_all(packed, "tx", split_axis=0, concat_axis=0, tiled=True),
        lax.all_to_all(tag_send, "tx", split_axis=0, concat_axis=0, tiled=True),
    )
    landing = (slot_ids + 1).astype(jnp.float32)[:, None] == tag_back.reshape(-1).astype(
        jnp.float32
    )[None, :]
    arrived = arrived.reshape(row_tiles * spread, own_bands + 1, BS * BS)
    coverage = arrived[:, own_bands:].astype(jnp.float32)
    payload = jnp.concatenate(
        [arrived[:, :own_bands].astype(jnp.float32) * coverage, coverage], axis=1
    )
    payload = payload.reshape(row_tiles * spread, (own_bands + 1) * BS * BS)
    slot_sums = jnp.dot(landing.astype(jnp.float32), payload, precision=lax.Precision.HIGHEST)
    per_row = TS // BS
    tile_field = slot_sums.reshape(per_row, per_row, own_bands + 1, BS, BS).transpose(2, 0, 3, 1, 4)
    tile_field = tile_field.reshape(own_bands + 1, TS, TS)

    def masked(field, extent, rim):
        row_mask = border(extent, rim, row_tile * extent, extent * row_tiles)
        col_mask = border(extent, rim, col_tile * extent, extent * col_tiles)
        return field * row_mask[:, None] * col_mask[None, :]

    def enlarge(field, rim_in, rim_out):
        return grow(field, rim_in, rim_out)

    ground = with_halo(tile_field, (("tx", 1), ("ty", 2)), MARGIN)
    margin = MARGIN
    needed = [0]
    for _ in range(1, LEVELS):
        needed.append((needed[-1] + 3) // 2)
    pyramid = [(ground, margin)]
    extent = TS
    for _ in range(1, LEVELS):
        source, rim_in = pyramid[-1]
        rim_out = (rim_in - 2) // 2
        extent = extent // 2
        reduced = masked(shrink(source, rim_in, rim_out), extent, rim_out)
        pyramid.append((reduced, rim_out))
    deepest = LEVELS - 1
    summit, rim_top = pyramid[-1]
    summit = trim(summit, rim_top, needed[deepest])
    collapsed = summit[:own_bands] / (BACKGROUND + summit[own_bands])
    for tier_index in range(LEVELS - 2, -1, -1):
        current, rim_here = pyramid[tier_index]
        coarser, rim_below = pyramid[tier_index + 1]
        current = trim(current, rim_here, needed[tier_index])
        detail = current[:own_bands] - enlarge(coarser[:own_bands], rim_below, needed[tier_index])
        band_part = detail / (BACKGROUND + current[own_bands])
        collapsed = band_part + enlarge(collapsed, needed[tier_index + 1], needed[tier_index])
        collapsed = masked(collapsed, TS >> tier_index, needed[tier_index])
    blended = collapsed.astype(jnp.bfloat16)
    flipped = jnp.swapaxes(blended, 1, 2)
    strips = lax.all_to_all(flipped, "tx", split_axis=1, concat_axis=2, tiled=True)
    return strips[:, None]


BF = jnp.bfloat16
F32 = jnp.float32
EDGE = 3
CODE_ROWS = 8
DEAD = -1024


def up8(v):
    return -(-v // 8) * 8


def shrink_grid(length):
    table = np.zeros((length // 2, length))
    for i in range(length // 2):
        for tap, weight in enumerate(BINOMIAL):
            k = 2 * i + tap - 2
            if 0 <= k < length:
                table[i, k] += weight
    return table


def grow_grid(length):
    table = np.zeros((2 * length, length))
    for i in range(length):
        for k, weight in ((i - 1, 0.125), (i, 0.75), (i + 1, 0.125)):
            if 0 <= k < length:
                table[2 * i, k] += weight
        for k in (i, i + 1):
            if k < length:
                table[2 * i + 1, k] += 0.5
    return table


def split_table(table):
    high = table.astype(BF)
    return high, (table - high.astype(np.float64)).astype(BF)


def row_shrinks(rows):
    tables, current = [], np.eye(rows)
    for level in range(1, LEVELS):
        current = shrink_grid(rows >> (level - 1)) @ current
        tables.append(current)
    return tables


class Plan:
    def __init__(self, n, m, bands):
        self.n, self.m, self.bands = n, m, bands
        self.rows = n * TS
        self.strip = TS // n
        self.slots = n * SLOTS
        self.slot_rows = n * (TS // BS)
        w = self.strip
        self.held = [w, w // 2 + 2, w // 4 + 3, w // 8 + 3]
        self.size = [w] + [up8(h) for h in self.held[1:]]
        self.first = [0, -1, -1, -1]
        self.at = [0]
        for size in self.size:
            self.at.append(self.at[-1] + size)
        self.edge_at = [None] + [self.at[LEVELS] + 8 * k for k in range(LEVELS - 1)]
        self.main = self.at[LEVELS] + 8 * (LEVELS - 1)
        self.low_at = self.main
        self.low_edge_at = self.main + self.size[3]
        self.total = self.main + self.size[3] + 8
        self.weight_at = bands // 2 * BS * BS
        self.code_at = self.weight_at + BS * BS // 2
        order = np.arange(self.rows)
        self.row_of = order % self.slot_rows * BS + order // self.slot_rows

    def column_tables(self):
        n, m, w = self.n, self.m, self.strip
        width = m * TS
        grids = [np.eye(width)] + row_shrinks(width)
        tables = np.zeros((n, m, self.total, TS))
        for t in range(n):
            for j in range(m):
                for level in range(LEVELS):
                    base = ((j * TS + t * w) >> level) + self.first[level]
                    for k in range(self.held[level]):
                        o = base + k
                        if 0 <= o < width >> level:
                            tables[t, j, self.at[level] + k] = grids[level][o, j * TS : (j + 1) * TS]
                    if level == 0:
                        continue
                    if 2 * t < n:
                        base = ((j + 1) * TS >> level) - 1
                    else:
                        base = (j * TS >> level) - 1
                    for k in range(EDGE):
                        o = base + k
                        if 0 <= o < width >> level:
                            tables[t, j, self.edge_at[level] + k] = grids[level][o, j * TS : (j + 1) * TS]
        high, low = split_table(tables)
        high[:, :, self.low_at : self.low_at + self.size[3]] = low[:, :, self.at[3] : self.at[4]]
        edge = self.edge_at[3]
        high[:, :, self.low_edge_at : self.low_edge_at + 8] = low[:, :, edge : edge + 8]
        return np.concatenate([high, high], axis=-1).reshape(n * m, self.total, 2 * TS)


def halves(value):
    high = value.astype(BF)
    return high, (value - high.astype(F32)).astype(BF)


def dot2(value, table):
    high, low = halves(value)
    return jnp.dot(high, table, preferred_element_type=F32) + jnp.dot(
        low, table, preferred_element_type=F32
    )


def pack_kernel(plan, count_ref, scenes_ref, cloud_ref, dest_ref, offset_ref, out_ref, raw, cloud, dest,
                offset, sems):
    rows = 2 * S_DEV
    pairs = plan.bands // 2
    copies = [
        pltpu.make_async_copy(source, target, sems.at[k])
        for k, (source, target) in enumerate(
            [(dest_ref, dest), (offset_ref, offset), (cloud_ref, cloud)]
            + [(scenes_ref.at[pl.ds(q * rows, rows)], raw.at[pl.ds(q * rows, rows)]) for q in range(pairs)]
        )
    ]
    for copy in copies:
        copy.start()
    for copy in copies[:2]:
        copy.wait()
    per_row = TS // BS
    slot = offset[...]
    code = (slot % per_row) * plan.slot_rows + dest[...] * per_row + slot // per_row
    live = lax.broadcasted_iota(jnp.int32, (1, S_DEV), 1) < count_ref[0, 0]
    code = jnp.where(live, code, DEAD).astype(F32)
    code = jnp.broadcast_to(jnp.concatenate([code, code], axis=1), (CODE_ROWS, rows))
    out_ref[plan.code_at :, :] = code.astype(BF)
    copies[2].wait()
    half = BS * BS // 2
    weights = jnp.concatenate([cloud[:, :half], cloud[:, half:]], axis=0)
    out_ref[plan.weight_at : plan.code_at, :] = weights.T
    for q in range(pairs):
        copies[3 + q].wait()
        out_ref[q * BS * BS : (q + 1) * BS * BS, :] = raw[q * rows : (q + 1) * rows, :].T


def landing_of(plan, pack):
    codes = pack[plan.code_at : plan.code_at + CODE_ROWS, :].astype(F32).T[:, :1]
    blocks = codes.shape[0]
    second = lax.broadcasted_iota(jnp.int32, (blocks, 1), 0) >= S_DEV
    codes = codes + jnp.where(second, float(plan.slots), 0.0)
    slot = lax.broadcasted_iota(jnp.int32, (blocks, 2 * plan.slots), 1).astype(F32)
    landing = jnp.where(slot == codes, 1.0, 0.0).astype(BF)
    return jnp.concatenate([landing, landing], axis=0)


def slot_sums(plan, pack):
    landing2 = landing_of(plan, pack)
    area = BS * BS
    blocks = 2 * S_DEV
    both = pack[plan.weight_at : plan.code_at, :].astype(F32)
    first = lax.broadcasted_iota(jnp.int32, both.shape, 1) < S_DEV
    turned = pltpu.roll(both, S_DEV, 1)
    weights = jnp.concatenate(
        [jnp.where(first, both, turned), jnp.where(first, turned, both)], axis=0
    )
    result = []
    for q in range(plan.bands // 2):
        value = pack[q * area : (q + 1) * area, :].astype(F32) * weights
        high, low = halves(value)
        pair = jnp.dot(
            jnp.concatenate([high, low], axis=1), landing2, preferred_element_type=F32
        )
        result += [pair[:, : plan.slots], pair[:, plan.slots :]]
    result.append(
        jnp.dot(weights.astype(BF), landing2[:blocks, : plan.slots], preferred_element_type=F32)
    )
    return result


def sum_kernel(plan, count, *refs):
    packs, rest = refs[:count], refs[count:]
    before_ref = rest[0] if len(rest) == 2 else None
    out_ref = rest[-1]
    for p, pack in enumerate(packs):
        for f, sums in enumerate(slot_sums(plan, pack)):
            if p:
                out_ref[f] += sums
            else:
                out_ref[f] = sums if before_ref is None else before_ref[f] + sums


def tile_of(plan, sums, tile_ref, tall):
    wide = plan.slot_rows
    ways = TS // wide
    group = lax.broadcasted_iota(jnp.int32, (BS, TS), 1) // wide
    for chunk in range(plan.slots // TS):
        for r0 in range(0, BS, ways):
            part = [
                sums[(r0 + k) * BS : (r0 + k + 1) * BS, chunk * TS : (chunk + 1) * TS]
                for k in range(ways)
            ]
            step = ways // 2
            while step:
                odd = (group & step) != 0
                for i in range(ways):
                    if i & step:
                        continue
                    a, b = part[i], part[i + step]
                    if 2 * step * wide == TS:
                        moved = pltpu.roll(jnp.where(odd, a, b), TS // 2, 1)
                        part[i] = jnp.where(odd, moved, a)
                        part[i + step] = jnp.where(odd, b, moved)
                    else:
                        part[i] = jnp.where(odd, pltpu.roll(b, step * wide, 1), a)
                        part[i + step] = jnp.where(odd, b, pltpu.roll(a, TS - step * wide, 1))
                step //= 2
            at = r0 * wide
            for k in range(ways):
                high, low = halves(part[k])
                row = (chunk * ways + k) * BS
                tile_ref[row : row + BS, at : at + TS] = high
                tile_ref[tall + row : tall + row + BS, at : at + TS] = low


def place_kernel(plan, count, *refs):
    bands = plan.bands
    packs = refs[:count]
    before_ref, column_ref, row1_ref, row2_ref, row3_ref = refs[count : count + 5]
    a0_ref, a1_ref, a2_ref, a3_ref, edge_ref = refs[count + 5 : count + 10]
    tile_ref, z1_ref, z2_ref, z3_ref = refs[count + 10 :]
    column = column_ref[...]
    added = [slot_sums(plan, pack) for pack in packs]
    at, size, edge = plan.at, plan.size, plan.edge_at
    for f in range(bands + 1):
        sums = before_ref[f]
        for one in added:
            sums = sums + one[f]
        tile = tile_ref.at[f % 2]
        tile_of(plan, sums, tile, TS)
        cols = jnp.dot(column, tile[...], preferred_element_type=F32)
        a0_ref[f] = cols[at[0] : at[1]]
        z1_ref[f, : size[1]] = cols[at[1] : at[2]]
        z1_ref[f, size[1] :] = cols[edge[1] : edge[1] + 8]
        z2_ref[f, : size[2]] = cols[at[2] : at[3]]
        z2_ref[f, size[2] :] = cols[edge[2] : edge[2] + 8]
        z3_ref[f, : size[3]] = (
            cols[at[3] : at[4]] + cols[plan.low_at : plan.low_at + size[3]]
        )
        z3_ref[f, size[3] :] = (
            cols[edge[3] : edge[3] + 8] + cols[plan.low_edge_at : plan.low_edge_at + 8]
        )
    planes = bands + 1
    rows = plan.rows
    z1 = dot2(z1_ref[...].reshape(planes * (size[1] + 8), rows), row1_ref[...])
    z2 = dot2(z2_ref[...].reshape(planes * (size[2] + 8), rows), row2_ref[...])
    z3 = z3_ref[...].reshape(planes * (size[3] + 8), rows)
    z3 = dot2(z3, row3_ref[0]) + jnp.dot(
        z3.astype(BF), row3_ref[1], preferred_element_type=F32
    )
    start = 0
    edge_ref[...] = jnp.zeros(edge_ref.shape, edge_ref.dtype)
    for z, out_ref, level in ((z1, a1_ref, 1), (z2, a2_ref, 2), (z3, a3_ref, 3)):
        lanes = z.shape[-1]
        z = z.reshape(planes, size[level] + 8, lanes)
        out_ref[...] = z[:, : size[level]]
        for f in range(planes):
            edge_ref[pl.ds(EDGE * f, EDGE), start : start + lanes] = z[
                f, size[level] : size[level] + EDGE
            ].astype(edge_ref.dtype)
        start += lanes


def grow_columns(value, outputs):
    half = outputs // 2
    a, b, c = value[:, :half], value[:, 1 : half + 1], value[:, 2 : half + 2]
    return (a + b) * 0.5, (a + 6.0 * b + c) * 0.125


def weave(even, odd, ref, size):
    k, half, lanes = even.shape
    if 2 * half < size:
        ref[...] = jnp.zeros(ref.shape, F32)
    for q in range(k):
        for chunk in range(lanes // TS):
            part = slice(chunk * TS, (chunk + 1) * TS)
            ref[q, chunk, pl.ds(0, half, stride=2), :] = even[q][:, part]
            ref[q, chunk, pl.ds(1, half, stride=2), :] = odd[q][:, part]
    return jnp.concatenate([ref[:, chunk] for chunk in range(lanes // TS)], axis=-1)


def blend_kernel(plan, flag_ref, a0_ref, a1_ref, a2_ref, a3_ref, edge_ref, grow1_ref, grow2_ref, grow3_ref,
                 natural_ref, out_ref, g1_ref, g2_ref, g3_ref, e2_ref, e1_ref, e0_ref, strip_ref, sems):
    bands = plan.bands
    planes = bands + 1
    w = plan.strip
    left, right = flag_ref[0], flag_ref[1]
    start = 0
    for level, (src, dst) in enumerate(((a1_ref, g1_ref), (a2_ref, g2_ref), (a3_ref, g3_ref)), 1):
        lanes = src.shape[-1]
        dst[...] = src[...]
        for f in range(planes):
            edge = edge_ref[pl.ds(EDGE * f, EDGE), start : start + lanes].astype(F32)
            far = w >> level
            dst[f, :EDGE] += jnp.where(left > 0, edge, 0.0)
            dst[f, far : far + EDGE] += jnp.where(right > 0, edge, 0.0)
        start += lanes
    first = flag_ref[2]
    last = flag_ref[3]

    def inside(level, columns):
        column = lax.broadcasted_iota(jnp.int32, (columns, 1), 0) - 1
        keep = ((column >= 0) | (first == 0)) & ((column < (w >> level)) | (last == 0))
        return keep.astype(F32)

    top = g3_ref[...]
    blend = top[:bands] / (BACKGROUND + top[bands:])
    for level, cur_ref, below_ref, grow_ref, up_ref in (
        (2, g2_ref, g3_ref, grow3_ref, e2_ref),
        (1, g1_ref, g2_ref, grow2_ref, e1_ref),
    ):
        stacked = jnp.concatenate([below_ref[:bands], blend], axis=0)
        k, c, r = stacked.shape
        wide = dot2(stacked.reshape(k * c, r), grow_ref[...])
        wide = wide.reshape(k, c, wide.shape[-1])
        pairs = up8(plan.held[level]) // 2
        pairs = min(pairs, c - 2)
        even, odd = grow_columns(wide, 2 * pairs)
        size = cur_ref.shape[1]
        up = weave(even, odd, up_ref, size)
        current = cur_ref[...]
        inverse = 1.0 / (BACKGROUND + current[bands])
        blend = (current[:bands] - up[:bands]) * inverse + up[bands:]
        blend = blend * inside(level, blend.shape[1])
    stacked = jnp.concatenate([g1_ref[:bands], blend], axis=0)
    k, c, r = stacked.shape
    wide = dot2(stacked.reshape(k * c, r), grow1_ref[...]).reshape(k, c, plan.rows)
    half = w // 2
    a, b, c = wide[:, :half], wide[:, 1 : half + 1], wide[:, 2 : half + 2]
    even, odd = (a + 6.0 * b + c) * 0.125, (b + c) * 0.5
    up = weave(even, odd, e0_ref, w)
    inverse = 1.0 / (BACKGROUND + a0_ref[bands])
    copies = []
    for f in range(bands):
        value = (a0_ref[f] - up[f]) * inverse + up[bands + f]
        value = jnp.dot(value.astype(BF), natural_ref[...], preferred_element_type=F32)
        strip_ref[f] = value.astype(BF)
        copies.append(pltpu.make_async_copy(strip_ref.at[f], out_ref.at[f], sems.at[f]))
        copies[-1].start()
    for copy in copies:
        copy.wait()


def on_chip(value):
    return pltpu.with_memory_space_constraint(value, pltpu.VMEM)


def off_chip(value):
    return pltpu.with_memory_space_constraint(value, pltpu.HBM)


def strip_local(scenes, cloud, destination, offset, counts):
    n, m = lax.axis_size("tx"), lax.axis_size("ty")
    row_tile, col_tile = lax.axis_index("tx"), lax.axis_index("ty")
    bands = scenes.shape[2]
    plan = Plan(n, m, bands)
    planes = bands + 1
    area = BS * BS
    vmem = pl.BlockSpec(memory_space=pltpu.VMEM)
    smem = pl.BlockSpec(memory_space=pltpu.SMEM)
    hbm = pl.BlockSpec(memory_space=pl.ANY)
    blocks = jnp.swapaxes(scenes[0], 0, 1).reshape(bands * S_DEV, area)
    pack = pl.pallas_call(
        functools.partial(pack_kernel, plan),
        out_shape=pltpu.VMEM((plan.code_at + CODE_ROWS, 2 * S_DEV), BF),
        in_specs=[smem] + [hbm] * 4,
        out_specs=vmem,
        scratch_shapes=[
            pltpu.VMEM(blocks.shape, BF),
            pltpu.VMEM(cloud[0].shape, BF),
            pltpu.VMEM(destination.shape, jnp.int32),
            pltpu.VMEM(offset.shape, jnp.int32),
            pltpu.SemaphoreType.DMA((3 + bands // 2,)),
        ],
        compiler_params=pltpu.CompilerParams(vmem_limit_bytes=4 << 20),
        name="pack",
    )(counts, *[off_chip(v) for v in (blocks, cloud[0], destination, offset)])

    def swap(value, mask):
        return lax.ppermute(value, "tx", [(i, i ^ mask) for i in range(n)])

    def sum_blocks(packs, before):
        count = len(packs)
        operands = [on_chip(v) for v in packs + before]
        return pl.pallas_call(
            functools.partial(sum_kernel, plan, count),
            out_shape=pltpu.VMEM((planes, area, plan.slots), F32),
            in_specs=[vmem] * len(operands),
            out_specs=vmem,
            input_output_aliases={count: 0} if before else {},
            compiler_params=pltpu.CompilerParams(vmem_limit_bytes=4 << 20),
            cost_estimate=pl.CostEstimate(
                flops=4 * planes * plan.slots * area * count * S_DEV,
                bytes_accessed=planes * plan.slots * area * 4,
                transcendentals=0,
            ),
        )(*operands)

    gathered = [pack]
    sums = [sum_blocks([pack], [])]
    mask = n - 1
    while mask:
        arrived = [swap(g, mask) for g in gathered]
        if mask == 1:
            early, late = gathered[1:] + arrived[:-1], arrived[-1:]
            if early:
                sums = [sum_blocks(early, sums)]
        gathered = gathered + arrived
        mask //= 2

    column = lax.dynamic_index_in_dim(
        jnp.asarray(plan.column_tables()), row_tile * m + col_tile, keepdims=False
    )
    shrinks = row_shrinks(plan.rows)
    row1 = jnp.asarray(shrinks[0].T[plan.row_of].astype(BF))
    row2 = jnp.asarray(shrinks[1].T[plan.row_of].astype(BF))
    top = plan.rows >> 3
    wide_top = max(top, 128)
    padded = np.zeros((plan.rows, wide_top))
    padded[:, :top] = shrinks[2].T[plan.row_of]
    row3 = jnp.asarray(np.stack(split_table(padded)))
    size = plan.size
    shapes = [
        (planes, size[0], plan.rows),
        (planes, size[1], plan.rows >> 1),
        (planes, size[2], plan.rows >> 2),
        (planes, size[3], wide_top),
    ]
    edge_lanes = sum(s[-1] for s in shapes[1:])
    edge_shape = (up8(EDGE * planes), edge_lanes)
    a0, a1, a2, a3, edge = pl.pallas_call(
        functools.partial(place_kernel, plan, len(late)),
        out_shape=[pltpu.VMEM(s, F32) for s in shapes] + [pltpu.VMEM(edge_shape, BF)],
        in_specs=[vmem] * (len(late) + 5),
        compiler_params=pltpu.CompilerParams(vmem_limit_bytes=16 << 20),
        out_specs=[vmem] * 5,
        scratch_shapes=[
            pltpu.VMEM((2, 2 * TS, plan.rows), BF),
            pltpu.VMEM((planes, size[1] + 8, plan.rows), F32),
            pltpu.VMEM((planes, size[2] + 8, plan.rows), F32),
            pltpu.VMEM((planes, size[3] + 8, plan.rows), F32),
        ],
        name="place",
    )(*[on_chip(v) for v in late + sums], column, row1, row2, row3)

    pairs = []
    for t in range(n):
        for j in range(m):
            other = (j + 1) % m if 2 * t < n else (j - 1) % m
            pairs.append((t * m + j, t * m + other))
    edge = lax.ppermute(edge, ("tx", "ty"), pairs)

    first, last = row_tile == 0, row_tile == n - 1
    flags = jnp.stack(
        [first & (col_tile > 0), last & (col_tile < m - 1), first & (col_tile == 0), last & (col_tile == m - 1)]
    ).astype(jnp.int32)
    grow3 = np.zeros((wide_top, plan.rows >> 2))
    grow3[:top] = grow_grid(top).T
    grow2 = grow_grid(plan.rows >> 2).T
    grow1 = grow_grid(plan.rows >> 1).T[:, plan.row_of]
    natural = np.eye(plan.rows)[plan.row_of]
    out = pl.pallas_call(
        functools.partial(blend_kernel, plan),
        out_shape=jax.ShapeDtypeStruct((bands, size[0], plan.rows), BF),
        in_specs=[smem] + [vmem] * 9,
        out_specs=hbm,
        scratch_shapes=[
            pltpu.VMEM(shapes[1], F32),
            pltpu.VMEM(shapes[2], F32),
            pltpu.VMEM(shapes[3], F32),
            pltpu.VMEM((2 * bands, (plan.rows >> 2) // TS, size[2], TS), F32),
            pltpu.VMEM((2 * bands, (plan.rows >> 1) // TS, size[1], TS), F32),
            pltpu.VMEM((2 * bands, plan.rows // TS, size[0], TS), F32),
            pltpu.VMEM((bands, size[0], plan.rows), BF),
            pltpu.SemaphoreType.DMA((bands,)),
        ],
        compiler_params=pltpu.CompilerParams(vmem_limit_bytes=16 << 20),
        name="blend",
    )(
        flags, *[on_chip(v) for v in (a0, a1, a2, a3, edge)],
        jnp.asarray(grow1.astype(BF)), jnp.asarray(grow2.astype(BF)), jnp.asarray(grow3.astype(BF)),
        jnp.asarray(natural.astype(BF)),
    )
    return out[:, None]


def strip_step(*arguments):
    return strip_local(*arguments)


def use_strips(n, m):
    power = n & (n - 1) == 0
    spread = max(2, 2 * S_DEV // n)
    return power and 2 <= n and TS // n >= 32 and m >= 2 and S_DEV <= 2 * spread


def solution(mesh):
    placed = (
        P(("region", "ty"), "tx", "band", None),
        P(("region", "ty"), "tx", None),
        P(("region", "ty"), "tx"),
        P(("region", "ty"), "tx"),
        P(("region", "ty"), "tx"),
    )
    strips = use_strips(mesh.shape["tx"], mesh.shape["ty"])
    return jax.shard_map(
        strip_step if strips else local,
        mesh=mesh,
        in_specs=placed,
        out_specs=P("band", ("region", "ty"), "tx", None),
        check_vma=False,
    )
```

```python
import functools

import jax
import jax.numpy as jnp
import numpy as np
from jax import lax
from jax.experimental import pallas as pl
from jax.experimental.pallas import tpu as pltpu
from jax.sharding import PartitionSpec as P


TS = 128
BS = 16
S_DEV = 64
MARGIN = 32
LEVELS = 4
SLOTS = 64


BINOMIAL = (0.0625, 0.25, 0.375, 0.25, 0.0625)
BACKGROUND = 0.25


def with_halo(shard, sides, width):
    for axis, dim in sides:
        devices, length = (lax.axis_size(axis), shard.shape[dim])
        up = [(i, (i + 1) % devices) for i in range(devices - 1)]
        down = [(j, i) for i, j in up]
        last = lax.slice_in_dim(shard, length - width, length, axis=dim)
        leading = lax.slice_in_dim(shard, 0, width, axis=dim)
        before = lax.ppermute(last, axis, up)
        after = lax.ppermute(leading, axis, down)
        shard = jnp.concatenate([before, shard, after], axis=dim)
    return shard


def shrink_table(length, rim_in, rim_out):
    extent = length - 2 * rim_in
    outputs = extent // 2 + 2 * rim_out
    first_index = rim_in - 2 - 2 * rim_out
    out_pos = jnp.arange(outputs, dtype=jnp.int32)[:, None]
    in_pos = jnp.arange(length, dtype=jnp.int32)[None, :]
    spacing = in_pos - first_index - 2 * out_pos
    table = jnp.zeros((outputs, length), jnp.float32)
    for tap_index, tap_weight in enumerate(BINOMIAL):
        table = table + tap_weight * (spacing == tap_index).astype(jnp.float32)
    return table


def grow_table(length, rim_in, rim_out):
    excess = 2 * rim_in - 2 - rim_out
    outputs = 2 * (length - 2) - 2 * excess
    paired = jnp.arange(outputs, dtype=jnp.int32)[:, None] + excess
    source = paired // 2
    parity = paired % 2
    spacing = jnp.arange(length, dtype=jnp.int32)[None, :] - source
    even_part = (
        0.125 * (spacing == 0).astype(jnp.float32)
        + 0.75 * (spacing == 1).astype(jnp.float32)
        + 0.125 * (spacing == 2).astype(jnp.float32)
    )
    odd_part = 0.5 * (spacing == 1).astype(jnp.float32) + 0.5 * (spacing == 2).astype(jnp.float32)
    return jnp.where(parity == 0, even_part, odd_part)


def apply_both(field, row_table, col_table):
    rows_done = jnp.einsum("ki,bic->bkc", row_table, field, precision=lax.Precision.HIGHEST)
    return jnp.einsum("bkc,mc->bkm", rows_done, col_table, precision=lax.Precision.HIGHEST)


def shrink(field, rim_in, rim_out):
    row_table = shrink_table(field.shape[-2], rim_in, rim_out)
    col_table = shrink_table(field.shape[-1], rim_in, rim_out)
    return apply_both(field, row_table, col_table)


def grow(field, rim_in, rim_out):
    row_table = grow_table(field.shape[-2], rim_in, rim_out)
    col_table = grow_table(field.shape[-1], rim_in, rim_out)
    return apply_both(field, row_table, col_table)


def trim(field, rim_have, rim_want):
    excess = rim_have - rim_want
    return field[..., excess : field.shape[-2] - excess, excess : field.shape[-1] - excess]


def border(extent, rim, begin, whole):
    position = begin - rim + jnp.arange(extent + 2 * rim, dtype=jnp.int32)
    return ((position >= 0) & (position < whole)).astype(jnp.float32)


def local(scenes, cloud, destination, offset, counts):
    row_tiles = lax.axis_size("tx")
    col_tiles = lax.axis_size("ty")
    row_tile = lax.axis_index("tx")
    col_tile = lax.axis_index("ty")
    spread = max(2, 2 * S_DEV // row_tiles)
    blocks = scenes[0]
    weights = cloud[0]
    target_row = destination[0]
    placed = offset[0]
    live_count = counts[0, 0]
    own_bands = blocks.shape[1]
    living = jnp.arange(S_DEV, dtype=jnp.int32) < live_count
    matches = (target_row[:, None] == jnp.arange(row_tiles, dtype=jnp.int32)[None, :]) & living[
        :, None
    ]
    ordinal = jnp.cumsum(matches.astype(jnp.int32), axis=0) - 1
    ranking = jnp.sum(jnp.where(matches, ordinal, 0), axis=1)
    target = target_row * spread + ranking
    chooser = (
        (jnp.arange(row_tiles * spread, dtype=jnp.int32)[:, None] == target[None, :])
        & living[None, :]
    ).astype(jnp.bfloat16)
    merged = jnp.concatenate([blocks, weights[:, None, :]], axis=1).reshape(
        S_DEV, (own_bands + 1) * BS * BS
    )
    packed = jnp.dot(chooser, merged, preferred_element_type=jnp.float32).astype(jnp.bfloat16)
    packed = packed.reshape(row_tiles, spread, own_bands + 1, BS * BS)
    slot_ids = jnp.arange(SLOTS, dtype=jnp.int32)
    tag_send = jnp.dot(
        chooser, (placed + 1).astype(jnp.bfloat16)[:, None], preferred_element_type=jnp.float32
    )
    tag_send = tag_send.astype(jnp.bfloat16).reshape(row_tiles, spread)
    arrived, tag_back = (
        lax.all_to_all(packed, "tx", split_axis=0, concat_axis=0, tiled=True),
        lax.all_to_all(tag_send, "tx", split_axis=0, concat_axis=0, tiled=True),
    )
    landing = (slot_ids + 1).astype(jnp.float32)[:, None] == tag_back.reshape(-1).astype(
        jnp.float32
    )[None, :]
    arrived = arrived.reshape(row_tiles * spread, own_bands + 1, BS * BS)
    coverage = arrived[:, own_bands:].astype(jnp.float32)
    payload = jnp.concatenate(
        [arrived[:, :own_bands].astype(jnp.float32) * coverage, coverage], axis=1
    )
    payload = payload.reshape(row_tiles * spread, (own_bands + 1) * BS * BS)
    slot_sums = jnp.dot(landing.astype(jnp.float32), payload, precision=lax.Precision.HIGHEST)
    per_row = TS // BS
    tile_field = slot_sums.reshape(per_row, per_row, own_bands + 1, BS, BS).transpose(2, 0, 3, 1, 4)
    tile_field = tile_field.reshape(own_bands + 1, TS, TS)

    def masked(field, extent, rim):
        row_mask = border(extent, rim, row_tile * extent, extent * row_tiles)
        col_mask = border(extent, rim, col_tile * extent, extent * col_tiles)
        return field * row_mask[:, None] * col_mask[None, :]

    def enlarge(field, rim_in, rim_out):
        return grow(field, rim_in, rim_out)

    ground = with_halo(tile_field, (("tx", 1), ("ty", 2)), MARGIN)
    margin = MARGIN
    needed = [0]
    for _ in range(1, LEVELS):
        needed.append((needed[-1] + 3) // 2)
    pyramid = [(ground, margin)]
    extent = TS
    for _ in range(1, LEVELS):
        source, rim_in = pyramid[-1]
        rim_out = (rim_in - 2) // 2
        extent = extent // 2
        reduced = masked(shrink(source, rim_in, rim_out), extent, rim_out)
        pyramid.append((reduced, rim_out))
    deepest = LEVELS - 1
    summit, rim_top = pyramid[-1]
    summit = trim(summit, rim_top, needed[deepest])
    collapsed = summit[:own_bands] / (BACKGROUND + summit[own_bands])
    for tier_index in range(LEVELS - 2, -1, -1):
        current, rim_here = pyramid[tier_index]
        coarser, rim_below = pyramid[tier_index + 1]
        current = trim(current, rim_here, needed[tier_index])
        detail = current[:own_bands] - enlarge(coarser[:own_bands], rim_below, needed[tier_index])
        band_part = detail / (BACKGROUND + current[own_bands])
        collapsed = band_part + enlarge(collapsed, needed[tier_index + 1], needed[tier_index])
        collapsed = masked(collapsed, TS >> tier_index, needed[tier_index])
    blended = collapsed.astype(jnp.bfloat16)
    flipped = jnp.swapaxes(blended, 1, 2)
    strips = lax.all_to_all(flipped, "tx", split_axis=1, concat_axis=2, tiled=True)
    return strips[:, None]


BF = jnp.bfloat16
F32 = jnp.float32
EDGE = 3
CODE_ROWS = 8
DEAD = -1024


def up8(v):
    return -(-v // 8) * 8


def shrink_grid(length):
    table = np.zeros((length // 2, length))
    for i in range(length // 2):
        for tap, weight in enumerate(BINOMIAL):
            k = 2 * i + tap - 2
            if 0 <= k < length:
                table[i, k] += weight
    return table


def grow_grid(length):
    table = np.zeros((2 * length, length))
    for i in range(length):
        for k, weight in ((i - 1, 0.125), (i, 0.75), (i + 1, 0.125)):
            if 0 <= k < length:
                table[2 * i, k] += weight
        for k in (i, i + 1):
            if k < length:
                table[2 * i + 1, k] += 0.5
    return table


def split_table(table):
    high = table.astype(BF)
    return high, (table - high.astype(np.float64)).astype(BF)


def row_shrinks(rows):
    tables, current = [], np.eye(rows)
    for level in range(1, LEVELS):
        current = shrink_grid(rows >> (level - 1)) @ current
        tables.append(current)
    return tables


class Plan:
    def __init__(self, n, m, bands):
        self.n, self.m, self.bands = n, m, bands
        self.rows = n * TS
        self.strip = TS // n
        self.slots = n * SLOTS
        self.slot_rows = n * (TS // BS)
        w = self.strip
        self.held = [w, w // 2 + 2, w // 4 + 3, w // 8 + 3]
        self.size = [w] + [up8(h) for h in self.held[1:]]
        self.first = [0, -1, -1, -1]
        self.at = [0]
        for size in self.size:
            self.at.append(self.at[-1] + size)
        self.low_at = self.at[LEVELS]
        self.main = self.low_at + self.size[3]
        self.edge_at = [None] + [self.main + 8 * k for k in range(LEVELS - 1)]
        self.total = self.main + 8 * (LEVELS - 1)
        self.near = TS // self.slot_rows * BS
        self.weight_at = bands // 2 * BS * BS
        self.code_at = self.weight_at + BS * BS // 2
        order = np.arange(self.rows)
        self.row_of = order % self.slot_rows * BS + order // self.slot_rows

    def column_tables(self):
        n, m, w = self.n, self.m, self.strip
        width = m * TS
        grids = [np.eye(width)] + row_shrinks(width)
        tables = np.zeros((n, m, self.total, TS))
        for t in range(n):
            for j in range(m):
                for level in range(LEVELS):
                    base = ((j * TS + t * w) >> level) + self.first[level]
                    for k in range(self.held[level]):
                        o = base + k
                        if 0 <= o < width >> level:
                            tables[t, j, self.at[level] + k] = grids[level][o, j * TS : (j + 1) * TS]
                    if level == 0:
                        continue
                    if 2 * t < n:
                        base = ((j + 1) * TS >> level) - 1
                    else:
                        base = (j * TS >> level) - 1
                    for k in range(EDGE):
                        o = base + k
                        if 0 <= o < width >> level:
                            row = grids[level][o, j * TS : (j + 1) * TS]
                            row = row[TS - self.near :] if 2 * t < n else row[: self.near]
                            tables[t, j, self.edge_at[level] + k, : self.near] = row
        high, low = split_table(tables)
        high[:, :, self.low_at : self.main] = low[:, :, self.at[3] : self.at[4]]
        return np.concatenate([high, high], axis=-1).reshape(n * m, self.total, 2 * TS)


def halves(value):
    high = value.astype(BF)
    return high, (value - high.astype(F32)).astype(BF)


def dot2(value, table):
    high, low = halves(value)
    return jnp.dot(high, table, preferred_element_type=F32) + jnp.dot(
        low, table, preferred_element_type=F32
    )


def pack_kernel(plan, count_ref, scenes_ref, cloud_ref, dest_ref, offset_ref, out_ref, raw, cloud, dest,
                offset, sems):
    rows = 2 * S_DEV
    pairs = plan.bands // 2
    copies = [
        pltpu.make_async_copy(source, target, sems.at[k])
        for k, (source, target) in enumerate(
            [(dest_ref, dest), (offset_ref, offset), (cloud_ref, cloud)]
            + [(scenes_ref.at[pl.ds(q * rows, rows)], raw.at[pl.ds(q * rows, rows)]) for q in range(pairs)]
        )
    ]
    for copy in copies:
        copy.start()
    for copy in copies[:2]:
        copy.wait()
    per_row = TS // BS
    slot = offset[...]
    code = (slot % per_row) * plan.slot_rows + dest[...] * per_row + slot // per_row
    live = lax.broadcasted_iota(jnp.int32, (1, S_DEV), 1) < count_ref[0, 0]
    code = jnp.where(live, code, DEAD).astype(F32)
    code = jnp.broadcast_to(jnp.concatenate([code, code], axis=1), (CODE_ROWS, rows))
    out_ref[plan.code_at :, :] = code.astype(BF)
    copies[2].wait()
    half = BS * BS // 2
    weights = jnp.concatenate([cloud[:, :half], cloud[:, half:]], axis=0)
    out_ref[plan.weight_at : plan.code_at, :] = weights.T
    for q in range(pairs):
        copies[3 + q].wait()
        out_ref[q * BS * BS : (q + 1) * BS * BS, :] = raw[q * rows : (q + 1) * rows, :].T


def landing_of(plan, pack):
    codes = pack[plan.code_at : plan.code_at + CODE_ROWS, :].astype(F32).T[:, :1]
    blocks = codes.shape[0]
    second = lax.broadcasted_iota(jnp.int32, (blocks, 1), 0) >= S_DEV
    codes = codes + jnp.where(second, float(plan.slots), 0.0)
    slot = lax.broadcasted_iota(jnp.int32, (blocks, 2 * plan.slots), 1).astype(F32)
    landing = jnp.where(slot == codes, 1.0, 0.0).astype(BF)
    return jnp.concatenate([landing, landing], axis=0)


def slot_sums(plan, pack):
    landing2 = landing_of(plan, pack)
    area = BS * BS
    blocks = 2 * S_DEV
    both = pack[plan.weight_at : plan.code_at, :].astype(F32)
    first = lax.broadcasted_iota(jnp.int32, both.shape, 1) < S_DEV
    turned = pltpu.roll(both, S_DEV, 1)
    weights = jnp.concatenate(
        [jnp.where(first, both, turned), jnp.where(first, turned, both)], axis=0
    )
    result = []
    for q in range(plan.bands // 2):
        value = pack[q * area : (q + 1) * area, :].astype(F32) * weights
        high, low = halves(value)
        pair = jnp.dot(
            jnp.concatenate([high, low], axis=1), landing2, preferred_element_type=F32
        )
        result += [pair[:, : plan.slots], pair[:, plan.slots :]]
    result.append(
        jnp.dot(weights.astype(BF), landing2[:blocks, : plan.slots], preferred_element_type=F32)
    )
    return result


def sum_kernel(plan, pack, out_ref):
    for f, sums in enumerate(slot_sums(plan, pack)):
        out_ref[f] = sums


def turn(plan, part):
    wide = plan.slot_rows
    ways = TS // wide
    group = lax.broadcasted_iota(jnp.int32, (BS, TS), 1) // wide
    step = ways // 2
    while step:
        odd = (group & step) != 0
        for i in range(ways):
            if i & step:
                continue
            a, b = part[i], part[i + step]
            if 2 * step * wide == TS:
                moved = pltpu.roll(jnp.where(odd, a, b), TS // 2, 1)
                part[i] = jnp.where(odd, moved, a)
                part[i + step] = jnp.where(odd, b, moved)
            else:
                part[i] = jnp.where(odd, pltpu.roll(b, step * wide, 1), a)
                part[i + step] = jnp.where(odd, b, pltpu.roll(a, TS - step * wide, 1))
        step //= 2
    return part


def first_kernel(plan, far, near, before_ref, column_ref, row1_ref, row2_ref, row3_ref,
                 out_ref, near_ref, far_ref, tile_ref, z_ref):
    planes = plan.bands + 1
    right = 2 * lax.axis_index("tx") < plan.n
    edge_table = column_ref[plan.main :, : plan.near]
    ways = TS // plan.slot_rows
    rows = plan.rows
    far_sums, near_sums = slot_sums(plan, far), slot_sums(plan, near)
    for f in range(planes):
        sums = before_ref[f] + far_sums[f] + near_sums[f]
        out_ref[f] = sums
        for which, one in enumerate((sums, far_sums[f])):
            side = jnp.where(right, one[:, plan.slots - TS :], one[:, :TS])
            tile = tile_ref.at[2 * (f % 2) + which]
            for r0 in range(0, BS, ways):
                part = [side[(r0 + k) * BS : (r0 + k + 1) * BS] for k in range(ways)]
                for k, value in enumerate(turn(plan, part)):
                    at = r0 * plan.slot_rows
                    tile[k * BS : (k + 1) * BS, at : at + TS] = value.astype(BF)
            cols = jnp.dot(edge_table, tile[...], preferred_element_type=F32)
            for level in range(1, LEVELS):
                z_ref[level - 1, which * planes + f] = cols[8 * level - 8 : 8 * level]
    start = 0
    for ref in (near_ref, far_ref):
        ref[...] = jnp.zeros(ref.shape, ref.dtype)
    for level, table in ((1, row1_ref[...]), (2, row2_ref[...]), (3, row3_ref[0])):
        lanes = table.shape[1]
        z = z_ref[level - 1].reshape(2 * planes * 8, rows).astype(BF)
        z = jnp.dot(z, table, preferred_element_type=F32).reshape(2 * planes, 8, lanes)
        for which, ref in enumerate((near_ref, far_ref)):
            for f in range(planes):
                ref[pl.ds(EDGE * f, EDGE), start : start + lanes] = z[which * planes + f, :EDGE].astype(BF)
        start += lanes


def tile_of(plan, sums, tile_ref, tall):
    ways = TS // plan.slot_rows
    for chunk in range(plan.slots // TS):
        for r0 in range(0, BS, ways):
            part = [
                sums[(r0 + k) * BS : (r0 + k + 1) * BS, chunk * TS : (chunk + 1) * TS]
                for k in range(ways)
            ]
            at = r0 * plan.slot_rows
            for k, value in enumerate(turn(plan, part)):
                high, low = halves(value)
                row = (chunk * ways + k) * BS
                tile_ref[row : row + BS, at : at + TS] = high
                tile_ref[tall + row : tall + row + BS, at : at + TS] = low


def place_kernel(plan, pack, before_ref, column_ref, row1_ref, row2_ref, row3_ref,
                 a0_ref, a1_ref, a2_ref, a3_ref, tile_ref, z1_ref, z2_ref, z3_ref):
    column = column_ref[: plan.main, :]
    at, size = plan.at, plan.size
    planes = plan.bands + 1
    for f, last in enumerate(slot_sums(plan, pack)):
        tile = tile_ref.at[f % 2]
        tile_of(plan, before_ref[f] + last, tile, TS)
        cols = jnp.dot(column, tile[...], preferred_element_type=F32)
        a0_ref[f] = cols[at[0] : at[1]]
        z1_ref[f] = cols[at[1] : at[2]]
        z2_ref[f] = cols[at[2] : at[3]]
        z3_ref[f] = cols[at[3] : at[4]] + cols[plan.low_at : plan.main]
    rows = plan.rows
    z1 = dot2(z1_ref[...].reshape(planes * size[1], rows), row1_ref[...])
    z2 = dot2(z2_ref[...].reshape(planes * size[2], rows), row2_ref[...])
    z3 = z3_ref[...].reshape(planes * size[3], rows)
    z3 = dot2(z3, row3_ref[0]) + jnp.dot(
        z3.astype(BF), row3_ref[1], preferred_element_type=F32
    )
    a1_ref[...] = z1.reshape(a1_ref.shape)
    a2_ref[...] = z2.reshape(a2_ref.shape)
    a3_ref[...] = z3.reshape(a3_ref.shape)


def grow_columns(value, outputs):
    half = outputs // 2
    a, b, c = value[:, :half], value[:, 1 : half + 1], value[:, 2 : half + 2]
    return (a + b) * 0.5, (a + 6.0 * b + c) * 0.125


def weave(even, odd, ref, size):
    k, half, lanes = even.shape
    if 2 * half < size:
        ref[...] = jnp.zeros(ref.shape, F32)
    for q in range(k):
        for chunk in range(lanes // TS):
            part = slice(chunk * TS, (chunk + 1) * TS)
            ref[q, chunk, pl.ds(0, half, stride=2), :] = even[q][:, part]
            ref[q, chunk, pl.ds(1, half, stride=2), :] = odd[q][:, part]
    return jnp.concatenate([ref[:, chunk] for chunk in range(lanes // TS)], axis=-1)


def blend_kernel(plan, a0_ref, a1_ref, a2_ref, a3_ref, near_ref, far_ref, grow1_ref, grow2_ref, grow3_ref,
                 natural_ref, out_ref, g1_ref, g2_ref, g3_ref, e2_ref, e1_ref, e0_ref, strip_ref, sems):
    bands = plan.bands
    planes = bands + 1
    w = plan.strip
    row_tile, col_tile = lax.axis_index("tx"), lax.axis_index("ty")
    first, last = row_tile == 0, row_tile == plan.n - 1
    left, right = first & (col_tile > 0), last & (col_tile < plan.m - 1)
    first, last = first & (col_tile == 0), last & (col_tile == plan.m - 1)
    edges = near_ref[...].astype(F32) + far_ref[...].astype(F32)
    start = 0
    for level, (src, dst) in enumerate(((a1_ref, g1_ref), (a2_ref, g2_ref), (a3_ref, g3_ref)), 1):
        lanes = src.shape[-1]
        dst[...] = src[...]
        for f in range(planes):
            edge = edges[EDGE * f : EDGE * (f + 1), start : start + lanes]
            far = w >> level
            dst[f, :EDGE] += jnp.where(left, edge, 0.0)
            dst[f, far : far + EDGE] += jnp.where(right, edge, 0.0)
        start += lanes

    def inside(level, columns):
        column = lax.broadcasted_iota(jnp.int32, (columns, 1), 0) - 1
        keep = ((column >= 0) | ~first) & ((column < (w >> level)) | ~last)
        return keep.astype(F32)

    top = g3_ref[...]
    blend = top[:bands] / (BACKGROUND + top[bands:])
    for level, cur_ref, below_ref, grow_ref, up_ref in (
        (2, g2_ref, g3_ref, grow3_ref, e2_ref),
        (1, g1_ref, g2_ref, grow2_ref, e1_ref),
    ):
        stacked = jnp.concatenate([below_ref[:bands], blend], axis=0)
        k, c, r = stacked.shape
        wide = dot2(stacked.reshape(k * c, r), grow_ref[...])
        wide = wide.reshape(k, c, wide.shape[-1])
        pairs = up8(plan.held[level]) // 2
        pairs = min(pairs, c - 2)
        even, odd = grow_columns(wide, 2 * pairs)
        size = cur_ref.shape[1]
        up = weave(even, odd, up_ref, size)
        current = cur_ref[...]
        inverse = 1.0 / (BACKGROUND + current[bands])
        blend = (current[:bands] - up[:bands]) * inverse + up[bands:]
        blend = blend * inside(level, blend.shape[1])
    stacked = jnp.concatenate([g1_ref[:bands], blend], axis=0)
    k, c, r = stacked.shape
    wide = dot2(stacked.reshape(k * c, r), grow1_ref[...]).reshape(k, c, plan.rows)
    half = w // 2
    a, b, c = wide[:, :half], wide[:, 1 : half + 1], wide[:, 2 : half + 2]
    even, odd = (a + 6.0 * b + c) * 0.125, (b + c) * 0.5
    up = weave(even, odd, e0_ref, w)
    inverse = 1.0 / (BACKGROUND + a0_ref[bands])
    copies = []
    part = bands // 2
    for f in range(0, bands, part):
        value = (a0_ref[f : f + part] - up[f : f + part]) * inverse + up[bands + f : bands + f + part]
        value = value.astype(BF).reshape(part * w, plan.rows)
        value = jnp.dot(value, natural_ref[...], preferred_element_type=F32)
        strip_ref[pl.ds(f, part)] = value.astype(BF).reshape(part, w, plan.rows)
        copies.append(
            pltpu.make_async_copy(
                strip_ref.at[pl.ds(f, part)], out_ref.at[pl.ds(f, part)], sems.at[len(copies)]
            )
        )
        copies[-1].start()
    for copy in copies:
        copy.wait()


def on_chip(value):
    return pltpu.with_memory_space_constraint(value, pltpu.VMEM)


def off_chip(value):
    return pltpu.with_memory_space_constraint(value, pltpu.HBM)


def strip_local(scenes, cloud, destination, offset, counts):
    n, m = lax.axis_size("tx"), lax.axis_size("ty")
    row_tile, col_tile = lax.axis_index("tx"), lax.axis_index("ty")
    bands = scenes.shape[2]
    plan = Plan(n, m, bands)
    planes = bands + 1
    area = BS * BS
    vmem = pl.BlockSpec(memory_space=pltpu.VMEM)
    smem = pl.BlockSpec(memory_space=pltpu.SMEM)
    hbm = pl.BlockSpec(memory_space=pl.ANY)
    blocks = jnp.swapaxes(scenes[0], 0, 1).reshape(bands * S_DEV, area)
    pack = pl.pallas_call(
        functools.partial(pack_kernel, plan),
        out_shape=pltpu.VMEM((plan.code_at + CODE_ROWS, 2 * S_DEV), BF),
        in_specs=[smem] + [hbm] * 4,
        out_specs=vmem,
        scratch_shapes=[
            pltpu.VMEM(blocks.shape, BF),
            pltpu.VMEM(cloud[0].shape, BF),
            pltpu.VMEM(destination.shape, jnp.int32),
            pltpu.VMEM(offset.shape, jnp.int32),
            pltpu.SemaphoreType.DMA((3 + bands // 2,)),
        ],
        compiler_params=pltpu.CompilerParams(vmem_limit_bytes=4 << 20),
        name="pack",
    )(counts, *[off_chip(v) for v in (blocks, cloud[0], destination, offset)])

    def call(kernel, operands, outputs, scratch=(), flops=0, out_specs=None):
        return pl.pallas_call(
            functools.partial(kernel, plan),
            out_shape=outputs,
            in_specs=[vmem] * len(operands),
            out_specs=out_specs or jax.tree.map(lambda _: vmem, outputs),
            scratch_shapes=list(scratch),
            compiler_params=pltpu.CompilerParams(vmem_limit_bytes=16 << 20),
            cost_estimate=pl.CostEstimate(flops=flops, bytes_accessed=1 << 20, transcendentals=0),
        )(*[on_chip(v) for v in operands])

    column = lax.dynamic_index_in_dim(
        jnp.asarray(plan.column_tables()), row_tile * m + col_tile, keepdims=False
    )
    shrinks = row_shrinks(plan.rows)
    row1 = jnp.asarray(shrinks[0].T[plan.row_of].astype(BF))
    row2 = jnp.asarray(shrinks[1].T[plan.row_of].astype(BF))
    top = plan.rows >> 3
    wide_top = max(top, 128)
    padded = np.zeros((plan.rows, wide_top))
    padded[:, :top] = shrinks[2].T[plan.row_of]
    row3 = jnp.asarray(np.stack(split_table(padded)))
    tables = [column, row1, row2, row3]
    size = plan.size
    shapes = [
        (planes, size[0], plan.rows),
        (planes, size[1], plan.rows >> 1),
        (planes, size[2], plan.rows >> 2),
        (planes, size[3], wide_top),
    ]
    edge_shape = (up8(EDGE * planes), sum(s[-1] for s in shapes[1:]))
    sums_shape = pltpu.VMEM((planes, area, plan.slots), F32)
    work = 2 * planes * area * plan.slots * 2 * S_DEV

    across = [(i, n - 1 - i) for i in range(n)]
    beside = [(i, i ^ 1) for i in range(n)]
    far = lax.ppermute(pack, "tx", across)
    near = lax.ppermute(pack, "tx", beside)
    sums = call(sum_kernel, [pack], sums_shape, flops=work)
    late = lax.ppermute(far, "tx", beside)
    sums, edge_near, edge_far = call(
        first_kernel,
        [far, near, sums] + tables,
        [sums_shape, pltpu.VMEM(edge_shape, BF), pltpu.VMEM(edge_shape, BF)],
        [
            pltpu.VMEM((4, plan.near, plan.rows), BF),
            pltpu.VMEM((LEVELS - 1, 2 * planes, 8, plan.rows), F32),
        ],
        flops=4 * work,
    )
    turns = [
        (t * m + j, (j + 1) % m if 2 * t < n else (j - 1) % m) for t in range(n) for j in range(m)
    ]
    edge_near = lax.ppermute(edge_near, ("tx", "ty"), [(k, k // m * m + j) for k, j in turns])
    edge_far = lax.ppermute(edge_far, ("tx", "ty"), [(k, (k // m ^ 1) * m + j) for k, j in turns])
    levels = call(
        place_kernel,
        [late, sums] + tables,
        [pltpu.VMEM(s, F32) for s in shapes],
        [pltpu.VMEM((2, 2 * TS, plan.rows), BF)]
        + [pltpu.VMEM((planes, s, plan.rows), F32) for s in size[1:]],
        flops=4 * work,
    )
    grow3 = np.zeros((wide_top, plan.rows >> 2))
    grow3[:top] = grow_grid(top).T
    grow2 = grow_grid(plan.rows >> 2).T
    grow1 = grow_grid(plan.rows >> 1).T[:, plan.row_of]
    natural = np.eye(plan.rows)[plan.row_of]
    out = call(
        blend_kernel,
        [*levels, edge_near, edge_far]
        + [jnp.asarray(table.astype(BF)) for table in (grow1, grow2, grow3, natural)],
        jax.ShapeDtypeStruct((bands, size[0], plan.rows), BF),
        [
            pltpu.VMEM(shapes[1], F32),
            pltpu.VMEM(shapes[2], F32),
            pltpu.VMEM(shapes[3], F32),
            pltpu.VMEM((2 * bands, (plan.rows >> 2) // TS, size[2], TS), F32),
            pltpu.VMEM((2 * bands, (plan.rows >> 1) // TS, size[1], TS), F32),
            pltpu.VMEM((2 * bands, plan.rows // TS, size[0], TS), F32),
            pltpu.VMEM((bands, size[0], plan.rows), BF),
            pltpu.SemaphoreType.DMA((2,)),
        ],
        flops=4 * work,
        out_specs=hbm,
    )
    return out[:, None]


def strip_step(*arguments):
    return strip_local(*arguments)


def use_strips(n, m):
    spread = max(2, 2 * S_DEV // n)
    return n == 4 and TS // n >= 32 and m >= 2 and S_DEV <= 2 * spread


def solution(mesh):
    placed = (
        P(("region", "ty"), "tx", "band", None),
        P(("region", "ty"), "tx", None),
        P(("region", "ty"), "tx"),
        P(("region", "ty"), "tx"),
        P(("region", "ty"), "tx"),
    )
    strips = use_strips(mesh.shape["tx"], mesh.shape["ty"])
    return jax.shard_map(
        strip_step if strips else local,
        mesh=mesh,
        in_specs=placed,
        out_specs=P("band", ("region", "ty"), "tx", None),
        check_vma=False,
    )
```

```python
import functools

import jax
import jax.numpy as jnp
import numpy as np
from jax import lax
from jax.experimental import pallas as pl
from jax.experimental.pallas import tpu as pltpu
from jax.sharding import PartitionSpec as P


TS = 128
BS = 16
S_DEV = 64
MARGIN = 32
LEVELS = 4
SLOTS = 64


BINOMIAL = (0.0625, 0.25, 0.375, 0.25, 0.0625)
BACKGROUND = 0.25


def with_halo(shard, sides, width):
    for axis, dim in sides:
        devices, length = (lax.axis_size(axis), shard.shape[dim])
        up = [(i, (i + 1) % devices) for i in range(devices - 1)]
        down = [(j, i) for i, j in up]
        last = lax.slice_in_dim(shard, length - width, length, axis=dim)
        leading = lax.slice_in_dim(shard, 0, width, axis=dim)
        before = lax.ppermute(last, axis, up)
        after = lax.ppermute(leading, axis, down)
        shard = jnp.concatenate([before, shard, after], axis=dim)
    return shard


def shrink_table(length, rim_in, rim_out):
    extent = length - 2 * rim_in
    outputs = extent // 2 + 2 * rim_out
    first_index = rim_in - 2 - 2 * rim_out
    out_pos = jnp.arange(outputs, dtype=jnp.int32)[:, None]
    in_pos = jnp.arange(length, dtype=jnp.int32)[None, :]
    spacing = in_pos - first_index - 2 * out_pos
    table = jnp.zeros((outputs, length), jnp.float32)
    for tap_index, tap_weight in enumerate(BINOMIAL):
        table = table + tap_weight * (spacing == tap_index).astype(jnp.float32)
    return table


def grow_table(length, rim_in, rim_out):
    excess = 2 * rim_in - 2 - rim_out
    outputs = 2 * (length - 2) - 2 * excess
    paired = jnp.arange(outputs, dtype=jnp.int32)[:, None] + excess
    source = paired // 2
    parity = paired % 2
    spacing = jnp.arange(length, dtype=jnp.int32)[None, :] - source
    even_part = (
        0.125 * (spacing == 0).astype(jnp.float32)
        + 0.75 * (spacing == 1).astype(jnp.float32)
        + 0.125 * (spacing == 2).astype(jnp.float32)
    )
    odd_part = 0.5 * (spacing == 1).astype(jnp.float32) + 0.5 * (spacing == 2).astype(jnp.float32)
    return jnp.where(parity == 0, even_part, odd_part)


def apply_both(field, row_table, col_table):
    rows_done = jnp.einsum("ki,bic->bkc", row_table, field, precision=lax.Precision.HIGHEST)
    return jnp.einsum("bkc,mc->bkm", rows_done, col_table, precision=lax.Precision.HIGHEST)


def shrink(field, rim_in, rim_out):
    row_table = shrink_table(field.shape[-2], rim_in, rim_out)
    col_table = shrink_table(field.shape[-1], rim_in, rim_out)
    return apply_both(field, row_table, col_table)


def grow(field, rim_in, rim_out):
    row_table = grow_table(field.shape[-2], rim_in, rim_out)
    col_table = grow_table(field.shape[-1], rim_in, rim_out)
    return apply_both(field, row_table, col_table)


def trim(field, rim_have, rim_want):
    excess = rim_have - rim_want
    return field[..., excess : field.shape[-2] - excess, excess : field.shape[-1] - excess]


def border(extent, rim, begin, whole):
    position = begin - rim + jnp.arange(extent + 2 * rim, dtype=jnp.int32)
    return ((position >= 0) & (position < whole)).astype(jnp.float32)


def local(scenes, cloud, destination, offset, counts):
    row_tiles = lax.axis_size("tx")
    col_tiles = lax.axis_size("ty")
    row_tile = lax.axis_index("tx")
    col_tile = lax.axis_index("ty")
    spread = max(2, 2 * S_DEV // row_tiles)
    blocks = scenes[0]
    weights = cloud[0]
    target_row = destination[0]
    placed = offset[0]
    live_count = counts[0, 0]
    own_bands = blocks.shape[1]
    living = jnp.arange(S_DEV, dtype=jnp.int32) < live_count
    matches = (target_row[:, None] == jnp.arange(row_tiles, dtype=jnp.int32)[None, :]) & living[
        :, None
    ]
    ordinal = jnp.cumsum(matches.astype(jnp.int32), axis=0) - 1
    ranking = jnp.sum(jnp.where(matches, ordinal, 0), axis=1)
    target = target_row * spread + ranking
    chooser = (
        (jnp.arange(row_tiles * spread, dtype=jnp.int32)[:, None] == target[None, :])
        & living[None, :]
    ).astype(jnp.bfloat16)
    merged = jnp.concatenate([blocks, weights[:, None, :]], axis=1).reshape(
        S_DEV, (own_bands + 1) * BS * BS
    )
    packed = jnp.dot(chooser, merged, preferred_element_type=jnp.float32).astype(jnp.bfloat16)
    packed = packed.reshape(row_tiles, spread, own_bands + 1, BS * BS)
    slot_ids = jnp.arange(SLOTS, dtype=jnp.int32)
    tag_send = jnp.dot(
        chooser, (placed + 1).astype(jnp.bfloat16)[:, None], preferred_element_type=jnp.float32
    )
    tag_send = tag_send.astype(jnp.bfloat16).reshape(row_tiles, spread)
    arrived, tag_back = (
        lax.all_to_all(packed, "tx", split_axis=0, concat_axis=0, tiled=True),
        lax.all_to_all(tag_send, "tx", split_axis=0, concat_axis=0, tiled=True),
    )
    landing = (slot_ids + 1).astype(jnp.float32)[:, None] == tag_back.reshape(-1).astype(
        jnp.float32
    )[None, :]
    arrived = arrived.reshape(row_tiles * spread, own_bands + 1, BS * BS)
    coverage = arrived[:, own_bands:].astype(jnp.float32)
    payload = jnp.concatenate(
        [arrived[:, :own_bands].astype(jnp.float32) * coverage, coverage], axis=1
    )
    payload = payload.reshape(row_tiles * spread, (own_bands + 1) * BS * BS)
    slot_sums = jnp.dot(landing.astype(jnp.float32), payload, precision=lax.Precision.HIGHEST)
    per_row = TS // BS
    tile_field = slot_sums.reshape(per_row, per_row, own_bands + 1, BS, BS).transpose(2, 0, 3, 1, 4)
    tile_field = tile_field.reshape(own_bands + 1, TS, TS)

    def masked(field, extent, rim):
        row_mask = border(extent, rim, row_tile * extent, extent * row_tiles)
        col_mask = border(extent, rim, col_tile * extent, extent * col_tiles)
        return field * row_mask[:, None] * col_mask[None, :]

    def enlarge(field, rim_in, rim_out):
        return grow(field, rim_in, rim_out)

    ground = with_halo(tile_field, (("tx", 1), ("ty", 2)), MARGIN)
    margin = MARGIN
    needed = [0]
    for _ in range(1, LEVELS):
        needed.append((needed[-1] + 3) // 2)
    pyramid = [(ground, margin)]
    extent = TS
    for _ in range(1, LEVELS):
        source, rim_in = pyramid[-1]
        rim_out = (rim_in - 2) // 2
        extent = extent // 2
        reduced = masked(shrink(source, rim_in, rim_out), extent, rim_out)
        pyramid.append((reduced, rim_out))
    deepest = LEVELS - 1
    summit, rim_top = pyramid[-1]
    summit = trim(summit, rim_top, needed[deepest])
    collapsed = summit[:own_bands] / (BACKGROUND + summit[own_bands])
    for tier_index in range(LEVELS - 2, -1, -1):
        current, rim_here = pyramid[tier_index]
        coarser, rim_below = pyramid[tier_index + 1]
        current = trim(current, rim_here, needed[tier_index])
        detail = current[:own_bands] - enlarge(coarser[:own_bands], rim_below, needed[tier_index])
        band_part = detail / (BACKGROUND + current[own_bands])
        collapsed = band_part + enlarge(collapsed, needed[tier_index + 1], needed[tier_index])
        collapsed = masked(collapsed, TS >> tier_index, needed[tier_index])
    blended = collapsed.astype(jnp.bfloat16)
    flipped = jnp.swapaxes(blended, 1, 2)
    strips = lax.all_to_all(flipped, "tx", split_axis=1, concat_axis=2, tiled=True)
    return strips[:, None]


BF = jnp.bfloat16
F32 = jnp.float32
EDGE = 3
CODE_ROWS = 8
DEAD = -1024


def up8(v):
    return -(-v // 8) * 8


def shrink_grid(length):
    table = np.zeros((length // 2, length))
    for i in range(length // 2):
        for tap, weight in enumerate(BINOMIAL):
            k = 2 * i + tap - 2
            if 0 <= k < length:
                table[i, k] += weight
    return table


def grow_grid(length):
    table = np.zeros((2 * length, length))
    for i in range(length):
        for k, weight in ((i - 1, 0.125), (i, 0.75), (i + 1, 0.125)):
            if 0 <= k < length:
                table[2 * i, k] += weight
        for k in (i, i + 1):
            if k < length:
                table[2 * i + 1, k] += 0.5
    return table


def split_table(table):
    high = table.astype(BF)
    return high, (table - high.astype(np.float64)).astype(BF)


def row_shrinks(rows):
    tables, current = [], np.eye(rows)
    for level in range(1, LEVELS):
        current = shrink_grid(rows >> (level - 1)) @ current
        tables.append(current)
    return tables


class Plan:
    def __init__(self, n, m, bands):
        self.n, self.m, self.bands = n, m, bands
        self.rows = n * TS
        self.strip = TS // n
        self.slots = n * SLOTS
        self.slot_rows = n * (TS // BS)
        w = self.strip
        self.held = [w, w // 2 + 2, w // 4 + 3, w // 8 + 3]
        self.size = [w] + [up8(h) for h in self.held[1:]]
        self.first = [0, -1, -1, -1]
        self.at = [0]
        for size in self.size:
            self.at.append(self.at[-1] + size)
        self.low_at = self.at[LEVELS]
        self.main = self.low_at + self.size[3]
        self.edge_rows = 8 * (LEVELS - 1)
        self.total = self.main + 2 * self.edge_rows
        self.near = 2 * BS
        self.half = BS * BS // 2
        self.weight_at = bands * self.half
        self.code_at = self.weight_at + self.half
        order = np.arange(self.rows)
        wide = self.slot_rows
        u, half, v = order // (4 * wide), order // (2 * wide) % 2, order // wide % 2
        self.row_of = order % wide * BS + half * (BS // 2) + 2 * u + v

    def column_tables(self):
        n, m, w = self.n, self.m, self.strip
        width = m * TS
        grids = [np.eye(width)] + row_shrinks(width)
        tables = np.zeros((n, m, self.total, TS))
        for t in range(n):
            for j in range(m):
                for level in range(LEVELS):
                    base = ((j * TS + t * w) >> level) + self.first[level]
                    for k in range(self.held[level]):
                        o = base + k
                        if 0 <= o < width >> level:
                            tables[t, j, self.at[level] + k] = grids[level][o, j * TS : (j + 1) * TS]
                    for which, target in enumerate((t, t ^ n // 2)):
                        right = 2 * target < n
                        base = ((j + 1 if right else j) * TS >> level) - 1
                        at = self.main + which * self.edge_rows + 8 * (level - 1)
                        for k in range(EDGE if level else 0):
                            if 0 <= base + k < width >> level:
                                row = grids[level][base + k, j * TS : (j + 1) * TS]
                                row = row[TS - self.near :] if right else row[: self.near]
                                tables[t, j, at + k, : self.near] = row
        high, low = split_table(tables)
        high[:, :, self.low_at : self.main] = low[:, :, self.at[3] : self.at[4]]
        return np.concatenate([high, high], axis=-1).reshape(n * m, self.total, 2 * TS)


def halves(value):
    high = value.astype(BF)
    return high, (value - high.astype(F32)).astype(BF)


def dot2(value, table):
    high, low = halves(value)
    return jnp.dot(high, table, preferred_element_type=F32) + jnp.dot(
        low, table, preferred_element_type=F32
    )


def pack_kernel(plan, count_ref, scenes_ref, cloud_ref, dest_ref, offset_ref, out_ref, raw, dest,
                offset, sems):
    rows = 2 * S_DEV
    half = plan.half
    copies = [
        pltpu.make_async_copy(source, target, sems.at[k])
        for k, (source, target) in enumerate(
            (
                (dest_ref, dest),
                (offset_ref, offset),
                (cloud_ref, raw.at[plan.bands]),
                (scenes_ref, raw.at[pl.ds(0, plan.bands)]),
            )
        )
    ]
    for copy in copies:
        copy.start()
    for copy in copies[:2]:
        copy.wait()
    per_row = TS // BS
    slot = offset[...]
    code = (slot % per_row) * plan.slot_rows + dest[...] * per_row + slot // per_row
    live = lax.broadcasted_iota(jnp.int32, (1, S_DEV), 1) < count_ref[0, 0]
    code = jnp.where(live, code, DEAD).astype(F32)
    code = jnp.broadcast_to(jnp.concatenate([code, code], axis=1), (CODE_ROWS, rows))
    out_ref[plan.code_at :, :] = code.astype(BF)
    for f in (plan.bands, *range(plan.bands)):
        if f == plan.bands:
            copies[2].wait()
        elif f == 0:
            copies[3].wait()
        block = raw[f]
        block = jnp.concatenate([block[:, :half], block[:, half:]], axis=0)
        out_ref[f * half : (f + 1) * half, :] = block.T


def load_kernel(plan, column_ref, *refs):
    count = (len(refs) - 2) // 2
    sources, targets, sems = refs[:count], refs[count:-1], refs[-1]
    mine = lax.axis_index("tx") * plan.m + lax.axis_index("ty")
    copies = [
        pltpu.make_async_copy(source, target, sems.at[k])
        for k, (source, target) in enumerate(zip((column_ref.at[mine], *sources), targets))
    ]
    for copy in copies:
        copy.start()
    for copy in copies:
        copy.wait()


def landing_of(plan, pack):
    codes = pack[plan.code_at : plan.code_at + CODE_ROWS, :].astype(F32).T[:, :1]
    blocks = codes.shape[0]
    pair = float(2 * plan.slot_rows)
    second = lax.broadcasted_iota(jnp.int32, (blocks, 1), 0) >= S_DEV
    codes = codes + pair * jnp.floor(codes / pair) + jnp.where(second, pair, 0.0)
    slot = lax.broadcasted_iota(jnp.int32, (blocks, 2 * plan.slots), 1).astype(F32)
    landing = jnp.where(slot == codes, 1.0, 0.0).astype(BF)
    return jnp.concatenate([landing, landing], axis=0)


def slot_sums(plan, pack, prod_ref):
    weight = pack[plan.weight_at : plan.code_at, :]
    half, blocks = plan.half, 2 * S_DEV
    for f in range(plan.bands):
        rows = pl.ds(f * half, half)
        high, low = halves(pack[f * half : (f + 1) * half, :].astype(F32) * weight.astype(F32))
        prod_ref[rows, :blocks] = high
        prod_ref[rows, blocks:] = low
    rows = pl.ds(plan.weight_at, half)
    prod_ref[rows, :blocks] = weight
    prod_ref[rows, blocks:] = jnp.zeros_like(weight)
    return jnp.dot(prod_ref[...], landing_of(plan, pack), preferred_element_type=F32)


def turn(plan, a, b):
    wide = plan.slot_rows
    odd = lax.broadcasted_iota(jnp.int32, a.shape, 1) // wide % 2 == 1
    return jnp.where(odd, pltpu.roll(b, wide, 1), a), jnp.where(odd, b, pltpu.roll(a, TS - wide, 1))


def edge_of(plan, side_ref, table, row_refs, out_ref, tile_ref, z_ref):
    planes = plan.bands + 1
    rows = plan.rows
    for f in range(planes):
        tile = tile_ref.at[f % 2]
        for u in range(BS // 4):
            at = f * plan.half + 2 * u * BS
            pair = turn(plan, side_ref[at : at + BS], side_ref[at + BS : at + 2 * BS])
            for k, value in enumerate(pair):
                tile[k * BS : (k + 1) * BS, u * TS : (u + 1) * TS] = value.astype(BF)
        cols = jnp.dot(table, tile[...], preferred_element_type=F32)
        for level in range(LEVELS - 1):
            z_ref[level, f] = cols[8 * level : 8 * level + 8]
    start = 0
    out_ref[...] = jnp.zeros(out_ref.shape, out_ref.dtype)
    for level, ref in enumerate(row_refs):
        row_table = ref[...] if len(ref.shape) == 2 else ref[0]
        lanes = row_table.shape[1]
        z = z_ref[level].reshape(planes * 8, rows).astype(BF)
        z = jnp.dot(z, row_table, preferred_element_type=F32).reshape(planes, 8, lanes)
        for f in range(planes):
            out_ref[pl.ds(EDGE * f, EDGE), start : start + lanes] = z[f, :EDGE].astype(BF)
        start += lanes


def side_of(plan, sums, right):
    return jnp.where(right, sums[:, 2 * plan.slots - TS :], sums[:, :TS])


def own_kernel(plan, pack, column_ref, row1_ref, row2_ref, row3_ref,
               out_ref, edge_ref, prod_ref, side_ref, tile_ref, z_ref):
    right = 2 * (lax.axis_index("tx") ^ plan.n // 2) < plan.n
    sums = slot_sums(plan, pack, prod_ref)
    out_ref[...] = sums
    side_ref[...] = side_of(plan, sums, right)
    table = column_ref[plan.main + plan.edge_rows :, : plan.near]
    edge_of(plan, side_ref, table, (row1_ref, row2_ref, row3_ref), edge_ref, tile_ref, z_ref)


def first_kernel(plan, far, near, before_ref, column_ref, row1_ref, row2_ref, row3_ref,
                 out_ref, edge_ref, prod_ref, side_ref, tile_ref, z_ref):
    right = 2 * lax.axis_index("tx") < plan.n
    one = slot_sums(plan, far, prod_ref.at[0])
    sums = before_ref[...] + one + slot_sums(plan, near, prod_ref.at[1])
    out_ref[...] = sums
    side_ref[...] = side_of(plan, sums, right)
    table = column_ref[plan.main : plan.main + plan.edge_rows, : plan.near]
    edge_of(plan, side_ref, table, (row1_ref, row2_ref, row3_ref), edge_ref, tile_ref, z_ref)


def tile_of(plan, sums, at, tile_ref):
    for pair in range(2 * plan.slots // TS):
        lanes = slice(pair * TS, (pair + 1) * TS)
        for u in range(BS // 4):
            row = at + 2 * u * BS
            both = turn(plan, sums[row : row + BS, lanes], sums[row + BS : row + 2 * BS, lanes])
            for k, value in enumerate(both):
                high, low = halves(value)
                row = (2 * pair + k) * BS
                tile_ref[row : row + BS, u * TS : (u + 1) * TS] = high
                tile_ref[TS + row : TS + row + BS, u * TS : (u + 1) * TS] = low


def place_kernel(plan, pack, before_ref, column_ref, row1_ref, row2_ref, row3_ref,
                 a0_ref, a1_ref, a2_ref, a3_ref, prod_ref, sums_ref, tile_ref, z1_ref, z2_ref, z3_ref):
    column = column_ref[: plan.main, :]
    at, size = plan.at, plan.size
    planes = plan.bands + 1
    rows = plan.rows
    sums_ref[...] = before_ref[...] + slot_sums(plan, pack, prod_ref)
    for f in range(planes):
        tile = tile_ref.at[f % 2]
        tile_of(plan, sums_ref, f * plan.half, tile)
        cols = jnp.dot(column, tile[...], preferred_element_type=F32)
        a0_ref[f] = cols[at[0] : at[1]]
        z1_ref[f] = cols[at[1] : at[2]]
        z2_ref[f] = cols[at[2] : at[3]]
        z3_ref[f] = cols[at[3] : at[4]] + cols[plan.low_at : plan.main]
    z1 = dot2(z1_ref[...].reshape(planes * size[1], rows), row1_ref[...])
    z2 = dot2(z2_ref[...].reshape(planes * size[2], rows), row2_ref[...])
    z3 = z3_ref[...].reshape(planes * size[3], rows)
    z3 = dot2(z3, row3_ref[0]) + jnp.dot(
        z3.astype(BF), row3_ref[1], preferred_element_type=F32
    )
    a1_ref[...] = z1.reshape(a1_ref.shape)
    a2_ref[...] = z2.reshape(a2_ref.shape)
    a3_ref[...] = z3.reshape(a3_ref.shape)


def grow_columns(value, outputs):
    half = outputs // 2
    a, b, c = value[:, :half], value[:, 1 : half + 1], value[:, 2 : half + 2]
    return (a + b) * 0.5, (a + 6.0 * b + c) * 0.125


def weave(even, odd, ref, size):
    k, half, lanes = even.shape
    if 2 * half < size:
        ref[...] = jnp.zeros(ref.shape, F32)
    for q in range(k):
        for chunk in range(lanes // TS):
            part = slice(chunk * TS, (chunk + 1) * TS)
            ref[q, chunk, pl.ds(0, half, stride=2), :] = even[q][:, part]
            ref[q, chunk, pl.ds(1, half, stride=2), :] = odd[q][:, part]
    return jnp.concatenate([ref[:, chunk] for chunk in range(lanes // TS)], axis=-1)


def blend_kernel(plan, a0_ref, a1_ref, a2_ref, a3_ref, near_ref, far_ref, grow1_ref, grow2_ref, grow3_ref,
                 natural_ref, out_ref, g1_ref, g2_ref, g3_ref, e2_ref, e1_ref, e0_ref, strip_ref, sems):
    bands = plan.bands
    planes = bands + 1
    w = plan.strip
    row_tile, col_tile = lax.axis_index("tx"), lax.axis_index("ty")
    first, last = row_tile == 0, row_tile == plan.n - 1
    left, right = first & (col_tile > 0), last & (col_tile < plan.m - 1)
    first, last = first & (col_tile == 0), last & (col_tile == plan.m - 1)
    edges = near_ref[...].astype(F32) + far_ref[...].astype(F32)
    start = 0
    for level, (src, dst) in enumerate(((a1_ref, g1_ref), (a2_ref, g2_ref), (a3_ref, g3_ref)), 1):
        lanes = src.shape[-1]
        dst[...] = src[...]
        for f in range(planes):
            edge = edges[EDGE * f : EDGE * (f + 1), start : start + lanes]
            far = w >> level
            dst[f, :EDGE] += jnp.where(left, edge, 0.0)
            dst[f, far : far + EDGE] += jnp.where(right, edge, 0.0)
        start += lanes

    def inside(level, columns):
        column = lax.broadcasted_iota(jnp.int32, (columns, 1), 0) - 1
        keep = ((column >= 0) | ~first) & ((column < (w >> level)) | ~last)
        return keep.astype(F32)

    top = g3_ref[...]
    blend = top[:bands] / (BACKGROUND + top[bands:])
    for level, cur_ref, below_ref, grow_ref, up_ref in (
        (2, g2_ref, g3_ref, grow3_ref, e2_ref),
        (1, g1_ref, g2_ref, grow2_ref, e1_ref),
    ):
        stacked = jnp.concatenate([below_ref[:bands], blend], axis=0)
        k, c, r = stacked.shape
        wide = dot2(stacked.reshape(k * c, r), grow_ref[...])
        wide = wide.reshape(k, c, wide.shape[-1])
        pairs = up8(plan.held[level]) // 2
        pairs = min(pairs, c - 2)
        even, odd = grow_columns(wide, 2 * pairs)
        size = cur_ref.shape[1]
        up = weave(even, odd, up_ref, size)
        current = cur_ref[...]
        inverse = 1.0 / (BACKGROUND + current[bands])
        blend = (current[:bands] - up[:bands]) * inverse + up[bands:]
        blend = blend * inside(level, blend.shape[1])
    stacked = jnp.concatenate([g1_ref[:bands], blend], axis=0)
    half = w // 2
    a, b, c = stacked[:, :half], stacked[:, 1 : half + 1], stacked[:, 2 : half + 2]
    even, odd = (a + 6.0 * b + c) * 0.125, (b + c) * 0.5
    tall = weave(even, odd, e0_ref, w)
    up = dot2(tall.reshape(2 * bands * w, tall.shape[-1]), grow1_ref[...])
    up = up.reshape(2 * bands, w, plan.rows)
    inverse = 1.0 / (BACKGROUND + a0_ref[bands])
    copies = []
    part = bands // 2
    for f in range(0, bands, part):
        value = (a0_ref[f : f + part] - up[f : f + part]) * inverse + up[bands + f : bands + f + part]
        value = value.astype(BF).reshape(part * w, plan.rows)
        value = jnp.dot(value, natural_ref[...], preferred_element_type=F32)
        strip_ref[pl.ds(f, part)] = value.astype(BF).reshape(part, w, plan.rows)
        copies.append(
            pltpu.make_async_copy(
                strip_ref.at[pl.ds(f, part)], out_ref.at[pl.ds(f, part)], sems.at[len(copies)]
            )
        )
        copies[-1].start()
    for copy in copies:
        copy.wait()


def on_chip(value):
    return pltpu.with_memory_space_constraint(value, pltpu.VMEM)


def off_chip(value):
    return pltpu.with_memory_space_constraint(value, pltpu.HBM)


def strip_local(scenes, cloud, destination, offset, counts):
    n, m = lax.axis_size("tx"), lax.axis_size("ty")
    bands = scenes.shape[2]
    plan = Plan(n, m, bands)
    planes = bands + 1
    area = BS * BS
    vmem = pl.BlockSpec(memory_space=pltpu.VMEM)
    smem = pl.BlockSpec(memory_space=pltpu.SMEM)
    hbm = pl.BlockSpec(memory_space=pl.ANY)
    blocks = jnp.swapaxes(scenes[0], 0, 1)
    pack = pl.pallas_call(
        functools.partial(pack_kernel, plan),
        out_shape=pltpu.VMEM((plan.code_at + CODE_ROWS, 2 * S_DEV), BF),
        in_specs=[smem] + [hbm] * 4,
        out_specs=vmem,
        scratch_shapes=[
            pltpu.VMEM((planes, S_DEV, area), BF),
            pltpu.VMEM(destination.shape, jnp.int32),
            pltpu.VMEM(offset.shape, jnp.int32),
            pltpu.SemaphoreType.DMA((4,)),
        ],
        compiler_params=pltpu.CompilerParams(vmem_limit_bytes=4 << 20),
        name="pack",
    )(counts, *[off_chip(v) for v in (blocks, cloud[0], destination, offset)])

    def call(kernel, operands, outputs, scratch=(), flops=0, out_specs=None):
        return pl.pallas_call(
            functools.partial(kernel, plan),
            out_shape=outputs,
            in_specs=[vmem] * len(operands),
            out_specs=out_specs or jax.tree.map(lambda _: vmem, outputs),
            scratch_shapes=list(scratch),
            compiler_params=pltpu.CompilerParams(vmem_limit_bytes=16 << 20),
            cost_estimate=pl.CostEstimate(flops=flops, bytes_accessed=1 << 20, transcendentals=0),
        )(*[on_chip(v) for v in operands])

    shrinks = row_shrinks(plan.rows)
    row1 = shrinks[0].T[plan.row_of]
    row2 = shrinks[1].T[plan.row_of]
    top = plan.rows >> 3
    wide_top = max(top, 128)
    padded = np.zeros((plan.rows, wide_top))
    padded[:, :top] = shrinks[2].T[plan.row_of]
    row3 = np.stack(split_table(padded))
    grow3 = np.zeros((wide_top, plan.rows >> 2))
    grow3[:top] = grow_grid(top).T
    grow2 = grow_grid(plan.rows >> 2).T
    grow1 = grow_grid(plan.rows >> 1).T[:, plan.row_of]
    natural = np.eye(plan.rows)[plan.row_of]
    constants = [plan.column_tables(), row1, row2, row3, grow1, grow2, grow3, natural]
    constants = [off_chip(jnp.asarray(table.astype(BF))) for table in constants]
    loaded = pl.pallas_call(
        functools.partial(load_kernel, plan),
        out_shape=[pltpu.VMEM(c.shape[k == 0 :], BF) for k, c in enumerate(constants)],
        in_specs=[hbm] * len(constants),
        out_specs=[vmem] * len(constants),
        scratch_shapes=[pltpu.SemaphoreType.DMA((len(constants),))],
        compiler_params=pltpu.CompilerParams(vmem_limit_bytes=4 << 20),
        name="load",
    )(*constants)
    tables, grows = list(loaded[:4]), list(loaded[4:])
    size = plan.size
    shapes = [
        (planes, size[0], plan.rows),
        (planes, size[1], plan.rows >> 1),
        (planes, size[2], plan.rows >> 2),
        (planes, size[3], wide_top),
    ]
    edge_shape = (up8(EDGE * planes), sum(s[-1] for s in shapes[1:]))
    sums_shape = pltpu.VMEM((planes * plan.half, 2 * plan.slots), F32)
    prod_shape = (planes * plan.half, 4 * S_DEV)
    work = 2 * planes * area * plan.slots * 2 * S_DEV

    across = [(i, n - 1 - i) for i in range(n)]
    beside = [(i, i ^ 1) for i in range(n)]
    far = lax.ppermute(pack, "tx", across)
    near = lax.ppermute(pack, "tx", beside)
    edge_work = [
        pltpu.VMEM((planes * plan.half, TS), F32),
        pltpu.VMEM((2, plan.near, plan.rows), BF),
        pltpu.VMEM((LEVELS - 1, planes, 8, plan.rows), F32),
    ]
    sums_and_edge = [sums_shape, pltpu.VMEM(edge_shape, BF)]
    sums, edge_far = call(
        own_kernel,
        [pack] + tables,
        sums_and_edge,
        [pltpu.VMEM(prod_shape, BF)] + edge_work,
        flops=work,
    )

    def over(value, shift):
        pairs = []
        for t in range(n):
            for j in range(m):
                target = t ^ shift
                pairs.append((t * m + j, target * m + (j + 1 if 2 * target < n else j - 1) % m))
        return lax.ppermute(value, ("tx", "ty"), pairs)

    edge_far = over(edge_far, n // 2)
    late = lax.ppermute(far, "tx", beside)
    sums, edge_near = call(
        first_kernel,
        [far, near, sums] + tables,
        sums_and_edge,
        [pltpu.VMEM((2, *prod_shape), BF)] + edge_work,
        flops=4 * work,
    )
    edge_near = over(edge_near, 0)
    levels = call(
        place_kernel,
        [late, sums] + tables,
        [pltpu.VMEM(s, F32) for s in shapes],
        [
            pltpu.VMEM(prod_shape, BF),
            pltpu.VMEM(sums_shape.shape, F32),
            pltpu.VMEM((2, 2 * TS, plan.rows), BF),
        ]
        + [pltpu.VMEM((planes, s, plan.rows), F32) for s in size[1:]],
        flops=4 * work,
    )
    out = call(
        blend_kernel,
        [*levels, edge_near, edge_far, *grows],
        jax.ShapeDtypeStruct((bands, size[0], plan.rows), BF),
        [
            pltpu.VMEM(shapes[1], F32),
            pltpu.VMEM(shapes[2], F32),
            pltpu.VMEM(shapes[3], F32),
            pltpu.VMEM((2 * bands, (plan.rows >> 2) // TS, size[2], TS), F32),
            pltpu.VMEM((2 * bands, (plan.rows >> 1) // TS, size[1], TS), F32),
            pltpu.VMEM((2 * bands, (plan.rows >> 1) // TS, size[0], TS), F32),
            pltpu.VMEM((bands, size[0], plan.rows), BF),
            pltpu.SemaphoreType.DMA((2,)),
        ],
        flops=4 * work,
        out_specs=hbm,
    )
    return out[:, None]


def strip_step(*arguments):
    return strip_local(*arguments)


def use_strips(n, m):
    spread = max(2, 2 * S_DEV // n)
    return n == 4 and TS // n >= 32 and m >= 2 and S_DEV <= 2 * spread


def solution(mesh):
    placed = (
        P(("region", "ty"), "tx", "band", None),
        P(("region", "ty"), "tx", None),
        P(("region", "ty"), "tx"),
        P(("region", "ty"), "tx"),
        P(("region", "ty"), "tx"),
    )
    strips = use_strips(mesh.shape["tx"], mesh.shape["ty"])
    return jax.shard_map(
        strip_step if strips else local,
        mesh=mesh,
        in_specs=placed,
        out_specs=P("band", ("region", "ty"), "tx", None),
        check_vma=False,
    )
```

```python
import functools

import jax
import jax.numpy as jnp
import numpy as np
from jax import lax
from jax.experimental import pallas as pl
from jax.experimental.pallas import tpu as pltpu
from jax.sharding import PartitionSpec as P


TS = 128
BS = 16
S_DEV = 64
MARGIN = 32
LEVELS = 4
SLOTS = 64


BINOMIAL = (0.0625, 0.25, 0.375, 0.25, 0.0625)
BACKGROUND = 0.25


def with_halo(shard, sides, width):
    for axis, dim in sides:
        devices, length = (lax.axis_size(axis), shard.shape[dim])
        up = [(i, (i + 1) % devices) for i in range(devices - 1)]
        down = [(j, i) for i, j in up]
        last = lax.slice_in_dim(shard, length - width, length, axis=dim)
        leading = lax.slice_in_dim(shard, 0, width, axis=dim)
        before = lax.ppermute(last, axis, up)
        after = lax.ppermute(leading, axis, down)
        shard = jnp.concatenate([before, shard, after], axis=dim)
    return shard


def shrink_table(length, rim_in, rim_out):
    extent = length - 2 * rim_in
    outputs = extent // 2 + 2 * rim_out
    first_index = rim_in - 2 - 2 * rim_out
    out_pos = jnp.arange(outputs, dtype=jnp.int32)[:, None]
    in_pos = jnp.arange(length, dtype=jnp.int32)[None, :]
    spacing = in_pos - first_index - 2 * out_pos
    table = jnp.zeros((outputs, length), jnp.float32)
    for tap_index, tap_weight in enumerate(BINOMIAL):
        table = table + tap_weight * (spacing == tap_index).astype(jnp.float32)
    return table


def grow_table(length, rim_in, rim_out):
    excess = 2 * rim_in - 2 - rim_out
    outputs = 2 * (length - 2) - 2 * excess
    paired = jnp.arange(outputs, dtype=jnp.int32)[:, None] + excess
    source = paired // 2
    parity = paired % 2
    spacing = jnp.arange(length, dtype=jnp.int32)[None, :] - source
    even_part = (
        0.125 * (spacing == 0).astype(jnp.float32)
        + 0.75 * (spacing == 1).astype(jnp.float32)
        + 0.125 * (spacing == 2).astype(jnp.float32)
    )
    odd_part = 0.5 * (spacing == 1).astype(jnp.float32) + 0.5 * (spacing == 2).astype(jnp.float32)
    return jnp.where(parity == 0, even_part, odd_part)


def apply_both(field, row_table, col_table):
    rows_done = jnp.einsum("ki,bic->bkc", row_table, field, precision=lax.Precision.HIGHEST)
    return jnp.einsum("bkc,mc->bkm", rows_done, col_table, precision=lax.Precision.HIGHEST)


def shrink(field, rim_in, rim_out):
    row_table = shrink_table(field.shape[-2], rim_in, rim_out)
    col_table = shrink_table(field.shape[-1], rim_in, rim_out)
    return apply_both(field, row_table, col_table)


def grow(field, rim_in, rim_out):
    row_table = grow_table(field.shape[-2], rim_in, rim_out)
    col_table = grow_table(field.shape[-1], rim_in, rim_out)
    return apply_both(field, row_table, col_table)


def trim(field, rim_have, rim_want):
    excess = rim_have - rim_want
    return field[..., excess : field.shape[-2] - excess, excess : field.shape[-1] - excess]


def border(extent, rim, begin, whole):
    position = begin - rim + jnp.arange(extent + 2 * rim, dtype=jnp.int32)
    return ((position >= 0) & (position < whole)).astype(jnp.float32)


def local(scenes, cloud, destination, offset, counts):
    row_tiles = lax.axis_size("tx")
    col_tiles = lax.axis_size("ty")
    row_tile = lax.axis_index("tx")
    col_tile = lax.axis_index("ty")
    spread = max(2, 2 * S_DEV // row_tiles)
    blocks = scenes[0]
    weights = cloud[0]
    target_row = destination[0]
    placed = offset[0]
    live_count = counts[0, 0]
    own_bands = blocks.shape[1]
    living = jnp.arange(S_DEV, dtype=jnp.int32) < live_count
    matches = (target_row[:, None] == jnp.arange(row_tiles, dtype=jnp.int32)[None, :]) & living[
        :, None
    ]
    ordinal = jnp.cumsum(matches.astype(jnp.int32), axis=0) - 1
    ranking = jnp.sum(jnp.where(matches, ordinal, 0), axis=1)
    target = target_row * spread + ranking
    chooser = (
        (jnp.arange(row_tiles * spread, dtype=jnp.int32)[:, None] == target[None, :])
        & living[None, :]
    ).astype(jnp.bfloat16)
    merged = jnp.concatenate([blocks, weights[:, None, :]], axis=1).reshape(
        S_DEV, (own_bands + 1) * BS * BS
    )
    packed = jnp.dot(chooser, merged, preferred_element_type=jnp.float32).astype(jnp.bfloat16)
    packed = packed.reshape(row_tiles, spread, own_bands + 1, BS * BS)
    slot_ids = jnp.arange(SLOTS, dtype=jnp.int32)
    tag_send = jnp.dot(
        chooser, (placed + 1).astype(jnp.bfloat16)[:, None], preferred_element_type=jnp.float32
    )
    tag_send = tag_send.astype(jnp.bfloat16).reshape(row_tiles, spread)
    arrived, tag_back = (
        lax.all_to_all(packed, "tx", split_axis=0, concat_axis=0, tiled=True),
        lax.all_to_all(tag_send, "tx", split_axis=0, concat_axis=0, tiled=True),
    )
    landing = (slot_ids + 1).astype(jnp.float32)[:, None] == tag_back.reshape(-1).astype(
        jnp.float32
    )[None, :]
    arrived = arrived.reshape(row_tiles * spread, own_bands + 1, BS * BS)
    coverage = arrived[:, own_bands:].astype(jnp.float32)
    payload = jnp.concatenate(
        [arrived[:, :own_bands].astype(jnp.float32) * coverage, coverage], axis=1
    )
    payload = payload.reshape(row_tiles * spread, (own_bands + 1) * BS * BS)
    slot_sums = jnp.dot(landing.astype(jnp.float32), payload, precision=lax.Precision.HIGHEST)
    per_row = TS // BS
    tile_field = slot_sums.reshape(per_row, per_row, own_bands + 1, BS, BS).transpose(2, 0, 3, 1, 4)
    tile_field = tile_field.reshape(own_bands + 1, TS, TS)

    def masked(field, extent, rim):
        row_mask = border(extent, rim, row_tile * extent, extent * row_tiles)
        col_mask = border(extent, rim, col_tile * extent, extent * col_tiles)
        return field * row_mask[:, None] * col_mask[None, :]

    def enlarge(field, rim_in, rim_out):
        return grow(field, rim_in, rim_out)

    ground = with_halo(tile_field, (("tx", 1), ("ty", 2)), MARGIN)
    margin = MARGIN
    needed = [0]
    for _ in range(1, LEVELS):
        needed.append((needed[-1] + 3) // 2)
    pyramid = [(ground, margin)]
    extent = TS
    for _ in range(1, LEVELS):
        source, rim_in = pyramid[-1]
        rim_out = (rim_in - 2) // 2
        extent = extent // 2
        reduced = masked(shrink(source, rim_in, rim_out), extent, rim_out)
        pyramid.append((reduced, rim_out))
    deepest = LEVELS - 1
    summit, rim_top = pyramid[-1]
    summit = trim(summit, rim_top, needed[deepest])
    collapsed = summit[:own_bands] / (BACKGROUND + summit[own_bands])
    for tier_index in range(LEVELS - 2, -1, -1):
        current, rim_here = pyramid[tier_index]
        coarser, rim_below = pyramid[tier_index + 1]
        current = trim(current, rim_here, needed[tier_index])
        detail = current[:own_bands] - enlarge(coarser[:own_bands], rim_below, needed[tier_index])
        band_part = detail / (BACKGROUND + current[own_bands])
        collapsed = band_part + enlarge(collapsed, needed[tier_index + 1], needed[tier_index])
        collapsed = masked(collapsed, TS >> tier_index, needed[tier_index])
    blended = collapsed.astype(jnp.bfloat16)
    flipped = jnp.swapaxes(blended, 1, 2)
    strips = lax.all_to_all(flipped, "tx", split_axis=1, concat_axis=2, tiled=True)
    return strips[:, None]


BF = jnp.bfloat16
F32 = jnp.float32
EDGE = 3
CODE_ROWS = 8
DEAD = -1024


def up8(v):
    return -(-v // 8) * 8


def shrink_grid(length):
    table = np.zeros((length // 2, length))
    for i in range(length // 2):
        for tap, weight in enumerate(BINOMIAL):
            k = 2 * i + tap - 2
            if 0 <= k < length:
                table[i, k] += weight
    return table


def grow_grid(length):
    table = np.zeros((2 * length, length))
    for i in range(length):
        for k, weight in ((i - 1, 0.125), (i, 0.75), (i + 1, 0.125)):
            if 0 <= k < length:
                table[2 * i, k] += weight
        for k in (i, i + 1):
            if k < length:
                table[2 * i + 1, k] += 0.5
    return table


def split_table(table):
    high = table.astype(BF)
    return high, (table - high.astype(np.float64)).astype(BF)


def row_shrinks(rows):
    tables, current = [], np.eye(rows)
    for level in range(1, LEVELS):
        current = shrink_grid(rows >> (level - 1)) @ current
        tables.append(current)
    return tables


class Plan:
    def __init__(self, n, m, bands):
        self.n, self.m, self.bands = n, m, bands
        self.rows = n * TS
        self.strip = TS // n
        self.slots = n * SLOTS
        self.slot_rows = n * (TS // BS)
        w = self.strip
        self.held = [w, w // 2 + 2, w // 4 + 3, w // 8 + 3]
        self.size = [w] + [up8(h) for h in self.held[1:]]
        self.first = [0, -1, -1, -1]
        self.at = [0]
        for size in self.size:
            self.at.append(self.at[-1] + size)
        self.low_at = self.at[LEVELS]
        self.main = self.low_at + self.size[3]
        self.edge_rows = 8 * (LEVELS - 1)
        self.total = self.main + 2 * self.edge_rows
        self.near = 2 * BS
        self.half = BS * BS // 2
        self.weight_at = bands * self.half
        self.code_at = self.weight_at + self.half
        order = np.arange(self.rows)
        wide = self.slot_rows
        u, half, v = order // (4 * wide), order // (2 * wide) % 2, order // wide % 2
        self.row_of = order % wide * BS + half * (BS // 2) + 2 * u + v

    def column_tables(self):
        n, m, w = self.n, self.m, self.strip
        width = m * TS
        grids = [np.eye(width)] + row_shrinks(width)
        tables = np.zeros((n, m, self.total, TS))
        for t in range(n):
            for j in range(m):
                for level in range(LEVELS):
                    base = ((j * TS + t * w) >> level) + self.first[level]
                    for k in range(self.held[level]):
                        o = base + k
                        if 0 <= o < width >> level:
                            tables[t, j, self.at[level] + k] = grids[level][o, j * TS : (j + 1) * TS]
                    for which, target in enumerate((t, t ^ n // 2)):
                        right = 2 * target < n
                        base = ((j + 1 if right else j) * TS >> level) - 1
                        at = self.main + which * self.edge_rows + 8 * (level - 1)
                        for k in range(EDGE if level else 0):
                            if 0 <= base + k < width >> level:
                                row = grids[level][base + k, j * TS : (j + 1) * TS]
                                row = row[TS - self.near :] if right else row[: self.near]
                                tables[t, j, at + k, : self.near] = row
        high, low = split_table(tables)
        high[:, :, self.low_at : self.main] = low[:, :, self.at[3] : self.at[4]]
        return np.concatenate([high, high], axis=-1).reshape(n * m, self.total, 2 * TS)


def halves(value):
    high = value.astype(BF)
    return high, (value - high.astype(F32)).astype(BF)


def dot2(value, table):
    high, low = halves(value)
    return jnp.dot(high, table, preferred_element_type=F32) + jnp.dot(
        low, table, preferred_element_type=F32
    )


def turned(plan, block):
    return jnp.concatenate([block[:, : plan.half], block[:, plan.half :]], axis=0).T


def pack_kernel(plan, count_ref, scenes_ref, cloud_ref, dest_ref, offset_ref, out_ref, note_ref, raw,
                dest, offset, sems):
    rows = 2 * S_DEV
    half = plan.half
    copies = [
        pltpu.make_async_copy(source, target, sems.at[k])
        for k, (source, target) in enumerate(
            (
                (dest_ref, dest),
                (offset_ref, offset),
                (cloud_ref, raw.at[plan.bands]),
                (scenes_ref, raw.at[pl.ds(0, plan.bands)]),
            )
        )
    ]
    for copy in copies:
        copy.start()
    for copy in copies[:2]:
        copy.wait()
    per_row = TS // BS
    slot = offset[...]
    code = (slot % per_row) * plan.slot_rows + dest[...] * per_row + slot // per_row
    live = lax.broadcasted_iota(jnp.int32, (1, S_DEV), 1) < count_ref[0, 0]
    code = jnp.where(live, code, DEAD).astype(F32)
    code = jnp.broadcast_to(jnp.concatenate([code, code], axis=1), (CODE_ROWS, rows))
    out_ref[plan.code_at :, :] = code.astype(BF)
    for f in (plan.bands, *range(plan.bands)):
        if f == plan.bands:
            copies[2].wait()
        elif f == 0:
            copies[3].wait()
        out_ref[f * half : (f + 1) * half, :] = turned(plan, raw[f])
    note_ref[...] = out_ref[plan.weight_at :, :]


def load_kernel(plan, column_ref, *refs):
    count = (len(refs) - 2) // 2
    sources, targets, sems = refs[:count], refs[count:-1], refs[-1]
    mine = lax.axis_index("tx") * plan.m + lax.axis_index("ty")
    copies = [
        pltpu.make_async_copy(source, target, sems.at[k])
        for k, (source, target) in enumerate(zip((column_ref.at[mine], *sources), targets))
    ]
    for copy in copies:
        copy.start()
    for copy in copies:
        copy.wait()


def landing_of(plan, codes):
    codes = codes.astype(F32).T[:, :1]
    blocks = codes.shape[0]
    pair = float(2 * plan.slot_rows)
    second = lax.broadcasted_iota(jnp.int32, (blocks, 1), 0) >= S_DEV
    codes = codes + pair * jnp.floor(codes / pair) + jnp.where(second, pair, 0.0)
    slot = lax.broadcasted_iota(jnp.int32, (blocks, 2 * plan.slots), 1).astype(F32)
    landing = jnp.where(slot == codes, 1.0, 0.0).astype(BF)
    return jnp.concatenate([landing, landing], axis=0)


def slot_sums(plan, scenes, note, prod_ref):
    half, blocks = plan.half, 2 * S_DEV
    weight = note[:half, :]
    for f in range(plan.bands):
        rows = pl.ds(f * half, half)
        if len(scenes.shape) == 3:
            value = turned(plan, scenes[f])
        else:
            value = scenes[f * half : (f + 1) * half, :]
        high, low = halves(value.astype(F32) * weight.astype(F32))
        prod_ref[rows, :blocks] = high
        prod_ref[rows, blocks:] = low
    rows = pl.ds(plan.weight_at, half)
    prod_ref[rows, :blocks] = weight
    prod_ref[rows, blocks:] = jnp.zeros_like(weight)
    return jnp.dot(prod_ref[...], landing_of(plan, note[half:, :]), preferred_element_type=F32)


def turn(plan, a, b):
    wide = plan.slot_rows
    odd = lax.broadcasted_iota(jnp.int32, a.shape, 1) // wide % 2 == 1
    return jnp.where(odd, pltpu.roll(b, wide, 1), a), jnp.where(odd, b, pltpu.roll(a, TS - wide, 1))


def twin_sum(value):
    return value + pltpu.roll(value, value.shape[-1] // 2, value.ndim - 1)


def edge_of(plan, side_ref, table, row1_ref, row23_ref, out_ref, tile_ref, z1_ref, z23_ref):
    planes = plan.bands + 1
    rows = plan.rows
    for f in range(planes):
        tile = tile_ref.at[f % 2]
        for u in range(BS // 4):
            at = f * plan.half + 2 * u * BS
            pair = turn(plan, side_ref[at : at + BS], side_ref[at + BS : at + 2 * BS])
            for k, value in enumerate(pair):
                tile[k * BS : (k + 1) * BS, u * TS : (u + 1) * TS] = value.astype(BF)
        cols = jnp.dot(table, tile[...], preferred_element_type=F32)
        z1_ref[f] = cols[:8]
        z23_ref[f] = cols[8:]
    out_ref[...] = jnp.zeros(out_ref.shape, out_ref.dtype)
    z1 = z1_ref[...].reshape(planes * 8, rows).astype(BF)
    z1 = jnp.dot(z1, row1_ref[...], preferred_element_type=F32).reshape(planes, 8, rows // 2)
    z23 = z23_ref[...].reshape(planes * 16, rows).astype(BF)
    z23 = jnp.dot(z23, row23_ref[...], preferred_element_type=F32).reshape(planes, 16, rows // 2)
    second = rows // 2 + rows // 4
    for f in range(planes):
        at = pl.ds(EDGE * f, EDGE)
        out_ref[at, : rows // 2] = z1[f, :EDGE].astype(BF)
        out_ref[at, rows // 2 : second] = z23[f, :EDGE, : rows // 4].astype(BF)
        top = twin_sum(z23[f, 8:, rows // 4 :])
        out_ref[at, second:] = top[:EDGE].astype(BF)


def side_of(plan, sums, right):
    return jnp.where(right, sums[:, 2 * plan.slots - TS :], sums[:, :TS])


def own_kernel(plan, pack, column_ref, row1_ref, row23_ref,
               out_ref, edge_ref, prod_ref, side_ref, tile_ref, z1_ref, z23_ref):
    right = 2 * (lax.axis_index("tx") ^ plan.n // 2) < plan.n
    sums = slot_sums(plan, pack, pack.at[pl.ds(plan.weight_at, plan.half + CODE_ROWS)], prod_ref)
    out_ref[...] = sums
    side_ref[...] = side_of(plan, sums, right)
    table = column_ref[plan.main + plan.edge_rows :, : plan.near]
    edge_of(plan, side_ref, table, row1_ref, row23_ref, edge_ref, tile_ref, z1_ref, z23_ref)


def first_kernel(plan, far, note, near, before_ref, column_ref, row1_ref, row23_ref,
                 out_ref, edge_ref, prod_ref, side_ref, tile_ref, z1_ref, z23_ref):
    right = 2 * lax.axis_index("tx") < plan.n
    near_note = near.at[pl.ds(plan.weight_at, plan.half + CODE_ROWS)]
    sums = slot_sums(plan, near, near_note, prod_ref.at[0])
    sums = before_ref[...] + sums + slot_sums(plan, far, note, prod_ref.at[1])
    out_ref[...] = sums
    side_ref[...] = side_of(plan, sums, right)
    table = column_ref[plan.main : plan.main + plan.edge_rows, : plan.near]
    edge_of(plan, side_ref, table, row1_ref, row23_ref, edge_ref, tile_ref, z1_ref, z23_ref)


def tile_of(plan, sums, at, tile_ref):
    for pair in range(2 * plan.slots // TS):
        lanes = slice(pair * TS, (pair + 1) * TS)
        for u in range(BS // 4):
            row = at + 2 * u * BS
            both = turn(plan, sums[row : row + BS, lanes], sums[row + BS : row + 2 * BS, lanes])
            for k, value in enumerate(both):
                high, low = halves(value)
                row = (2 * pair + k) * BS
                tile_ref[row : row + BS, u * TS : (u + 1) * TS] = high
                tile_ref[TS + row : TS + row + BS, u * TS : (u + 1) * TS] = low


def place_kernel(plan, late, note, before_ref, column_ref, row1_ref, row23_ref,
                 a0_ref, a1_ref, a2_ref, a3_ref, prod_ref, sums_ref, tile_ref, z1_ref, z23_ref):
    column = column_ref[: plan.main, :]
    at, size = plan.at, plan.size
    planes = plan.bands + 1
    rows = plan.rows
    sums_ref[...] = before_ref[...] + slot_sums(plan, late, note, prod_ref)
    for f in range(planes):
        tile = tile_ref.at[f % 2]
        tile_of(plan, sums_ref, f * plan.half, tile)
        cols = jnp.dot(column, tile[...], preferred_element_type=F32)
        a0_ref[f] = cols[at[0] : at[1]]
        z1_ref[f] = cols[at[1] : at[2]]
        z23_ref[f, : size[2]] = cols[at[2] : at[3]]
        z23_ref[f, size[2] :] = cols[at[3] : at[4]] + cols[plan.low_at : plan.main]
    z1 = dot2(z1_ref[...].reshape(planes * size[1], rows), row1_ref[...])
    a1_ref[...] = z1.reshape(a1_ref.shape)
    z23 = dot2(z23_ref[...].reshape(planes * (size[2] + size[3]), rows), row23_ref[...])
    z23 = z23.reshape(planes, size[2] + size[3], rows // 2)
    a2_ref[...] = z23[:, : size[2], : rows // 4]
    for f in range(planes):
        a3_ref[f] = twin_sum(z23[f, size[2] :, rows // 4 :])


def grow_columns(value, outputs):
    half = outputs // 2
    a, b, c = value[:, :half], value[:, 1 : half + 1], value[:, 2 : half + 2]
    return (a + b) * 0.5, (a + 6.0 * b + c) * 0.125


def weave(even, odd, ref, size):
    k, half, lanes = even.shape
    if 2 * half < size:
        ref[...] = jnp.zeros(ref.shape, F32)
    for q in range(k):
        for chunk in range(lanes // TS):
            part = slice(chunk * TS, (chunk + 1) * TS)
            ref[q, chunk, pl.ds(0, half, stride=2), :] = even[q][:, part]
            ref[q, chunk, pl.ds(1, half, stride=2), :] = odd[q][:, part]
    return jnp.concatenate([ref[:, chunk] for chunk in range(lanes // TS)], axis=-1)


def blend_kernel(plan, a0_ref, a1_ref, a2_ref, a3_ref, near_ref, far_ref, grow1_ref, grow2_ref, grow3_ref,
                 natural_ref, out_ref, g1_ref, g2_ref, g3_ref, e2_ref, e1_ref, e0_ref, strip_ref, sems):
    bands = plan.bands
    planes = bands + 1
    w = plan.strip
    row_tile, col_tile = lax.axis_index("tx"), lax.axis_index("ty")
    first, last = row_tile == 0, row_tile == plan.n - 1
    left, right = first & (col_tile > 0), last & (col_tile < plan.m - 1)
    first, last = first & (col_tile == 0), last & (col_tile == plan.m - 1)
    edges = near_ref[...].astype(F32) + far_ref[...].astype(F32)
    start = 0
    for level, (src, dst) in enumerate(((a1_ref, g1_ref), (a2_ref, g2_ref), (a3_ref, g3_ref)), 1):
        lanes = src.shape[-1]
        dst[...] = src[...]
        for f in range(planes):
            edge = edges[EDGE * f : EDGE * (f + 1), start : start + lanes]
            far = w >> level
            dst[f, :EDGE] += jnp.where(left, edge, 0.0)
            dst[f, far : far + EDGE] += jnp.where(right, edge, 0.0)
        start += lanes

    def inside(level, columns):
        column = lax.broadcasted_iota(jnp.int32, (columns, 1), 0) - 1
        keep = ((column >= 0) | ~first) & ((column < (w >> level)) | ~last)
        return keep.astype(F32)

    top = g3_ref[...]
    blend = top[:bands] / (BACKGROUND + top[bands:])
    for level, cur_ref, below_ref, grow_ref, up_ref in (
        (2, g2_ref, g3_ref, grow3_ref, e2_ref),
        (1, g1_ref, g2_ref, grow2_ref, e1_ref),
    ):
        stacked = jnp.concatenate([below_ref[:bands], blend], axis=0)
        k, c, r = stacked.shape
        wide = dot2(stacked.reshape(k * c, r), grow_ref[...])
        wide = wide.reshape(k, c, wide.shape[-1])
        pairs = up8(plan.held[level]) // 2
        pairs = min(pairs, c - 2)
        even, odd = grow_columns(wide, 2 * pairs)
        size = cur_ref.shape[1]
        up = weave(even, odd, up_ref, size)
        current = cur_ref[...]
        inverse = 1.0 / (BACKGROUND + current[bands])
        blend = (current[:bands] - up[:bands]) * inverse + up[bands:]
        blend = blend * inside(level, blend.shape[1])
    stacked = jnp.concatenate([g1_ref[:bands], blend], axis=0)
    half = w // 2
    a, b, c = stacked[:, :half], stacked[:, 1 : half + 1], stacked[:, 2 : half + 2]
    even, odd = (a + 6.0 * b + c) * 0.125, (b + c) * 0.5
    tall = weave(even, odd, e0_ref, w)
    up = dot2(tall.reshape(2 * bands * w, tall.shape[-1]), grow1_ref[...])
    up = up.reshape(2 * bands, w, plan.rows)
    inverse = 1.0 / (BACKGROUND + a0_ref[bands])
    copies = []
    part = bands // 2
    for f in range(0, bands, part):
        value = (a0_ref[f : f + part] - up[f : f + part]) * inverse + up[bands + f : bands + f + part]
        value = value.astype(BF).reshape(part * w, plan.rows)
        value = jnp.dot(value, natural_ref[...], preferred_element_type=F32)
        strip_ref[pl.ds(f, part)] = value.astype(BF).reshape(part, w, plan.rows)
        copies.append(
            pltpu.make_async_copy(
                strip_ref.at[pl.ds(f, part)], out_ref.at[pl.ds(f, part)], sems.at[len(copies)]
            )
        )
        copies[-1].start()
    for copy in copies:
        copy.wait()


def on_chip(value):
    return pltpu.with_memory_space_constraint(value, pltpu.VMEM)


def off_chip(value):
    return pltpu.with_memory_space_constraint(value, pltpu.HBM)


def strip_local(scenes, cloud, destination, offset, counts):
    n, m = lax.axis_size("tx"), lax.axis_size("ty")
    bands = scenes.shape[2]
    plan = Plan(n, m, bands)
    planes = bands + 1
    area = BS * BS
    vmem = pl.BlockSpec(memory_space=pltpu.VMEM)
    smem = pl.BlockSpec(memory_space=pltpu.SMEM)
    hbm = pl.BlockSpec(memory_space=pl.ANY)
    blocks = jnp.swapaxes(scenes[0], 0, 1)

    def call(kernel, operands, outputs, scratch=(), flops=0, out_specs=None):
        return pl.pallas_call(
            functools.partial(kernel, plan),
            out_shape=outputs,
            in_specs=[vmem] * len(operands),
            out_specs=out_specs or jax.tree.map(lambda _: vmem, outputs),
            scratch_shapes=list(scratch),
            compiler_params=pltpu.CompilerParams(vmem_limit_bytes=16 << 20),
            cost_estimate=pl.CostEstimate(flops=flops, bytes_accessed=1 << 20, transcendentals=0),
        )(*[on_chip(v) for v in operands])

    shrinks = row_shrinks(plan.rows)
    row1 = shrinks[0].T[plan.row_of]
    row2 = shrinks[1].T[plan.row_of]
    top = plan.rows >> 3
    wide_top = 2 * top
    row23 = np.concatenate([row2, *split_table(shrinks[2].T[plan.row_of])], axis=1)
    grow3 = np.zeros((wide_top, plan.rows >> 2))
    grow3[:top] = grow_grid(top).T
    grow2 = grow_grid(plan.rows >> 2).T
    grow1 = grow_grid(plan.rows >> 1).T[:, plan.row_of]
    natural = np.eye(plan.rows)[plan.row_of]
    constants = [plan.column_tables(), row1, row23, grow1, grow2, grow3, natural]
    constants = [off_chip(jnp.asarray(table.astype(BF))) for table in constants]
    loaded = pl.pallas_call(
        functools.partial(load_kernel, plan),
        out_shape=[pltpu.VMEM(c.shape[k == 0 :], BF) for k, c in enumerate(constants)],
        in_specs=[hbm] * len(constants),
        out_specs=[vmem] * len(constants),
        scratch_shapes=[pltpu.SemaphoreType.DMA((len(constants),))],
        compiler_params=pltpu.CompilerParams(vmem_limit_bytes=4 << 20),
        name="load",
    )(*constants)
    tables, grows = list(loaded[:3]), list(loaded[3:])
    size = plan.size
    shapes = [
        (planes, size[0], plan.rows),
        (planes, size[1], plan.rows >> 1),
        (planes, size[2], plan.rows >> 2),
        (planes, size[3], wide_top),
    ]
    edge_shape = (up8(EDGE * planes), sum(s[-1] for s in shapes[1:]))
    sums_shape = pltpu.VMEM((planes * plan.half, 2 * plan.slots), F32)
    prod_shape = (planes * plan.half, 4 * S_DEV)
    work = 2 * planes * area * plan.slots * 2 * S_DEV

    across = [(i, n - 1 - i) for i in range(n)]
    beside = [(i, i ^ 1) for i in range(n)]
    far = lax.ppermute(blocks, "tx", across)
    pack, note = pl.pallas_call(
        functools.partial(pack_kernel, plan),
        out_shape=[
            pltpu.VMEM((plan.code_at + CODE_ROWS, 2 * S_DEV), BF),
            pltpu.VMEM((plan.half + CODE_ROWS, 2 * S_DEV), BF),
        ],
        in_specs=[smem] + [hbm] * 4,
        out_specs=[vmem] * 2,
        scratch_shapes=[
            pltpu.VMEM((planes, S_DEV, area), BF),
            pltpu.VMEM(destination.shape, jnp.int32),
            pltpu.VMEM(offset.shape, jnp.int32),
            pltpu.SemaphoreType.DMA((4,)),
        ],
        compiler_params=pltpu.CompilerParams(vmem_limit_bytes=4 << 20),
        name="pack",
    )(counts, *[off_chip(v) for v in (blocks, cloud[0], destination, offset)])

    far_note = lax.ppermute(note, "tx", across)
    near = lax.ppermute(pack, "tx", beside)
    edge_work = [
        pltpu.VMEM((planes * plan.half, TS), F32),
        pltpu.VMEM((2, plan.near, plan.rows), BF),
        pltpu.VMEM((planes, 8, plan.rows), F32),
        pltpu.VMEM((planes, 16, plan.rows), F32),
    ]
    sums_and_edge = [sums_shape, pltpu.VMEM(edge_shape, BF)]
    sums, edge_far = call(
        own_kernel,
        [pack] + tables,
        sums_and_edge,
        [pltpu.VMEM(prod_shape, BF)] + edge_work,
        flops=work,
    )

    def over(value, shift):
        pairs = []
        for t in range(n):
            for j in range(m):
                target = t ^ shift
                pairs.append((t * m + j, target * m + (j + 1 if 2 * target < n else j - 1) % m))
        return lax.ppermute(value, ("tx", "ty"), pairs)

    edge_far = over(edge_far, n // 2)
    late = lax.ppermute(far, "tx", beside)
    late_note = lax.ppermute(far_note, "tx", beside)
    sums, edge_near = call(
        first_kernel,
        [far, far_note, near, sums] + tables,
        sums_and_edge,
        [pltpu.VMEM((2, *prod_shape), BF)] + edge_work,
        flops=4 * work,
    )
    edge_near = over(edge_near, 0)
    levels = call(
        place_kernel,
        [late, late_note, sums] + tables,
        [pltpu.VMEM(s, F32) for s in shapes],
        [
            pltpu.VMEM(prod_shape, BF),
            pltpu.VMEM(sums_shape.shape, F32),
            pltpu.VMEM((2, 2 * TS, plan.rows), BF),
            pltpu.VMEM((planes, size[1], plan.rows), F32),
            pltpu.VMEM((planes, size[2] + size[3], plan.rows), F32),
        ],
        flops=4 * work,
    )
    out = call(
        blend_kernel,
        [*levels, edge_near, edge_far, *grows],
        jax.ShapeDtypeStruct((bands, size[0], plan.rows), BF),
        [
            pltpu.VMEM(shapes[1], F32),
            pltpu.VMEM(shapes[2], F32),
            pltpu.VMEM(shapes[3], F32),
            pltpu.VMEM((2 * bands, (plan.rows >> 2) // TS, size[2], TS), F32),
            pltpu.VMEM((2 * bands, (plan.rows >> 1) // TS, size[1], TS), F32),
            pltpu.VMEM((2 * bands, (plan.rows >> 1) // TS, size[0], TS), F32),
            pltpu.VMEM((bands, size[0], plan.rows), BF),
            pltpu.SemaphoreType.DMA((2,)),
        ],
        flops=4 * work,
        out_specs=hbm,
    )
    return out[:, None]


def strip_step(*arguments):
    return strip_local(*arguments)


def use_strips(n, m):
    spread = max(2, 2 * S_DEV // n)
    return n == 4 and TS // n >= 32 and m >= 2 and S_DEV <= 2 * spread


def solution(mesh):
    placed = (
        P(("region", "ty"), "tx", "band", None),
        P(("region", "ty"), "tx", None),
        P(("region", "ty"), "tx"),
        P(("region", "ty"), "tx"),
        P(("region", "ty"), "tx"),
    )
    strips = use_strips(mesh.shape["tx"], mesh.shape["ty"])
    return jax.shard_map(
        strip_step if strips else local,
        mesh=mesh,
        in_specs=placed,
        out_specs=P("band", ("region", "ty"), "tx", None),
        check_vma=False,
    )
```

```python
import functools

import jax
import jax.numpy as jnp
import numpy as np
from jax import lax
from jax.experimental import pallas as pl
from jax.experimental.pallas import tpu as pltpu
from jax.sharding import PartitionSpec as P


TS = 128
BS = 16
S_DEV = 64
MARGIN = 32
LEVELS = 4
SLOTS = 64


BINOMIAL = (0.0625, 0.25, 0.375, 0.25, 0.0625)
BACKGROUND = 0.25


def with_halo(shard, sides, width):
    for axis, dim in sides:
        devices, length = (lax.axis_size(axis), shard.shape[dim])
        up = [(i, (i + 1) % devices) for i in range(devices - 1)]
        down = [(j, i) for i, j in up]
        last = lax.slice_in_dim(shard, length - width, length, axis=dim)
        leading = lax.slice_in_dim(shard, 0, width, axis=dim)
        before = lax.ppermute(last, axis, up)
        after = lax.ppermute(leading, axis, down)
        shard = jnp.concatenate([before, shard, after], axis=dim)
    return shard


def shrink_table(length, rim_in, rim_out):
    extent = length - 2 * rim_in
    outputs = extent // 2 + 2 * rim_out
    first_index = rim_in - 2 - 2 * rim_out
    out_pos = jnp.arange(outputs, dtype=jnp.int32)[:, None]
    in_pos = jnp.arange(length, dtype=jnp.int32)[None, :]
    spacing = in_pos - first_index - 2 * out_pos
    table = jnp.zeros((outputs, length), jnp.float32)
    for tap_index, tap_weight in enumerate(BINOMIAL):
        table = table + tap_weight * (spacing == tap_index).astype(jnp.float32)
    return table


def grow_table(length, rim_in, rim_out):
    excess = 2 * rim_in - 2 - rim_out
    outputs = 2 * (length - 2) - 2 * excess
    paired = jnp.arange(outputs, dtype=jnp.int32)[:, None] + excess
    source = paired // 2
    parity = paired % 2
    spacing = jnp.arange(length, dtype=jnp.int32)[None, :] - source
    even_part = (
        0.125 * (spacing == 0).astype(jnp.float32)
        + 0.75 * (spacing == 1).astype(jnp.float32)
        + 0.125 * (spacing == 2).astype(jnp.float32)
    )
    odd_part = 0.5 * (spacing == 1).astype(jnp.float32) + 0.5 * (spacing == 2).astype(jnp.float32)
    return jnp.where(parity == 0, even_part, odd_part)


def apply_both(field, row_table, col_table):
    rows_done = jnp.einsum("ki,bic->bkc", row_table, field, precision=lax.Precision.HIGHEST)
    return jnp.einsum("bkc,mc->bkm", rows_done, col_table, precision=lax.Precision.HIGHEST)


def shrink(field, rim_in, rim_out):
    row_table = shrink_table(field.shape[-2], rim_in, rim_out)
    col_table = shrink_table(field.shape[-1], rim_in, rim_out)
    return apply_both(field, row_table, col_table)


def grow(field, rim_in, rim_out):
    row_table = grow_table(field.shape[-2], rim_in, rim_out)
    col_table = grow_table(field.shape[-1], rim_in, rim_out)
    return apply_both(field, row_table, col_table)


def trim(field, rim_have, rim_want):
    excess = rim_have - rim_want
    return field[..., excess : field.shape[-2] - excess, excess : field.shape[-1] - excess]


def border(extent, rim, begin, whole):
    position = begin - rim + jnp.arange(extent + 2 * rim, dtype=jnp.int32)
    return ((position >= 0) & (position < whole)).astype(jnp.float32)


def local(scenes, cloud, destination, offset, counts):
    row_tiles = lax.axis_size("tx")
    col_tiles = lax.axis_size("ty")
    row_tile = lax.axis_index("tx")
    col_tile = lax.axis_index("ty")
    spread = max(2, 2 * S_DEV // row_tiles)
    blocks = scenes[0]
    weights = cloud[0]
    target_row = destination[0]
    placed = offset[0]
    live_count = counts[0, 0]
    own_bands = blocks.shape[1]
    living = jnp.arange(S_DEV, dtype=jnp.int32) < live_count
    matches = (target_row[:, None] == jnp.arange(row_tiles, dtype=jnp.int32)[None, :]) & living[
        :, None
    ]
    ordinal = jnp.cumsum(matches.astype(jnp.int32), axis=0) - 1
    ranking = jnp.sum(jnp.where(matches, ordinal, 0), axis=1)
    target = target_row * spread + ranking
    chooser = (
        (jnp.arange(row_tiles * spread, dtype=jnp.int32)[:, None] == target[None, :])
        & living[None, :]
    ).astype(jnp.bfloat16)
    merged = jnp.concatenate([blocks, weights[:, None, :]], axis=1).reshape(
        S_DEV, (own_bands + 1) * BS * BS
    )
    packed = jnp.dot(chooser, merged, preferred_element_type=jnp.float32).astype(jnp.bfloat16)
    packed = packed.reshape(row_tiles, spread, own_bands + 1, BS * BS)
    slot_ids = jnp.arange(SLOTS, dtype=jnp.int32)
    tag_send = jnp.dot(
        chooser, (placed + 1).astype(jnp.bfloat16)[:, None], preferred_element_type=jnp.float32
    )
    tag_send = tag_send.astype(jnp.bfloat16).reshape(row_tiles, spread)
    arrived, tag_back = (
        lax.all_to_all(packed, "tx", split_axis=0, concat_axis=0, tiled=True),
        lax.all_to_all(tag_send, "tx", split_axis=0, concat_axis=0, tiled=True),
    )
    landing = (slot_ids + 1).astype(jnp.float32)[:, None] == tag_back.reshape(-1).astype(
        jnp.float32
    )[None, :]
    arrived = arrived.reshape(row_tiles * spread, own_bands + 1, BS * BS)
    coverage = arrived[:, own_bands:].astype(jnp.float32)
    payload = jnp.concatenate(
        [arrived[:, :own_bands].astype(jnp.float32) * coverage, coverage], axis=1
    )
    payload = payload.reshape(row_tiles * spread, (own_bands + 1) * BS * BS)
    slot_sums = jnp.dot(landing.astype(jnp.float32), payload, precision=lax.Precision.HIGHEST)
    per_row = TS // BS
    tile_field = slot_sums.reshape(per_row, per_row, own_bands + 1, BS, BS).transpose(2, 0, 3, 1, 4)
    tile_field = tile_field.reshape(own_bands + 1, TS, TS)

    def masked(field, extent, rim):
        row_mask = border(extent, rim, row_tile * extent, extent * row_tiles)
        col_mask = border(extent, rim, col_tile * extent, extent * col_tiles)
        return field * row_mask[:, None] * col_mask[None, :]

    def enlarge(field, rim_in, rim_out):
        return grow(field, rim_in, rim_out)

    ground = with_halo(tile_field, (("tx", 1), ("ty", 2)), MARGIN)
    margin = MARGIN
    needed = [0]
    for _ in range(1, LEVELS):
        needed.append((needed[-1] + 3) // 2)
    pyramid = [(ground, margin)]
    extent = TS
    for _ in range(1, LEVELS):
        source, rim_in = pyramid[-1]
        rim_out = (rim_in - 2) // 2
        extent = extent // 2
        reduced = masked(shrink(source, rim_in, rim_out), extent, rim_out)
        pyramid.append((reduced, rim_out))
    deepest = LEVELS - 1
    summit, rim_top = pyramid[-1]
    summit = trim(summit, rim_top, needed[deepest])
    collapsed = summit[:own_bands] / (BACKGROUND + summit[own_bands])
    for tier_index in range(LEVELS - 2, -1, -1):
        current, rim_here = pyramid[tier_index]
        coarser, rim_below = pyramid[tier_index + 1]
        current = trim(current, rim_here, needed[tier_index])
        detail = current[:own_bands] - enlarge(coarser[:own_bands], rim_below, needed[tier_index])
        band_part = detail / (BACKGROUND + current[own_bands])
        collapsed = band_part + enlarge(collapsed, needed[tier_index + 1], needed[tier_index])
        collapsed = masked(collapsed, TS >> tier_index, needed[tier_index])
    blended = collapsed.astype(jnp.bfloat16)
    flipped = jnp.swapaxes(blended, 1, 2)
    strips = lax.all_to_all(flipped, "tx", split_axis=1, concat_axis=2, tiled=True)
    return strips[:, None]


BF = jnp.bfloat16
F32 = jnp.float32
EDGE = 3
CODE_ROWS = 8
DEAD = -1024


def up8(v):
    return -(-v // 8) * 8


def shrink_grid(length):
    table = np.zeros((length // 2, length))
    for i in range(length // 2):
        for tap, weight in enumerate(BINOMIAL):
            k = 2 * i + tap - 2
            if 0 <= k < length:
                table[i, k] += weight
    return table


def grow_grid(length):
    table = np.zeros((2 * length, length))
    for i in range(length):
        for k, weight in ((i - 1, 0.125), (i, 0.75), (i + 1, 0.125)):
            if 0 <= k < length:
                table[2 * i, k] += weight
        for k in (i, i + 1):
            if k < length:
                table[2 * i + 1, k] += 0.5
    return table


def split_table(table):
    high = table.astype(BF)
    return high, (table - high.astype(np.float64)).astype(BF)


def row_shrinks(rows):
    tables, current = [], np.eye(rows)
    for level in range(1, LEVELS):
        current = shrink_grid(rows >> (level - 1)) @ current
        tables.append(current)
    return tables


class Plan:
    def __init__(self, n, m, bands):
        self.n, self.m, self.bands = n, m, bands
        self.rows = n * TS
        self.strip = TS // n
        self.slots = n * SLOTS
        self.slot_rows = n * (TS // BS)
        w = self.strip
        self.held = [w, w // 2 + 2, w // 4 + 3, w // 8 + 3]
        self.size = [w] + [up8(h) for h in self.held[1:]]
        self.first = [0, -1, -1, -1]
        self.at = [0]
        for size in self.size:
            self.at.append(self.at[-1] + size)
        self.low_at = self.at[LEVELS]
        self.main = self.low_at + self.size[3]
        self.edge_rows = 8 * (LEVELS - 1)
        self.total = self.main + 2 * self.edge_rows
        self.near = 2 * BS
        self.half = BS * BS // 2
        self.weight_at = bands * self.half
        self.code_at = self.weight_at + self.half
        order = np.arange(self.rows)
        wide = self.slot_rows
        u, half, v = order // (4 * wide), order // (2 * wide) % 2, order // wide % 2
        self.row_of = order % wide * BS + half * (BS // 2) + 2 * u + v

    def column_tables(self):
        n, m, w = self.n, self.m, self.strip
        width = m * TS
        grids = [np.eye(width)] + row_shrinks(width)
        tables = np.zeros((n, m, self.total, TS))
        for t in range(n):
            for j in range(m):
                for level in range(LEVELS):
                    base = ((j * TS + t * w) >> level) + self.first[level]
                    for k in range(self.held[level]):
                        o = base + k
                        if 0 <= o < width >> level:
                            tables[t, j, self.at[level] + k] = grids[level][o, j * TS : (j + 1) * TS]
                    for which, target in enumerate((t, t ^ n // 2)):
                        right = 2 * target < n
                        base = ((j + 1 if right else j) * TS >> level) - 1
                        at = self.main + which * self.edge_rows + 8 * (level - 1)
                        for k in range(EDGE if level else 0):
                            if 0 <= base + k < width >> level:
                                row = grids[level][base + k, j * TS : (j + 1) * TS]
                                row = row[TS - self.near :] if right else row[: self.near]
                                tables[t, j, at + k, : self.near] = row
        high, low = split_table(tables)
        high[:, :, self.low_at : self.main] = low[:, :, self.at[3] : self.at[4]]
        return np.concatenate([high, high], axis=-1).reshape(n * m, self.total, 2 * TS)


def halves(value):
    high = value.astype(BF)
    return high, (value - high.astype(F32)).astype(BF)


def dot2(value, table):
    high, low = halves(value)
    return jnp.dot(high, table, preferred_element_type=F32) + jnp.dot(
        low, table, preferred_element_type=F32
    )


def turned(plan, block):
    return jnp.concatenate([block[:, : plan.half], block[:, plan.half :]], axis=0).T


def pack_kernel(plan, count_ref, scenes_ref, cloud_ref, dest_ref, offset_ref, out_ref, note_ref, raw,
                dest, offset, sems):
    rows = 2 * S_DEV
    half = plan.half
    copies = [
        pltpu.make_async_copy(source, target, sems.at[k])
        for k, (source, target) in enumerate(
            (
                (dest_ref, dest),
                (offset_ref, offset),
                (cloud_ref, raw.at[plan.bands]),
                (scenes_ref, raw.at[pl.ds(0, plan.bands)]),
            )
        )
    ]
    for copy in copies:
        copy.start()
    for copy in copies[:2]:
        copy.wait()
    per_row = TS // BS
    slot = offset[...]
    code = (slot % per_row) * plan.slot_rows + dest[...] * per_row + slot // per_row
    live = lax.broadcasted_iota(jnp.int32, (1, S_DEV), 1) < count_ref[0, 0]
    code = jnp.where(live, code, DEAD).astype(F32)
    code = jnp.broadcast_to(jnp.concatenate([code, code], axis=1), (CODE_ROWS, rows))
    out_ref[plan.code_at :, :] = code.astype(BF)
    for f in (plan.bands, *range(plan.bands)):
        if f == plan.bands:
            copies[2].wait()
        elif f == 0:
            copies[3].wait()
        out_ref[f * half : (f + 1) * half, :] = turned(plan, raw[f])
    note_ref[...] = out_ref[plan.weight_at :, :]


def load_kernel(plan, column_ref, *refs):
    count = (len(refs) - 2) // 2
    sources, targets, sems = refs[:count], refs[count:-1], refs[-1]
    mine = lax.axis_index("tx") * plan.m + lax.axis_index("ty")
    copies = [
        pltpu.make_async_copy(source, target, sems.at[k])
        for k, (source, target) in enumerate(zip((column_ref.at[mine], *sources), targets))
    ]
    for copy in copies:
        copy.start()
    for copy in copies:
        copy.wait()


def landing_of(plan, codes):
    codes = codes.astype(F32).T[:, :1]
    blocks = codes.shape[0]
    pair = float(2 * plan.slot_rows)
    second = lax.broadcasted_iota(jnp.int32, (blocks, 1), 0) >= S_DEV
    codes = codes + pair * jnp.floor(codes / pair) + jnp.where(second, pair, 0.0)
    slot = lax.broadcasted_iota(jnp.int32, (blocks, 2 * plan.slots), 1).astype(F32)
    landing = jnp.where(slot == codes, 1.0, 0.0).astype(BF)
    return jnp.concatenate([landing, landing], axis=0)


def slot_sums(plan, scenes, note, prod_ref):
    half, blocks = plan.half, 2 * S_DEV
    weight = note[:half, :]
    for f in range(plan.bands):
        rows = pl.ds(f * half, half)
        if len(scenes.shape) == 3:
            value = turned(plan, scenes[f])
        else:
            value = scenes[f * half : (f + 1) * half, :]
        high, low = halves(value.astype(F32) * weight.astype(F32))
        prod_ref[rows, :blocks] = high
        prod_ref[rows, blocks:] = low
    rows = pl.ds(plan.weight_at, half)
    prod_ref[rows, :blocks] = weight
    prod_ref[rows, blocks:] = jnp.zeros_like(weight)
    return jnp.dot(prod_ref[...], landing_of(plan, note[half:, :]), preferred_element_type=F32)


def turn(plan, a, b):
    wide = plan.slot_rows
    odd = lax.broadcasted_iota(jnp.int32, a.shape, 1) // wide % 2 == 1
    return jnp.where(odd, pltpu.roll(b, wide, 1), a), jnp.where(odd, b, pltpu.roll(a, TS - wide, 1))


def twin_sum(value):
    return value + pltpu.roll(value, value.shape[-1] // 2, value.ndim - 1)


def edge_of(plan, side_ref, table, row1_ref, row23_ref, out_ref, tile_ref, z1_ref, z23_ref):
    planes = plan.bands + 1
    rows = plan.rows
    for f in range(planes):
        tile = tile_ref.at[f % 2]
        for u in range(BS // 4):
            at = f * plan.half + 2 * u * BS
            pair = turn(plan, side_ref[at : at + BS], side_ref[at + BS : at + 2 * BS])
            for k, value in enumerate(pair):
                tile[k * BS : (k + 1) * BS, u * TS : (u + 1) * TS] = value.astype(BF)
        cols = jnp.dot(table, tile[...], preferred_element_type=F32)
        z1_ref[f] = cols[:8]
        z23_ref[f] = cols[8:]
    out_ref[...] = jnp.zeros(out_ref.shape, out_ref.dtype)
    z1 = z1_ref[...].reshape(planes * 8, rows).astype(BF)
    z1 = jnp.dot(z1, row1_ref[...], preferred_element_type=F32).reshape(planes, 8, rows // 2)
    z23 = z23_ref[...].reshape(planes * 16, rows).astype(BF)
    z23 = jnp.dot(z23, row23_ref[...], preferred_element_type=F32).reshape(planes, 16, rows // 2)
    second = rows // 2 + rows // 4
    for f in range(planes):
        at = pl.ds(EDGE * f, EDGE)
        out_ref[at, : rows // 2] = z1[f, :EDGE].astype(BF)
        out_ref[at, rows // 2 : second] = z23[f, :EDGE, : rows // 4].astype(BF)
        top = twin_sum(z23[f, 8:, rows // 4 :])
        out_ref[at, second:] = top[:EDGE].astype(BF)


def side_of(plan, sums, right):
    return jnp.where(right, sums[:, 2 * plan.slots - TS :], sums[:, :TS])


def own_kernel(plan, pack, column_ref, row1_ref, row23_ref,
               out_ref, edge_ref, prod_ref, side_ref, tile_ref, z1_ref, z23_ref):
    right = 2 * (lax.axis_index("tx") ^ plan.n // 2) < plan.n
    sums = slot_sums(plan, pack, pack.at[pl.ds(plan.weight_at, plan.half + CODE_ROWS)], prod_ref)
    out_ref[...] = sums
    side_ref[...] = side_of(plan, sums, right)
    table = column_ref[plan.main + plan.edge_rows :, : plan.near]
    edge_of(plan, side_ref, table, row1_ref, row23_ref, edge_ref, tile_ref, z1_ref, z23_ref)


def first_kernel(plan, far, note, near, before_ref, column_ref, row1_ref, row23_ref,
                 out_ref, edge_ref, prod_ref, side_ref, tile_ref, z1_ref, z23_ref):
    right = 2 * lax.axis_index("tx") < plan.n
    near_note = near.at[pl.ds(plan.weight_at, plan.half + CODE_ROWS)]
    sums = slot_sums(plan, near, near_note, prod_ref.at[0])
    sums = before_ref[...] + sums + slot_sums(plan, far, note, prod_ref.at[1])
    out_ref[...] = sums
    side_ref[...] = side_of(plan, sums, right)
    table = column_ref[plan.main : plan.main + plan.edge_rows, : plan.near]
    edge_of(plan, side_ref, table, row1_ref, row23_ref, edge_ref, tile_ref, z1_ref, z23_ref)


def tile_of(plan, sums, at, tile_ref):
    for pair in range(2 * plan.slots // TS):
        lanes = slice(pair * TS, (pair + 1) * TS)
        for u in range(BS // 4):
            row = at + 2 * u * BS
            both = turn(plan, sums[row : row + BS, lanes], sums[row + BS : row + 2 * BS, lanes])
            for k, value in enumerate(both):
                high, low = halves(value)
                row = (2 * pair + k) * BS
                tile_ref[row : row + BS, u * TS : (u + 1) * TS] = high
                tile_ref[TS + row : TS + row + BS, u * TS : (u + 1) * TS] = low


def place_kernel(plan, late, note, before_ref, column_ref, row1_ref, row23_ref,
                 a0_ref, a1_ref, a2_ref, a3_ref, prod_ref, sums_ref, tile_ref, z1_ref, z23_ref):
    column = column_ref[: plan.main, :]
    at, size = plan.at, plan.size
    planes = plan.bands + 1
    rows = plan.rows
    sums_ref[...] = before_ref[...] + slot_sums(plan, late, note, prod_ref)
    for f in range(planes):
        tile = tile_ref.at[f % 2]
        tile_of(plan, sums_ref, f * plan.half, tile)
        cols = jnp.dot(column, tile[...], preferred_element_type=F32)
        a0_ref[f] = cols[at[0] : at[1]]
        z1_ref[f] = cols[at[1] : at[2]]
        z23_ref[f, : size[2]] = cols[at[2] : at[3]]
        z23_ref[f, size[2] :] = cols[at[3] : at[4]] + cols[plan.low_at : plan.main]
    z1 = dot2(z1_ref[...].reshape(planes * size[1], rows), row1_ref[...])
    a1_ref[...] = z1.reshape(a1_ref.shape)
    z23 = dot2(z23_ref[...].reshape(planes * (size[2] + size[3]), rows), row23_ref[...])
    z23 = z23.reshape(planes, size[2] + size[3], rows // 2)
    a2_ref[...] = z23[:, : size[2], : rows // 4]
    for f in range(planes):
        a3_ref[f] = twin_sum(z23[f, size[2] :, rows // 4 :])


def grow_columns(value, outputs):
    half = outputs // 2
    a, b, c = value[:, :half], value[:, 1 : half + 1], value[:, 2 : half + 2]
    return (a + b) * 0.5, (a + 6.0 * b + c) * 0.125


def weave(even, odd, ref, size):
    k, half, lanes = even.shape
    if 2 * half < size:
        ref[...] = jnp.zeros(ref.shape, F32)
    for q in range(k):
        for chunk in range(lanes // TS):
            part = slice(chunk * TS, (chunk + 1) * TS)
            ref[q, chunk, pl.ds(0, half, stride=2), :] = even[q][:, part]
            ref[q, chunk, pl.ds(1, half, stride=2), :] = odd[q][:, part]
    return jnp.concatenate([ref[:, chunk] for chunk in range(lanes // TS)], axis=-1)


def blend_kernel(plan, a0_ref, a1_ref, a2_ref, a3_ref, near_ref, far_ref, grow1_ref, grow2_ref, grow3_ref,
                 natural_ref, out_ref, g1_ref, g2_ref, g3_ref, e2_ref, e1_ref, e0_ref, strip_ref, sems):
    bands = plan.bands
    planes = bands + 1
    w = plan.strip
    row_tile, col_tile = lax.axis_index("tx"), lax.axis_index("ty")
    first, last = row_tile == 0, row_tile == plan.n - 1
    left, right = first & (col_tile > 0), last & (col_tile < plan.m - 1)
    first, last = first & (col_tile == 0), last & (col_tile == plan.m - 1)
    edges = near_ref[...].astype(F32) + far_ref[...].astype(F32)
    start = 0
    for level, (src, dst) in enumerate(((a1_ref, g1_ref), (a2_ref, g2_ref), (a3_ref, g3_ref)), 1):
        lanes = src.shape[-1]
        dst[...] = src[...]
        for f in range(planes):
            edge = edges[EDGE * f : EDGE * (f + 1), start : start + lanes]
            far = w >> level
            dst[f, :EDGE] += jnp.where(left, edge, 0.0)
            dst[f, far : far + EDGE] += jnp.where(right, edge, 0.0)
        start += lanes

    def inside(level, columns):
        column = lax.broadcasted_iota(jnp.int32, (columns, 1), 0) - 1
        keep = ((column >= 0) | ~first) & ((column < (w >> level)) | ~last)
        return keep.astype(F32)

    def grown(level, value, up_ref):
        k, c, r = value.shape
        if level == 0:
            half = w // 2
            x, y, z = value[:, :half], value[:, 1 : half + 1], value[:, 2 : half + 2]
            tall = weave((x + 6.0 * y + z) * 0.125, (y + z) * 0.5, up_ref, w)
            return dot2(tall.reshape(k * w, r), grow1_ref[...]).reshape(k, w, plan.rows)
        grow_ref = (grow2_ref, grow3_ref)[level - 1]
        wide = dot2(value.reshape(k * c, r), grow_ref[...])
        wide = wide.reshape(k, c, wide.shape[-1])
        pairs = min(up8(plan.held[level]) // 2, c - 2)
        return weave(*grow_columns(wide, 2 * pairs), up_ref, plan.size[level])

    e2a_ref, e1a_ref, e0a_ref = (ref.at[pl.ds(0, bands)] for ref in (e2_ref, e1_ref, e0_ref))
    e2b_ref, e1b_ref, e0b_ref = (ref.at[pl.ds(bands, bands)] for ref in (e2_ref, e1_ref, e0_ref))
    inverses = [1.0 / (BACKGROUND + ref[bands]) for ref in (a0_ref, g1_ref, g2_ref, g3_ref)]
    blend = g3_ref[:bands] * inverses[3]
    detail2 = (g2_ref[:bands] - grown(2, g3_ref[:bands], e2a_ref)) * inverses[2]
    blend = (detail2 + grown(2, blend, e2b_ref)) * inside(2, plan.size[2])
    detail1 = (g1_ref[:bands] - grown(1, g2_ref[:bands], e1a_ref)) * inverses[1]
    blend = (detail1 + grown(1, blend, e1b_ref)) * inside(1, plan.size[1])
    detail0 = (a0_ref[:bands] - grown(0, g1_ref[:bands], e0a_ref)) * inverses[0]
    up = grown(0, blend, e0b_ref)
    copies = []
    part = bands // 2
    for f in range(0, bands, part):
        value = detail0[f : f + part] + up[f : f + part]
        value = value.astype(BF).reshape(part * w, plan.rows)
        value = jnp.dot(value, natural_ref[...], preferred_element_type=F32)
        strip_ref[pl.ds(f, part)] = value.astype(BF).reshape(part, w, plan.rows)
        copies.append(
            pltpu.make_async_copy(
                strip_ref.at[pl.ds(f, part)], out_ref.at[pl.ds(f, part)], sems.at[len(copies)]
            )
        )
        copies[-1].start()
    for copy in copies:
        copy.wait()


def on_chip(value):
    return pltpu.with_memory_space_constraint(value, pltpu.VMEM)


def off_chip(value):
    return pltpu.with_memory_space_constraint(value, pltpu.HBM)


def strip_local(scenes, cloud, destination, offset, counts):
    n, m = lax.axis_size("tx"), lax.axis_size("ty")
    bands = scenes.shape[2]
    plan = Plan(n, m, bands)
    planes = bands + 1
    area = BS * BS
    vmem = pl.BlockSpec(memory_space=pltpu.VMEM)
    smem = pl.BlockSpec(memory_space=pltpu.SMEM)
    hbm = pl.BlockSpec(memory_space=pl.ANY)
    blocks = jnp.swapaxes(scenes[0], 0, 1)

    def call(kernel, operands, outputs, scratch=(), flops=0, out_specs=None):
        return pl.pallas_call(
            functools.partial(kernel, plan),
            out_shape=outputs,
            in_specs=[vmem] * len(operands),
            out_specs=out_specs or jax.tree.map(lambda _: vmem, outputs),
            scratch_shapes=list(scratch),
            compiler_params=pltpu.CompilerParams(vmem_limit_bytes=16 << 20),
            cost_estimate=pl.CostEstimate(flops=flops, bytes_accessed=1 << 20, transcendentals=0),
        )(*[on_chip(v) for v in operands])

    shrinks = row_shrinks(plan.rows)
    row1 = shrinks[0].T[plan.row_of]
    row2 = shrinks[1].T[plan.row_of]
    top = plan.rows >> 3
    wide_top = 2 * top
    row23 = np.concatenate([row2, *split_table(shrinks[2].T[plan.row_of])], axis=1)
    grow3 = np.zeros((wide_top, plan.rows >> 2))
    grow3[:top] = grow_grid(top).T
    grow2 = grow_grid(plan.rows >> 2).T
    grow1 = grow_grid(plan.rows >> 1).T[:, plan.row_of]
    natural = np.eye(plan.rows)[plan.row_of]
    constants = [plan.column_tables(), row1, row23, grow1, grow2, grow3, natural]
    constants = [off_chip(jnp.asarray(table.astype(BF))) for table in constants]
    loaded = pl.pallas_call(
        functools.partial(load_kernel, plan),
        out_shape=[pltpu.VMEM(c.shape[k == 0 :], BF) for k, c in enumerate(constants)],
        in_specs=[hbm] * len(constants),
        out_specs=[vmem] * len(constants),
        scratch_shapes=[pltpu.SemaphoreType.DMA((len(constants),))],
        compiler_params=pltpu.CompilerParams(vmem_limit_bytes=4 << 20),
        name="load",
    )(*constants)
    tables, grows = list(loaded[:3]), list(loaded[3:])
    size = plan.size
    shapes = [
        (planes, size[0], plan.rows),
        (planes, size[1], plan.rows >> 1),
        (planes, size[2], plan.rows >> 2),
        (planes, size[3], wide_top),
    ]
    edge_shape = (up8(EDGE * planes), sum(s[-1] for s in shapes[1:]))
    sums_shape = pltpu.VMEM((planes * plan.half, 2 * plan.slots), F32)
    prod_shape = (planes * plan.half, 4 * S_DEV)
    work = 2 * planes * area * plan.slots * 2 * S_DEV

    across = [(i, n - 1 - i) for i in range(n)]
    beside = [(i, i ^ 1) for i in range(n)]
    far = lax.ppermute(blocks, "tx", across)
    pack, note = pl.pallas_call(
        functools.partial(pack_kernel, plan),
        out_shape=[
            pltpu.VMEM((plan.code_at + CODE_ROWS, 2 * S_DEV), BF),
            pltpu.VMEM((plan.half + CODE_ROWS, 2 * S_DEV), BF),
        ],
        in_specs=[smem] + [hbm] * 4,
        out_specs=[vmem] * 2,
        scratch_shapes=[
            pltpu.VMEM((planes, S_DEV, area), BF),
            pltpu.VMEM(destination.shape, jnp.int32),
            pltpu.VMEM(offset.shape, jnp.int32),
            pltpu.SemaphoreType.DMA((4,)),
        ],
        compiler_params=pltpu.CompilerParams(vmem_limit_bytes=4 << 20),
        name="pack",
    )(counts, *[off_chip(v) for v in (blocks, cloud[0], destination, offset)])

    far_note = lax.ppermute(note, "tx", across)
    near = lax.ppermute(pack, "tx", beside)
    edge_work = [
        pltpu.VMEM((planes * plan.half, TS), F32),
        pltpu.VMEM((2, plan.near, plan.rows), BF),
        pltpu.VMEM((planes, 8, plan.rows), F32),
        pltpu.VMEM((planes, 16, plan.rows), F32),
    ]
    sums_and_edge = [sums_shape, pltpu.VMEM(edge_shape, BF)]
    sums, edge_far = call(
        own_kernel,
        [pack] + tables,
        sums_and_edge,
        [pltpu.VMEM(prod_shape, BF)] + edge_work,
        flops=work,
    )

    def over(value, shift):
        pairs = []
        for t in range(n):
            for j in range(m):
                target = t ^ shift
                pairs.append((t * m + j, target * m + (j + 1 if 2 * target < n else j - 1) % m))
        return lax.ppermute(value, ("tx", "ty"), pairs)

    edge_far = over(edge_far, n // 2)
    late = lax.ppermute(far, "tx", beside)
    late_note = lax.ppermute(far_note, "tx", beside)
    sums, edge_near = call(
        first_kernel,
        [far, far_note, near, sums] + tables,
        sums_and_edge,
        [pltpu.VMEM((2, *prod_shape), BF)] + edge_work,
        flops=4 * work,
    )
    edge_near = over(edge_near, 0)
    levels = call(
        place_kernel,
        [late, late_note, sums] + tables,
        [pltpu.VMEM(s, F32) for s in shapes],
        [
            pltpu.VMEM(prod_shape, BF),
            pltpu.VMEM(sums_shape.shape, F32),
            pltpu.VMEM((2, 2 * TS, plan.rows), BF),
            pltpu.VMEM((planes, size[1], plan.rows), F32),
            pltpu.VMEM((planes, size[2] + size[3], plan.rows), F32),
        ],
        flops=4 * work,
    )
    out = call(
        blend_kernel,
        [*levels, edge_near, edge_far, *grows],
        jax.ShapeDtypeStruct((bands, size[0], plan.rows), BF),
        [
            pltpu.VMEM(shapes[1], F32),
            pltpu.VMEM(shapes[2], F32),
            pltpu.VMEM(shapes[3], F32),
            pltpu.VMEM((2 * bands, (plan.rows >> 2) // TS, size[2], TS), F32),
            pltpu.VMEM((2 * bands, (plan.rows >> 1) // TS, size[1], TS), F32),
            pltpu.VMEM((2 * bands, (plan.rows >> 1) // TS, size[0], TS), F32),
            pltpu.VMEM((bands, size[0], plan.rows), BF),
            pltpu.SemaphoreType.DMA((2,)),
        ],
        flops=4 * work,
        out_specs=hbm,
    )
    return out[:, None]


def strip_step(*arguments):
    return strip_local(*arguments)


def use_strips(n, m):
    spread = max(2, 2 * S_DEV // n)
    return n == 4 and TS // n >= 32 and m >= 2 and S_DEV <= 2 * spread


def solution(mesh):
    placed = (
        P(("region", "ty"), "tx", "band", None),
        P(("region", "ty"), "tx", None),
        P(("region", "ty"), "tx"),
        P(("region", "ty"), "tx"),
        P(("region", "ty"), "tx"),
    )
    strips = use_strips(mesh.shape["tx"], mesh.shape["ty"])
    return jax.shard_map(
        strip_step if strips else local,
        mesh=mesh,
        in_specs=placed,
        out_specs=P("band", ("region", "ty"), "tx", None),
        check_vma=False,
    )
```

```python
import functools

import jax
import jax.numpy as jnp
import numpy as np
from jax import lax
from jax.experimental import pallas as pl
from jax.experimental.pallas import tpu as pltpu
from jax.sharding import PartitionSpec as P


TS = 128
BS = 16
S_DEV = 64
MARGIN = 32
LEVELS = 4
SLOTS = 64


BINOMIAL = (0.0625, 0.25, 0.375, 0.25, 0.0625)
BACKGROUND = 0.25


def with_halo(shard, sides, width):
    for axis, dim in sides:
        devices, length = (lax.axis_size(axis), shard.shape[dim])
        up = [(i, (i + 1) % devices) for i in range(devices - 1)]
        down = [(j, i) for i, j in up]
        last = lax.slice_in_dim(shard, length - width, length, axis=dim)
        leading = lax.slice_in_dim(shard, 0, width, axis=dim)
        before = lax.ppermute(last, axis, up)
        after = lax.ppermute(leading, axis, down)
        shard = jnp.concatenate([before, shard, after], axis=dim)
    return shard


def shrink_table(length, rim_in, rim_out):
    extent = length - 2 * rim_in
    outputs = extent // 2 + 2 * rim_out
    first_index = rim_in - 2 - 2 * rim_out
    out_pos = jnp.arange(outputs, dtype=jnp.int32)[:, None]
    in_pos = jnp.arange(length, dtype=jnp.int32)[None, :]
    spacing = in_pos - first_index - 2 * out_pos
    table = jnp.zeros((outputs, length), jnp.float32)
    for tap_index, tap_weight in enumerate(BINOMIAL):
        table = table + tap_weight * (spacing == tap_index).astype(jnp.float32)
    return table


def grow_table(length, rim_in, rim_out):
    excess = 2 * rim_in - 2 - rim_out
    outputs = 2 * (length - 2) - 2 * excess
    paired = jnp.arange(outputs, dtype=jnp.int32)[:, None] + excess
    source = paired // 2
    parity = paired % 2
    spacing = jnp.arange(length, dtype=jnp.int32)[None, :] - source
    even_part = (
        0.125 * (spacing == 0).astype(jnp.float32)
        + 0.75 * (spacing == 1).astype(jnp.float32)
        + 0.125 * (spacing == 2).astype(jnp.float32)
    )
    odd_part = 0.5 * (spacing == 1).astype(jnp.float32) + 0.5 * (spacing == 2).astype(jnp.float32)
    return jnp.where(parity == 0, even_part, odd_part)


def apply_both(field, row_table, col_table):
    rows_done = jnp.einsum("ki,bic->bkc", row_table, field, precision=lax.Precision.HIGHEST)
    return jnp.einsum("bkc,mc->bkm", rows_done, col_table, precision=lax.Precision.HIGHEST)


def shrink(field, rim_in, rim_out):
    row_table = shrink_table(field.shape[-2], rim_in, rim_out)
    col_table = shrink_table(field.shape[-1], rim_in, rim_out)
    return apply_both(field, row_table, col_table)


def grow(field, rim_in, rim_out):
    row_table = grow_table(field.shape[-2], rim_in, rim_out)
    col_table = grow_table(field.shape[-1], rim_in, rim_out)
    return apply_both(field, row_table, col_table)


def trim(field, rim_have, rim_want):
    excess = rim_have - rim_want
    return field[..., excess : field.shape[-2] - excess, excess : field.shape[-1] - excess]


def border(extent, rim, begin, whole):
    position = begin - rim + jnp.arange(extent + 2 * rim, dtype=jnp.int32)
    return ((position >= 0) & (position < whole)).astype(jnp.float32)


def local(scenes, cloud, destination, offset, counts):
    row_tiles = lax.axis_size("tx")
    col_tiles = lax.axis_size("ty")
    row_tile = lax.axis_index("tx")
    col_tile = lax.axis_index("ty")
    spread = max(2, 2 * S_DEV // row_tiles)
    blocks = scenes[0]
    weights = cloud[0]
    target_row = destination[0]
    placed = offset[0]
    live_count = counts[0, 0]
    own_bands = blocks.shape[1]
    living = jnp.arange(S_DEV, dtype=jnp.int32) < live_count
    matches = (target_row[:, None] == jnp.arange(row_tiles, dtype=jnp.int32)[None, :]) & living[
        :, None
    ]
    ordinal = jnp.cumsum(matches.astype(jnp.int32), axis=0) - 1
    ranking = jnp.sum(jnp.where(matches, ordinal, 0), axis=1)
    target = target_row * spread + ranking
    chooser = (
        (jnp.arange(row_tiles * spread, dtype=jnp.int32)[:, None] == target[None, :])
        & living[None, :]
    ).astype(jnp.bfloat16)
    merged = jnp.concatenate([blocks, weights[:, None, :]], axis=1).reshape(
        S_DEV, (own_bands + 1) * BS * BS
    )
    packed = jnp.dot(chooser, merged, preferred_element_type=jnp.float32).astype(jnp.bfloat16)
    packed = packed.reshape(row_tiles, spread, own_bands + 1, BS * BS)
    slot_ids = jnp.arange(SLOTS, dtype=jnp.int32)
    tag_send = jnp.dot(
        chooser, (placed + 1).astype(jnp.bfloat16)[:, None], preferred_element_type=jnp.float32
    )
    tag_send = tag_send.astype(jnp.bfloat16).reshape(row_tiles, spread)
    arrived, tag_back = (
        lax.all_to_all(packed, "tx", split_axis=0, concat_axis=0, tiled=True),
        lax.all_to_all(tag_send, "tx", split_axis=0, concat_axis=0, tiled=True),
    )
    landing = (slot_ids + 1).astype(jnp.float32)[:, None] == tag_back.reshape(-1).astype(
        jnp.float32
    )[None, :]
    arrived = arrived.reshape(row_tiles * spread, own_bands + 1, BS * BS)
    coverage = arrived[:, own_bands:].astype(jnp.float32)
    payload = jnp.concatenate(
        [arrived[:, :own_bands].astype(jnp.float32) * coverage, coverage], axis=1
    )
    payload = payload.reshape(row_tiles * spread, (own_bands + 1) * BS * BS)
    slot_sums = jnp.dot(landing.astype(jnp.float32), payload, precision=lax.Precision.HIGHEST)
    per_row = TS // BS
    tile_field = slot_sums.reshape(per_row, per_row, own_bands + 1, BS, BS).transpose(2, 0, 3, 1, 4)
    tile_field = tile_field.reshape(own_bands + 1, TS, TS)

    def masked(field, extent, rim):
        row_mask = border(extent, rim, row_tile * extent, extent * row_tiles)
        col_mask = border(extent, rim, col_tile * extent, extent * col_tiles)
        return field * row_mask[:, None] * col_mask[None, :]

    def enlarge(field, rim_in, rim_out):
        return grow(field, rim_in, rim_out)

    ground = with_halo(tile_field, (("tx", 1), ("ty", 2)), MARGIN)
    margin = MARGIN
    needed = [0]
    for _ in range(1, LEVELS):
        needed.append((needed[-1] + 3) // 2)
    pyramid = [(ground, margin)]
    extent = TS
    for _ in range(1, LEVELS):
        source, rim_in = pyramid[-1]
        rim_out = (rim_in - 2) // 2
        extent = extent // 2
        reduced = masked(shrink(source, rim_in, rim_out), extent, rim_out)
        pyramid.append((reduced, rim_out))
    deepest = LEVELS - 1
    summit, rim_top = pyramid[-1]
    summit = trim(summit, rim_top, needed[deepest])
    collapsed = summit[:own_bands] / (BACKGROUND + summit[own_bands])
    for tier_index in range(LEVELS - 2, -1, -1):
        current, rim_here = pyramid[tier_index]
        coarser, rim_below = pyramid[tier_index + 1]
        current = trim(current, rim_here, needed[tier_index])
        detail = current[:own_bands] - enlarge(coarser[:own_bands], rim_below, needed[tier_index])
        band_part = detail / (BACKGROUND + current[own_bands])
        collapsed = band_part + enlarge(collapsed, needed[tier_index + 1], needed[tier_index])
        collapsed = masked(collapsed, TS >> tier_index, needed[tier_index])
    blended = collapsed.astype(jnp.bfloat16)
    flipped = jnp.swapaxes(blended, 1, 2)
    strips = lax.all_to_all(flipped, "tx", split_axis=1, concat_axis=2, tiled=True)
    return strips[:, None]


BF = jnp.bfloat16
F32 = jnp.float32
EDGE = 3
CODE_ROWS = 8
DEAD = -1024


def up8(v):
    return -(-v // 8) * 8


def shrink_grid(length):
    table = np.zeros((length // 2, length))
    for i in range(length // 2):
        for tap, weight in enumerate(BINOMIAL):
            k = 2 * i + tap - 2
            if 0 <= k < length:
                table[i, k] += weight
    return table


def grow_grid(length):
    table = np.zeros((2 * length, length))
    for i in range(length):
        for k, weight in ((i - 1, 0.125), (i, 0.75), (i + 1, 0.125)):
            if 0 <= k < length:
                table[2 * i, k] += weight
        for k in (i, i + 1):
            if k < length:
                table[2 * i + 1, k] += 0.5
    return table


def split_table(table):
    high = table.astype(BF)
    return high, (table - high.astype(np.float64)).astype(BF)


def row_shrinks(rows):
    tables, current = [], np.eye(rows)
    for level in range(1, LEVELS):
        current = shrink_grid(rows >> (level - 1)) @ current
        tables.append(current)
    return tables


class Plan:
    def __init__(self, n, m, bands):
        self.n, self.m, self.bands = n, m, bands
        self.rows = n * TS
        self.strip = TS // n
        self.slots = n * SLOTS
        self.slot_rows = n * (TS // BS)
        w = self.strip
        self.held = [w, w // 2 + 2, w // 4 + 3, w // 8 + 3]
        self.size = [w] + [up8(h) for h in self.held[1:]]
        self.first = [0, -1, -1, -1]
        self.at = [0]
        for size in self.size:
            self.at.append(self.at[-1] + size)
        self.low_at = self.at[LEVELS]
        self.main = self.low_at + self.size[3]
        self.edge_rows = 8 * LEVELS
        self.total = self.main + 2 * self.edge_rows
        self.near = 2 * BS
        self.half = BS * BS // 2
        self.weight_at = bands * self.half
        self.code_at = self.weight_at + self.half
        order = np.arange(self.rows)
        wide = self.slot_rows
        u, half, v = order // (4 * wide), order // (2 * wide) % 2, order // wide % 2
        self.row_of = order % wide * BS + half * (BS // 2) + 2 * u + v

    def column_tables(self):
        n, m, w = self.n, self.m, self.strip
        width = m * TS
        grids = [np.eye(width)] + row_shrinks(width)
        tables = np.zeros((n, m, self.total, TS))
        for t in range(n):
            for j in range(m):
                for level in range(LEVELS):
                    base = ((j * TS + t * w) >> level) + self.first[level]
                    for k in range(self.held[level]):
                        o = base + k
                        if 0 <= o < width >> level:
                            tables[t, j, self.at[level] + k] = grids[level][o, j * TS : (j + 1) * TS]
                    for which, target in enumerate((t, t ^ n // 2)):
                        right = 2 * target < n
                        base = ((j + 1 if right else j) * TS >> level) - 1
                        at = self.main + which * self.edge_rows + 8 * (level - 1)
                        for k in range(EDGE if level else 0):
                            if 0 <= base + k < width >> level:
                                row = grids[level][base + k, j * TS : (j + 1) * TS]
                                row = row[TS - self.near :] if right else row[: self.near]
                                tables[t, j, at + k, : 2 * self.near] = np.concatenate([row, row])
        high, low = split_table(tables)
        high[:, :, self.low_at : self.main] = low[:, :, self.at[3] : self.at[4]]
        for at in (self.main + self.edge_rows, self.total):
            high[:, :, at - 8 : at] = low[:, :, at - 16 : at - 8]
        return np.concatenate([high, high], axis=-1).reshape(n * m, self.total, 2 * TS)


def halves(value):
    high = value.astype(BF)
    return high, (value - high.astype(F32)).astype(BF)


def dot2(value, table):
    high, low = halves(value)
    return jnp.dot(high, table, preferred_element_type=F32) + jnp.dot(
        low, table, preferred_element_type=F32
    )


def turned(plan, block):
    return jnp.concatenate([block[:, : plan.half], block[:, plan.half :]], axis=0).T


def pack_kernel(plan, count_ref, scenes_ref, cloud_ref, dest_ref, offset_ref, out_ref, note_ref, raw,
                dest, offset, sems):
    rows = 2 * S_DEV
    half = plan.half
    copies = [
        pltpu.make_async_copy(source, target, sems.at[k])
        for k, (source, target) in enumerate(
            (
                (dest_ref, dest),
                (offset_ref, offset),
                (cloud_ref, raw.at[plan.bands]),
                (scenes_ref, raw.at[pl.ds(0, plan.bands)]),
            )
        )
    ]
    for copy in copies:
        copy.start()
    for copy in copies[:2]:
        copy.wait()
    per_row = TS // BS
    slot = offset[...]
    code = (slot % per_row) * plan.slot_rows + dest[...] * per_row + slot // per_row
    live = lax.broadcasted_iota(jnp.int32, (1, S_DEV), 1) < count_ref[0, 0]
    code = jnp.where(live, code, DEAD).astype(F32)
    code = jnp.broadcast_to(jnp.concatenate([code, code], axis=1), (CODE_ROWS, rows))
    out_ref[plan.code_at :, :] = code.astype(BF)
    for f in (plan.bands, *range(plan.bands)):
        if f == plan.bands:
            copies[2].wait()
        elif f == 0:
            copies[3].wait()
        out_ref[f * half : (f + 1) * half, :] = turned(plan, raw[f])
    note_ref[...] = out_ref[plan.weight_at :, :]


def load_kernel(plan, column_ref, *refs):
    count = (len(refs) - 2) // 2
    sources, targets, sems = refs[:count], refs[count:-1], refs[-1]
    mine = lax.axis_index("tx") * plan.m + lax.axis_index("ty")
    copies = [
        pltpu.make_async_copy(source, target, sems.at[k])
        for k, (source, target) in enumerate(zip((column_ref.at[mine], *sources), targets))
    ]
    for copy in copies:
        copy.start()
    for copy in copies:
        copy.wait()


def landing_of(plan, codes):
    codes = codes.astype(F32).T[:, :1]
    blocks = codes.shape[0]
    pair = float(2 * plan.slot_rows)
    second = lax.broadcasted_iota(jnp.int32, (blocks, 1), 0) >= S_DEV
    codes = codes + pair * jnp.floor(codes / pair) + jnp.where(second, pair, 0.0)
    slot = lax.broadcasted_iota(jnp.int32, (blocks, 2 * plan.slots), 1).astype(F32)
    landing = jnp.where(slot == codes, 1.0, 0.0).astype(BF)
    return jnp.concatenate([landing, landing], axis=0)


def slot_sums(plan, scenes, note, prod_ref):
    half, blocks = plan.half, 2 * S_DEV
    weight = note[:half, :]
    for f in range(plan.bands):
        rows = pl.ds(f * half, half)
        if len(scenes.shape) == 3:
            value = turned(plan, scenes[f])
        else:
            value = scenes[f * half : (f + 1) * half, :]
        high, low = halves(value.astype(F32) * weight.astype(F32))
        prod_ref[rows, :blocks] = high
        prod_ref[rows, blocks:] = low
    rows = pl.ds(plan.weight_at, half)
    prod_ref[rows, :blocks] = weight
    prod_ref[rows, blocks:] = jnp.zeros_like(weight)
    return jnp.dot(prod_ref[...], landing_of(plan, note[half:, :]), preferred_element_type=F32)


def turn(plan, a, b):
    wide = plan.slot_rows
    odd = lax.broadcasted_iota(jnp.int32, a.shape, 1) // wide % 2 == 1
    return jnp.where(odd, pltpu.roll(b, wide, 1), a), jnp.where(odd, b, pltpu.roll(a, TS - wide, 1))


def twin_sum(value):
    return value + pltpu.roll(value, value.shape[-1] // 2, value.ndim - 1)


def edge_of(plan, side_ref, table, row1_ref, row23_ref, out_ref, tile_ref, z1_ref, z23_ref):
    planes = plan.bands + 1
    rows = plan.rows
    for f in range(planes):
        tile = tile_ref.at[f % 2]
        for u in range(BS // 4):
            at = f * plan.half + 2 * u * BS
            pair = turn(plan, side_ref[at : at + BS], side_ref[at + BS : at + 2 * BS])
            for k, value in enumerate(pair):
                high, low = halves(value)
                tile[k * BS : (k + 1) * BS, u * TS : (u + 1) * TS] = high
                tile[plan.near + k * BS : plan.near + (k + 1) * BS, u * TS : (u + 1) * TS] = low
        cols = jnp.dot(table, tile[...], preferred_element_type=F32)
        z1_ref[f] = cols[:8]
        z23_ref[f, :8] = cols[8:16]
        z23_ref[f, 8:] = cols[16:24] + cols[24:]
    kind = out_ref.dtype
    out_ref[...] = jnp.zeros(out_ref.shape, kind)
    z1 = dot2(z1_ref[...].reshape(planes * 8, rows), row1_ref[...])
    z1 = z1.reshape(planes, 8, rows // 2)
    z23 = dot2(z23_ref[...].reshape(planes * 16, rows), row23_ref[...])
    z23 = z23.reshape(planes, 16, rows // 2)
    second = rows // 2 + rows // 4
    for f in range(planes):
        at = pl.ds(EDGE * f, EDGE)
        out_ref[at, : rows // 2] = z1[f, :EDGE].astype(kind)
        out_ref[at, rows // 2 : second] = z23[f, :EDGE, : rows // 4].astype(kind)
        out_ref[at, second:] = twin_sum(z23[f, 8:, rows // 4 :])[:EDGE].astype(kind)


def side_of(plan, sums, right):
    return jnp.where(right, sums[:, 2 * plan.slots - TS :], sums[:, :TS])


def own_kernel(plan, pack, column_ref, row1_ref, row23_ref,
               out_ref, edge_ref, prod_ref, side_ref, tile_ref, z1_ref, z23_ref):
    right = 2 * (lax.axis_index("tx") ^ plan.n // 2) < plan.n
    sums = slot_sums(plan, pack, pack.at[pl.ds(plan.weight_at, plan.half + CODE_ROWS)], prod_ref)
    out_ref[...] = sums
    side_ref[...] = side_of(plan, sums, right)
    table = column_ref[plan.main + plan.edge_rows :, : 2 * plan.near]
    edge_of(plan, side_ref, table, row1_ref, row23_ref, edge_ref, tile_ref, z1_ref, z23_ref)


def first_kernel(plan, far, note, near, before_ref, column_ref, row1_ref, row23_ref,
                 out_ref, edge_ref, prod_ref, side_ref, tile_ref, z1_ref, z23_ref):
    right = 2 * lax.axis_index("tx") < plan.n
    near_note = near.at[pl.ds(plan.weight_at, plan.half + CODE_ROWS)]
    sums = slot_sums(plan, near, near_note, prod_ref.at[0])
    sums = before_ref[...] + sums + slot_sums(plan, far, note, prod_ref.at[1])
    out_ref[...] = sums
    side_ref[...] = side_of(plan, sums, right)
    table = column_ref[plan.main : plan.main + plan.edge_rows, : 2 * plan.near]
    edge_of(plan, side_ref, table, row1_ref, row23_ref, edge_ref, tile_ref, z1_ref, z23_ref)


def tile_of(plan, sums, at, tile_ref):
    for pair in range(2 * plan.slots // TS):
        lanes = slice(pair * TS, (pair + 1) * TS)
        for u in range(BS // 4):
            row = at + 2 * u * BS
            both = turn(plan, sums[row : row + BS, lanes], sums[row + BS : row + 2 * BS, lanes])
            for k, value in enumerate(both):
                high, low = halves(value)
                row = (2 * pair + k) * BS
                tile_ref[row : row + BS, u * TS : (u + 1) * TS] = high
                tile_ref[TS + row : TS + row + BS, u * TS : (u + 1) * TS] = low


def place_kernel(plan, late, note, before_ref, column_ref, row1_ref, row23_ref,
                 a0_ref, a1_ref, a2_ref, a3_ref, prod_ref, sums_ref, tile_ref, z1_ref, z23_ref):
    column = column_ref[: plan.main, :]
    at, size = plan.at, plan.size
    planes = plan.bands + 1
    rows = plan.rows
    sums_ref[...] = before_ref[...] + slot_sums(plan, late, note, prod_ref)
    for f in range(planes):
        tile = tile_ref.at[f % 2]
        tile_of(plan, sums_ref, f * plan.half, tile)
        cols = jnp.dot(column, tile[...], preferred_element_type=F32)
        a0_ref[f] = cols[at[0] : at[1]]
        z1_ref[f] = cols[at[1] : at[2]]
        z23_ref[f, : size[2]] = cols[at[2] : at[3]]
        z23_ref[f, size[2] :] = cols[at[3] : at[4]] + cols[plan.low_at : plan.main]
    z1 = dot2(z1_ref[...].reshape(planes * size[1], rows), row1_ref[...])
    a1_ref[...] = z1.reshape(a1_ref.shape)
    z23 = dot2(z23_ref[...].reshape(planes * (size[2] + size[3]), rows), row23_ref[...])
    z23 = z23.reshape(planes, size[2] + size[3], rows // 2)
    a2_ref[...] = z23[:, : size[2], : rows // 4]
    for f in range(planes):
        a3_ref[f] = twin_sum(z23[f, size[2] :, rows // 4 :])


def grow_columns(value, outputs):
    half = outputs // 2
    a, b, c = value[:, :half], value[:, 1 : half + 1], value[:, 2 : half + 2]
    return (a + b) * 0.5, (a + 6.0 * b + c) * 0.125


def weave(even, odd, ref, size):
    k, half, lanes = even.shape
    if 2 * half < size:
        ref[...] = jnp.zeros(ref.shape, F32)
    for q in range(k):
        for chunk in range(lanes // TS):
            part = slice(chunk * TS, (chunk + 1) * TS)
            ref[q, chunk, pl.ds(0, half, stride=2), :] = even[q][:, part]
            ref[q, chunk, pl.ds(1, half, stride=2), :] = odd[q][:, part]
    return jnp.concatenate([ref[:, chunk] for chunk in range(lanes // TS)], axis=-1)


def blend_kernel(plan, a0_ref, a1_ref, a2_ref, a3_ref, near_ref, far_ref, grow1_ref, grow2_ref, grow3_ref,
                 natural_ref, out_ref, g1_ref, g2_ref, g3_ref, e2_ref, e1_ref, e0_ref, strip_ref, sems):
    bands = plan.bands
    planes = bands + 1
    w = plan.strip
    row_tile, col_tile = lax.axis_index("tx"), lax.axis_index("ty")
    first, last = row_tile == 0, row_tile == plan.n - 1
    left, right = first & (col_tile > 0), last & (col_tile < plan.m - 1)
    first, last = first & (col_tile == 0), last & (col_tile == plan.m - 1)
    edges = near_ref[...] + far_ref[...].astype(F32)
    start = 0
    for level, (src, dst) in enumerate(((a1_ref, g1_ref), (a2_ref, g2_ref), (a3_ref, g3_ref)), 1):
        lanes = src.shape[-1]
        dst[...] = src[...]
        for f in range(planes):
            edge = edges[EDGE * f : EDGE * (f + 1), start : start + lanes]
            far = w >> level
            dst[f, :EDGE] += jnp.where(left, edge, 0.0)
            dst[f, far : far + EDGE] += jnp.where(right, edge, 0.0)
        start += lanes

    def inside(level, columns):
        column = lax.broadcasted_iota(jnp.int32, (columns, 1), 0) - 1
        keep = ((column >= 0) | ~first) & ((column < (w >> level)) | ~last)
        return keep.astype(F32)

    def grown(level, value, up_ref):
        k, c, r = value.shape
        if level == 0:
            half = w // 2
            x, y, z = value[:, :half], value[:, 1 : half + 1], value[:, 2 : half + 2]
            tall = weave((x + 6.0 * y + z) * 0.125, (y + z) * 0.5, up_ref, w)
            return dot2(tall.reshape(k * w, r), grow1_ref[...]).reshape(k, w, plan.rows)
        grow_ref = (grow2_ref, grow3_ref)[level - 1]
        wide = dot2(value.reshape(k * c, r), grow_ref[...])
        wide = wide.reshape(k, c, wide.shape[-1])
        pairs = min(up8(plan.held[level]) // 2, c - 2)
        return weave(*grow_columns(wide, 2 * pairs), up_ref, plan.size[level])

    e2a_ref, e1a_ref, e0a_ref = (ref.at[pl.ds(0, bands)] for ref in (e2_ref, e1_ref, e0_ref))
    e2b_ref, e1b_ref, e0b_ref = (ref.at[pl.ds(bands, bands)] for ref in (e2_ref, e1_ref, e0_ref))
    inverses = [1.0 / (BACKGROUND + ref[bands]) for ref in (a0_ref, g1_ref, g2_ref, g3_ref)]
    blend = g3_ref[:bands] * inverses[3]
    detail2 = (g2_ref[:bands] - grown(2, g3_ref[:bands], e2a_ref)) * inverses[2]
    blend = (detail2 + grown(2, blend, e2b_ref)) * inside(2, plan.size[2])
    detail1 = (g1_ref[:bands] - grown(1, g2_ref[:bands], e1a_ref)) * inverses[1]
    blend = (detail1 + grown(1, blend, e1b_ref)) * inside(1, plan.size[1])
    detail0 = (a0_ref[:bands] - grown(0, g1_ref[:bands], e0a_ref)) * inverses[0]
    up = grown(0, blend, e0b_ref)
    copies = []
    part = bands // 2
    for f in range(0, bands, part):
        value = detail0[f : f + part] + up[f : f + part]
        value = value.astype(BF).reshape(part * w, plan.rows)
        value = jnp.dot(value, natural_ref[...], preferred_element_type=F32)
        strip_ref[pl.ds(f, part)] = value.astype(BF).reshape(part, w, plan.rows)
        copies.append(
            pltpu.make_async_copy(
                strip_ref.at[pl.ds(f, part)], out_ref.at[pl.ds(f, part)], sems.at[len(copies)]
            )
        )
        copies[-1].start()
    for copy in copies:
        copy.wait()


def on_chip(value):
    return pltpu.with_memory_space_constraint(value, pltpu.VMEM)


def off_chip(value):
    return pltpu.with_memory_space_constraint(value, pltpu.HBM)


def strip_local(scenes, cloud, destination, offset, counts):
    n, m = lax.axis_size("tx"), lax.axis_size("ty")
    bands = scenes.shape[2]
    plan = Plan(n, m, bands)
    planes = bands + 1
    area = BS * BS
    vmem = pl.BlockSpec(memory_space=pltpu.VMEM)
    smem = pl.BlockSpec(memory_space=pltpu.SMEM)
    hbm = pl.BlockSpec(memory_space=pl.ANY)
    blocks = jnp.swapaxes(scenes[0], 0, 1)

    def call(kernel, operands, outputs, scratch=(), flops=0, out_specs=None):
        return pl.pallas_call(
            functools.partial(kernel, plan),
            out_shape=outputs,
            in_specs=[vmem] * len(operands),
            out_specs=out_specs or jax.tree.map(lambda _: vmem, outputs),
            scratch_shapes=list(scratch),
            compiler_params=pltpu.CompilerParams(vmem_limit_bytes=16 << 20),
            cost_estimate=pl.CostEstimate(flops=flops, bytes_accessed=1 << 20, transcendentals=0),
        )(*[on_chip(v) for v in operands])

    shrinks = row_shrinks(plan.rows)
    row1 = shrinks[0].T[plan.row_of]
    row2 = shrinks[1].T[plan.row_of]
    top = plan.rows >> 3
    wide_top = 2 * top
    row23 = np.concatenate([row2, *split_table(shrinks[2].T[plan.row_of])], axis=1)
    grow3 = np.zeros((wide_top, plan.rows >> 2))
    grow3[:top] = grow_grid(top).T
    grow2 = grow_grid(plan.rows >> 2).T
    grow1 = grow_grid(plan.rows >> 1).T[:, plan.row_of]
    natural = np.eye(plan.rows)[plan.row_of]
    constants = [plan.column_tables(), row1, row23, grow1, grow2, grow3, natural]
    constants = [off_chip(jnp.asarray(table.astype(BF))) for table in constants]
    loaded = pl.pallas_call(
        functools.partial(load_kernel, plan),
        out_shape=[pltpu.VMEM(c.shape[k == 0 :], BF) for k, c in enumerate(constants)],
        in_specs=[hbm] * len(constants),
        out_specs=[vmem] * len(constants),
        scratch_shapes=[pltpu.SemaphoreType.DMA((len(constants),))],
        compiler_params=pltpu.CompilerParams(vmem_limit_bytes=4 << 20),
        name="load",
    )(*constants)
    tables, grows = list(loaded[:3]), list(loaded[3:])
    size = plan.size
    shapes = [
        (planes, size[0], plan.rows),
        (planes, size[1], plan.rows >> 1),
        (planes, size[2], plan.rows >> 2),
        (planes, size[3], wide_top),
    ]
    edge_shape = (up8(EDGE * planes), sum(s[-1] for s in shapes[1:]))
    sums_shape = pltpu.VMEM((planes * plan.half, 2 * plan.slots), F32)
    prod_shape = (planes * plan.half, 4 * S_DEV)
    work = 2 * planes * area * plan.slots * 2 * S_DEV

    across = [(i, n - 1 - i) for i in range(n)]
    beside = [(i, i ^ 1) for i in range(n)]
    far = lax.ppermute(blocks, "tx", across)
    pack, note = pl.pallas_call(
        functools.partial(pack_kernel, plan),
        out_shape=[
            pltpu.VMEM((plan.code_at + CODE_ROWS, 2 * S_DEV), BF),
            pltpu.VMEM((plan.half + CODE_ROWS, 2 * S_DEV), BF),
        ],
        in_specs=[smem] + [hbm] * 4,
        out_specs=[vmem] * 2,
        scratch_shapes=[
            pltpu.VMEM((planes, S_DEV, area), BF),
            pltpu.VMEM(destination.shape, jnp.int32),
            pltpu.VMEM(offset.shape, jnp.int32),
            pltpu.SemaphoreType.DMA((4,)),
        ],
        compiler_params=pltpu.CompilerParams(vmem_limit_bytes=4 << 20),
        name="pack",
    )(counts, *[off_chip(v) for v in (blocks, cloud[0], destination, offset)])

    far_note = lax.ppermute(note, "tx", across)
    near = lax.ppermute(pack, "tx", beside)
    edge_work = [
        pltpu.VMEM((planes * plan.half, TS), F32),
        pltpu.VMEM((2, 2 * plan.near, plan.rows), BF),
        pltpu.VMEM((planes, 8, plan.rows), F32),
        pltpu.VMEM((planes, 16, plan.rows), F32),
    ]
    sums, edge_far = call(
        own_kernel,
        [pack] + tables,
        [sums_shape, pltpu.VMEM(edge_shape, BF)],
        [pltpu.VMEM(prod_shape, BF)] + edge_work,
        flops=work,
    )

    def over(value, shift):
        pairs = []
        for t in range(n):
            for j in range(m):
                target = t ^ shift
                pairs.append((t * m + j, target * m + (j + 1 if 2 * target < n else j - 1) % m))
        return lax.ppermute(value, ("tx", "ty"), pairs)

    edge_far = over(edge_far, n // 2)
    late = lax.ppermute(far, "tx", beside)
    late_note = lax.ppermute(far_note, "tx", beside)
    sums, edge_near = call(
        first_kernel,
        [far, far_note, near, sums] + tables,
        [sums_shape, pltpu.VMEM(edge_shape, F32)],
        [pltpu.VMEM((2, *prod_shape), BF)] + edge_work,
        flops=4 * work,
    )
    edge_near = over(edge_near, 0)
    levels = call(
        place_kernel,
        [late, late_note, sums] + tables,
        [pltpu.VMEM(s, F32) for s in shapes],
        [
            pltpu.VMEM(prod_shape, BF),
            pltpu.VMEM(sums_shape.shape, F32),
            pltpu.VMEM((2, 2 * TS, plan.rows), BF),
            pltpu.VMEM((planes, size[1], plan.rows), F32),
            pltpu.VMEM((planes, size[2] + size[3], plan.rows), F32),
        ],
        flops=4 * work,
    )
    out = call(
        blend_kernel,
        [*levels, edge_near, edge_far, *grows],
        jax.ShapeDtypeStruct((bands, size[0], plan.rows), BF),
        [
            pltpu.VMEM(shapes[1], F32),
            pltpu.VMEM(shapes[2], F32),
            pltpu.VMEM(shapes[3], F32),
            pltpu.VMEM((2 * bands, (plan.rows >> 2) // TS, size[2], TS), F32),
            pltpu.VMEM((2 * bands, (plan.rows >> 1) // TS, size[1], TS), F32),
            pltpu.VMEM((2 * bands, (plan.rows >> 1) // TS, size[0], TS), F32),
            pltpu.VMEM((bands, size[0], plan.rows), BF),
            pltpu.SemaphoreType.DMA((2,)),
        ],
        flops=4 * work,
        out_specs=hbm,
    )
    return out[:, None]


def strip_step(*arguments):
    return strip_local(*arguments)


def use_strips(n, m):
    spread = max(2, 2 * S_DEV // n)
    return n == 4 and TS // n >= 32 and m >= 2 and S_DEV <= 2 * spread


def solution(mesh):
    placed = (
        P(("region", "ty"), "tx", "band", None),
        P(("region", "ty"), "tx", None),
        P(("region", "ty"), "tx"),
        P(("region", "ty"), "tx"),
        P(("region", "ty"), "tx"),
    )
    strips = use_strips(mesh.shape["tx"], mesh.shape["ty"])
    return jax.shard_map(
        strip_step if strips else local,
        mesh=mesh,
        in_specs=placed,
        out_specs=P("band", ("region", "ty"), "tx", None),
        check_vma=False,
    )
```

```python
import functools

import jax
import jax.numpy as jnp
import numpy as np
from jax import lax
from jax.experimental import pallas as pl
from jax.experimental.pallas import tpu as pltpu
from jax.sharding import PartitionSpec as P


TS = 128
BS = 16
S_DEV = 64
MARGIN = 32
LEVELS = 4
SLOTS = 64


BINOMIAL = (0.0625, 0.25, 0.375, 0.25, 0.0625)
BACKGROUND = 0.25


def with_halo(shard, sides, width):
    for axis, dim in sides:
        devices, length = (lax.axis_size(axis), shard.shape[dim])
        up = [(i, (i + 1) % devices) for i in range(devices - 1)]
        down = [(j, i) for i, j in up]
        last = lax.slice_in_dim(shard, length - width, length, axis=dim)
        leading = lax.slice_in_dim(shard, 0, width, axis=dim)
        before = lax.ppermute(last, axis, up)
        after = lax.ppermute(leading, axis, down)
        shard = jnp.concatenate([before, shard, after], axis=dim)
    return shard


def shrink_table(length, rim_in, rim_out):
    extent = length - 2 * rim_in
    outputs = extent // 2 + 2 * rim_out
    first_index = rim_in - 2 - 2 * rim_out
    out_pos = jnp.arange(outputs, dtype=jnp.int32)[:, None]
    in_pos = jnp.arange(length, dtype=jnp.int32)[None, :]
    spacing = in_pos - first_index - 2 * out_pos
    table = jnp.zeros((outputs, length), jnp.float32)
    for tap_index, tap_weight in enumerate(BINOMIAL):
        table = table + tap_weight * (spacing == tap_index).astype(jnp.float32)
    return table


def grow_table(length, rim_in, rim_out):
    excess = 2 * rim_in - 2 - rim_out
    outputs = 2 * (length - 2) - 2 * excess
    paired = jnp.arange(outputs, dtype=jnp.int32)[:, None] + excess
    source = paired // 2
    parity = paired % 2
    spacing = jnp.arange(length, dtype=jnp.int32)[None, :] - source
    even_part = (
        0.125 * (spacing == 0).astype(jnp.float32)
        + 0.75 * (spacing == 1).astype(jnp.float32)
        + 0.125 * (spacing == 2).astype(jnp.float32)
    )
    odd_part = 0.5 * (spacing == 1).astype(jnp.float32) + 0.5 * (spacing == 2).astype(jnp.float32)
    return jnp.where(parity == 0, even_part, odd_part)


def apply_both(field, row_table, col_table):
    rows_done = jnp.einsum("ki,bic->bkc", row_table, field, precision=lax.Precision.HIGHEST)
    return jnp.einsum("bkc,mc->bkm", rows_done, col_table, precision=lax.Precision.HIGHEST)


def shrink(field, rim_in, rim_out):
    row_table = shrink_table(field.shape[-2], rim_in, rim_out)
    col_table = shrink_table(field.shape[-1], rim_in, rim_out)
    return apply_both(field, row_table, col_table)


def grow(field, rim_in, rim_out):
    row_table = grow_table(field.shape[-2], rim_in, rim_out)
    col_table = grow_table(field.shape[-1], rim_in, rim_out)
    return apply_both(field, row_table, col_table)


def trim(field, rim_have, rim_want):
    excess = rim_have - rim_want
    return field[..., excess : field.shape[-2] - excess, excess : field.shape[-1] - excess]


def border(extent, rim, begin, whole):
    position = begin - rim + jnp.arange(extent + 2 * rim, dtype=jnp.int32)
    return ((position >= 0) & (position < whole)).astype(jnp.float32)


def local(scenes, cloud, destination, offset, counts):
    row_tiles = lax.axis_size("tx")
    col_tiles = lax.axis_size("ty")
    row_tile = lax.axis_index("tx")
    col_tile = lax.axis_index("ty")
    spread = max(2, 2 * S_DEV // row_tiles)
    blocks = scenes[0]
    weights = cloud[0]
    target_row = destination[0]
    placed = offset[0]
    live_count = counts[0, 0]
    own_bands = blocks.shape[1]
    living = jnp.arange(S_DEV, dtype=jnp.int32) < live_count
    matches = (target_row[:, None] == jnp.arange(row_tiles, dtype=jnp.int32)[None, :]) & living[
        :, None
    ]
    ordinal = jnp.cumsum(matches.astype(jnp.int32), axis=0) - 1
    ranking = jnp.sum(jnp.where(matches, ordinal, 0), axis=1)
    target = target_row * spread + ranking
    chooser = (
        (jnp.arange(row_tiles * spread, dtype=jnp.int32)[:, None] == target[None, :])
        & living[None, :]
    ).astype(jnp.bfloat16)
    merged = jnp.concatenate([blocks, weights[:, None, :]], axis=1).reshape(
        S_DEV, (own_bands + 1) * BS * BS
    )
    packed = jnp.dot(chooser, merged, preferred_element_type=jnp.float32).astype(jnp.bfloat16)
    packed = packed.reshape(row_tiles, spread, own_bands + 1, BS * BS)
    slot_ids = jnp.arange(SLOTS, dtype=jnp.int32)
    tag_send = jnp.dot(
        chooser, (placed + 1).astype(jnp.bfloat16)[:, None], preferred_element_type=jnp.float32
    )
    tag_send = tag_send.astype(jnp.bfloat16).reshape(row_tiles, spread)
    arrived, tag_back = (
        lax.all_to_all(packed, "tx", split_axis=0, concat_axis=0, tiled=True),
        lax.all_to_all(tag_send, "tx", split_axis=0, concat_axis=0, tiled=True),
    )
    landing = (slot_ids + 1).astype(jnp.float32)[:, None] == tag_back.reshape(-1).astype(
        jnp.float32
    )[None, :]
    arrived = arrived.reshape(row_tiles * spread, own_bands + 1, BS * BS)
    coverage = arrived[:, own_bands:].astype(jnp.float32)
    payload = jnp.concatenate(
        [arrived[:, :own_bands].astype(jnp.float32) * coverage, coverage], axis=1
    )
    payload = payload.reshape(row_tiles * spread, (own_bands + 1) * BS * BS)
    slot_sums = jnp.dot(landing.astype(jnp.float32), payload, precision=lax.Precision.HIGHEST)
    per_row = TS // BS
    tile_field = slot_sums.reshape(per_row, per_row, own_bands + 1, BS, BS).transpose(2, 0, 3, 1, 4)
    tile_field = tile_field.reshape(own_bands + 1, TS, TS)

    def masked(field, extent, rim):
        row_mask = border(extent, rim, row_tile * extent, extent * row_tiles)
        col_mask = border(extent, rim, col_tile * extent, extent * col_tiles)
        return field * row_mask[:, None] * col_mask[None, :]

    def enlarge(field, rim_in, rim_out):
        return grow(field, rim_in, rim_out)

    ground = with_halo(tile_field, (("tx", 1), ("ty", 2)), MARGIN)
    margin = MARGIN
    needed = [0]
    for _ in range(1, LEVELS):
        needed.append((needed[-1] + 3) // 2)
    pyramid = [(ground, margin)]
    extent = TS
    for _ in range(1, LEVELS):
        source, rim_in = pyramid[-1]
        rim_out = (rim_in - 2) // 2
        extent = extent // 2
        reduced = masked(shrink(source, rim_in, rim_out), extent, rim_out)
        pyramid.append((reduced, rim_out))
    deepest = LEVELS - 1
    summit, rim_top = pyramid[-1]
    summit = trim(summit, rim_top, needed[deepest])
    collapsed = summit[:own_bands] / (BACKGROUND + summit[own_bands])
    for tier_index in range(LEVELS - 2, -1, -1):
        current, rim_here = pyramid[tier_index]
        coarser, rim_below = pyramid[tier_index + 1]
        current = trim(current, rim_here, needed[tier_index])
        detail = current[:own_bands] - enlarge(coarser[:own_bands], rim_below, needed[tier_index])
        band_part = detail / (BACKGROUND + current[own_bands])
        collapsed = band_part + enlarge(collapsed, needed[tier_index + 1], needed[tier_index])
        collapsed = masked(collapsed, TS >> tier_index, needed[tier_index])
    blended = collapsed.astype(jnp.bfloat16)
    flipped = jnp.swapaxes(blended, 1, 2)
    strips = lax.all_to_all(flipped, "tx", split_axis=1, concat_axis=2, tiled=True)
    return strips[:, None]


BF = jnp.bfloat16
F32 = jnp.float32
EDGE = 3
CODE_ROWS = 8
DEAD = -1024


def up8(v):
    return -(-v // 8) * 8


def shrink_grid(length):
    table = np.zeros((length // 2, length))
    for i in range(length // 2):
        for tap, weight in enumerate(BINOMIAL):
            k = 2 * i + tap - 2
            if 0 <= k < length:
                table[i, k] += weight
    return table


def grow_grid(length):
    table = np.zeros((2 * length, length))
    for i in range(length):
        for k, weight in ((i - 1, 0.125), (i, 0.75), (i + 1, 0.125)):
            if 0 <= k < length:
                table[2 * i, k] += weight
        for k in (i, i + 1):
            if k < length:
                table[2 * i + 1, k] += 0.5
    return table


def split_table(table):
    high = table.astype(BF)
    return high, (table - high.astype(np.float64)).astype(BF)


def row_shrinks(rows):
    tables, current = [], np.eye(rows)
    for level in range(1, LEVELS):
        current = shrink_grid(rows >> (level - 1)) @ current
        tables.append(current)
    return tables


class Plan:
    def __init__(self, n, m, bands):
        self.n, self.m, self.bands = n, m, bands
        self.rows = n * TS
        self.strip = TS // n
        self.slots = n * SLOTS
        self.slot_rows = n * (TS // BS)
        w = self.strip
        self.held = [w, w // 2 + 2, w // 4 + 3, w // 8 + 3]
        self.size = [w] + [up8(h) for h in self.held[1:]]
        self.first = [0, -1, -1, -1]
        self.at = [0]
        for size in self.size:
            self.at.append(self.at[-1] + size)
        self.low_at = self.at[LEVELS]
        self.main = self.low_at + self.size[3]
        self.edge_rows = 8 * LEVELS
        self.total = self.main + 2 * self.edge_rows
        self.near = 2 * BS
        self.half = BS * BS // 2
        self.weight_at = bands * self.half
        self.code_at = self.weight_at + self.half
        order = np.arange(self.rows)
        wide = self.slot_rows
        u, half, v = order // (4 * wide), order // (2 * wide) % 2, order // wide % 2
        self.row_of = order % wide * BS + half * (BS // 2) + 2 * u + v

    def column_tables(self):
        n, m, w = self.n, self.m, self.strip
        width = m * TS
        grids = [np.eye(width)] + row_shrinks(width)
        tables = np.zeros((n, m, self.total, TS))
        for t in range(n):
            for j in range(m):
                for level in range(LEVELS):
                    base = ((j * TS + t * w) >> level) + self.first[level]
                    for k in range(self.held[level]):
                        o = base + k
                        if 0 <= o < width >> level:
                            tables[t, j, self.at[level] + k] = grids[level][o, j * TS : (j + 1) * TS]
                    for which, target in enumerate((t, t ^ n // 2)):
                        right = 2 * target < n
                        base = ((j + 1 if right else j) * TS >> level) - 1
                        at = self.main + which * self.edge_rows + 8 * (level - 1)
                        for k in range(EDGE if level else 0):
                            if 0 <= base + k < width >> level:
                                row = grids[level][base + k, j * TS : (j + 1) * TS]
                                row = row[TS - self.near :] if right else row[: self.near]
                                tables[t, j, at + k, : 2 * self.near] = np.concatenate([row, row])
        high, low = split_table(tables)
        high[:, :, self.low_at : self.main] = low[:, :, self.at[3] : self.at[4]]
        for at in (self.main + self.edge_rows, self.total):
            high[:, :, at - 8 : at] = low[:, :, at - 16 : at - 8]
        return np.concatenate([high, high], axis=-1).reshape(n * m, self.total, 2 * TS)


def halves(value):
    high = value.astype(BF)
    return high, (value - high.astype(F32)).astype(BF)


def dot2(value, table):
    high, low = halves(value)
    return jnp.dot(high, table, preferred_element_type=F32) + jnp.dot(
        low, table, preferred_element_type=F32
    )


def turned(plan, block):
    return jnp.concatenate([block[:, : plan.half], block[:, plan.half :]], axis=0).T


def pack_kernel(plan, count_ref, scenes_ref, cloud_ref, dest_ref, offset_ref, out_ref, note_ref, raw,
                dest, offset, sems):
    rows = 2 * S_DEV
    half = plan.half
    copies = [
        pltpu.make_async_copy(source, target, sems.at[k])
        for k, (source, target) in enumerate(
            (
                (dest_ref, dest),
                (offset_ref, offset),
                (cloud_ref, raw.at[plan.bands]),
                (scenes_ref, raw.at[pl.ds(0, plan.bands)]),
            )
        )
    ]
    for copy in copies:
        copy.start()
    for copy in copies[:2]:
        copy.wait()
    per_row = TS // BS
    slot = offset[...]
    code = (slot % per_row) * plan.slot_rows + dest[...] * per_row + slot // per_row
    live = lax.broadcasted_iota(jnp.int32, (1, S_DEV), 1) < count_ref[0, 0]
    code = jnp.where(live, code, DEAD).astype(F32)
    code = jnp.broadcast_to(jnp.concatenate([code, code], axis=1), (CODE_ROWS, rows))
    out_ref[plan.code_at :, :] = code.astype(BF)
    for f in (plan.bands, *range(plan.bands)):
        if f == plan.bands:
            copies[2].wait()
        elif f == 0:
            copies[3].wait()
        out_ref[f * half : (f + 1) * half, :] = turned(plan, raw[f])
    note_ref[...] = out_ref[plan.weight_at :, :]


def load_kernel(plan, column_ref, *refs):
    count = (len(refs) - 2) // 2
    sources, targets, sems = refs[:count], refs[count:-1], refs[-1]
    mine = lax.axis_index("tx") * plan.m + lax.axis_index("ty")
    copies = [
        pltpu.make_async_copy(source, target, sems.at[k])
        for k, (source, target) in enumerate(zip((column_ref.at[mine], *sources), targets))
    ]
    for copy in copies:
        copy.start()
    for copy in copies:
        copy.wait()


def landing_of(plan, codes):
    codes = codes.astype(F32).T[:, :1]
    blocks = codes.shape[0]
    pair = float(2 * plan.slot_rows)
    second = lax.broadcasted_iota(jnp.int32, (blocks, 1), 0) >= S_DEV
    codes = codes + pair * jnp.floor(codes / pair) + jnp.where(second, pair, 0.0)
    slot = lax.broadcasted_iota(jnp.int32, (blocks, 2 * plan.slots), 1).astype(F32)
    landing = jnp.where(slot == codes, 1.0, 0.0).astype(BF)
    return jnp.concatenate([landing, landing], axis=0)


def slot_sums(plan, scenes, note, prod_ref):
    half, blocks = plan.half, 2 * S_DEV
    weight = note[:half, :]
    for f in range(plan.bands):
        rows = pl.ds(f * half, half)
        if len(scenes.shape) == 3:
            value = turned(plan, scenes[f])
        else:
            value = scenes[f * half : (f + 1) * half, :]
        high, low = halves(value.astype(F32) * weight.astype(F32))
        prod_ref[rows, :blocks] = high
        prod_ref[rows, blocks:] = low
    rows = pl.ds(plan.weight_at, half)
    prod_ref[rows, :blocks] = weight
    prod_ref[rows, blocks:] = jnp.zeros_like(weight)
    return jnp.dot(prod_ref[...], landing_of(plan, note[half:, :]), preferred_element_type=F32)


def turn(plan, a, b):
    wide = plan.slot_rows
    odd = lax.broadcasted_iota(jnp.int32, a.shape, 1) // wide % 2 == 1
    return jnp.where(odd, pltpu.roll(b, wide, 1), a), jnp.where(odd, b, pltpu.roll(a, TS - wide, 1))


def twin_sum(value):
    return value + pltpu.roll(value, value.shape[-1] // 2, value.ndim - 1)


def edge_of(plan, side_ref, table, row1_ref, row23_ref, out_ref, tile_ref, z1_ref, z23_ref):
    planes = plan.bands + 1
    rows = plan.rows
    for f in range(planes):
        tile = tile_ref.at[f % 2]
        for u in range(BS // 4):
            at = f * plan.half + 2 * u * BS
            pair = turn(plan, side_ref[at : at + BS], side_ref[at + BS : at + 2 * BS])
            for k, value in enumerate(pair):
                high, low = halves(value)
                tile[k * BS : (k + 1) * BS, u * TS : (u + 1) * TS] = high
                tile[plan.near + k * BS : plan.near + (k + 1) * BS, u * TS : (u + 1) * TS] = low
        cols = jnp.dot(table, tile[...], preferred_element_type=F32)
        z1_ref[f] = cols[:8]
        z23_ref[f, :8] = cols[8:16]
        z23_ref[f, 8:] = cols[16:24] + cols[24:]
    kind = out_ref.dtype
    out_ref[...] = jnp.zeros(out_ref.shape, kind)
    z1 = dot2(z1_ref[...].reshape(planes * 8, rows), row1_ref[...])
    z1 = z1.reshape(planes, 8, rows // 2)
    z23 = dot2(z23_ref[...].reshape(planes * 16, rows), row23_ref[...])
    z23 = z23.reshape(planes, 16, rows // 2)
    second = rows // 2 + rows // 4
    for f in range(planes):
        at = pl.ds(EDGE * f, EDGE)
        out_ref[at, : rows // 2] = z1[f, :EDGE].astype(kind)
        out_ref[at, rows // 2 : second] = z23[f, :EDGE, : rows // 4].astype(kind)
        out_ref[at, second:] = twin_sum(z23[f, 8:, rows // 4 :])[:EDGE].astype(kind)


def side_of(plan, sums, right):
    return jnp.where(right, sums[:, 2 * plan.slots - TS :], sums[:, :TS])


def own_kernel(plan, pack, column_ref, row1_ref, row23_ref,
               out_ref, edge_ref, prod_ref, side_ref, tile_ref, z1_ref, z23_ref):
    right = 2 * (lax.axis_index("tx") ^ plan.n // 2) < plan.n
    sums = slot_sums(plan, pack, pack.at[pl.ds(plan.weight_at, plan.half + CODE_ROWS)], prod_ref)
    out_ref[...] = sums
    side_ref[...] = side_of(plan, sums, right)
    table = column_ref[plan.main + plan.edge_rows :, : 2 * plan.near]
    edge_of(plan, side_ref, table, row1_ref, row23_ref, edge_ref, tile_ref, z1_ref, z23_ref)


def first_kernel(plan, far, note, near, near_note, before_ref, column_ref, row1_ref, row23_ref,
                 out_ref, edge_ref, prod_ref, side_ref, tile_ref, z1_ref, z23_ref):
    right = 2 * lax.axis_index("tx") < plan.n
    sums = slot_sums(plan, near, near_note, prod_ref.at[0])
    sums = before_ref[...] + sums + slot_sums(plan, far, note, prod_ref.at[1])
    out_ref[...] = sums
    side_ref[...] = side_of(plan, sums, right)
    table = column_ref[plan.main : plan.main + plan.edge_rows, : 2 * plan.near]
    edge_of(plan, side_ref, table, row1_ref, row23_ref, edge_ref, tile_ref, z1_ref, z23_ref)


def tile_of(plan, sums, at, tile_ref):
    for pair in range(2 * plan.slots // TS):
        lanes = slice(pair * TS, (pair + 1) * TS)
        for u in range(BS // 4):
            row = at + 2 * u * BS
            both = turn(plan, sums[row : row + BS, lanes], sums[row + BS : row + 2 * BS, lanes])
            for k, value in enumerate(both):
                high, low = halves(value)
                row = (2 * pair + k) * BS
                tile_ref[row : row + BS, u * TS : (u + 1) * TS] = high
                tile_ref[TS + row : TS + row + BS, u * TS : (u + 1) * TS] = low


def place_kernel(plan, late, note, before_ref, column_ref, row1_ref, row23_ref,
                 a0_ref, a1_ref, a2_ref, a3_ref, prod_ref, sums_ref, tile_ref, z1_ref, z23_ref):
    column = column_ref[: plan.main, :]
    at, size = plan.at, plan.size
    planes = plan.bands + 1
    rows = plan.rows
    sums_ref[...] = before_ref[...] + slot_sums(plan, late, note, prod_ref)
    for f in range(planes):
        tile = tile_ref.at[f % 2]
        tile_of(plan, sums_ref, f * plan.half, tile)
        cols = jnp.dot(column, tile[...], preferred_element_type=F32)
        a0_ref[f] = cols[at[0] : at[1]]
        z1_ref[f] = cols[at[1] : at[2]]
        z23_ref[f, : size[2]] = cols[at[2] : at[3]]
        z23_ref[f, size[2] :] = cols[at[3] : at[4]] + cols[plan.low_at : plan.main]
    z1 = dot2(z1_ref[...].reshape(planes * size[1], rows), row1_ref[...])
    a1_ref[...] = z1.reshape(a1_ref.shape)
    z23 = dot2(z23_ref[...].reshape(planes * (size[2] + size[3]), rows), row23_ref[...])
    z23 = z23.reshape(planes, size[2] + size[3], rows // 2)
    a2_ref[...] = z23[:, : size[2], : rows // 4]
    for f in range(planes):
        a3_ref[f] = twin_sum(z23[f, size[2] :, rows // 4 :])


def grow_columns(value, outputs):
    half = outputs // 2
    a, b, c = value[:, :half], value[:, 1 : half + 1], value[:, 2 : half + 2]
    return (a + b) * 0.5, (a + 6.0 * b + c) * 0.125


def weave(even, odd, ref, size):
    k, half, lanes = even.shape
    if 2 * half < size:
        ref[...] = jnp.zeros(ref.shape, F32)
    for q in range(k):
        for chunk in range(lanes // TS):
            part = slice(chunk * TS, (chunk + 1) * TS)
            ref[q, chunk, pl.ds(0, half, stride=2), :] = even[q][:, part]
            ref[q, chunk, pl.ds(1, half, stride=2), :] = odd[q][:, part]
    return jnp.concatenate([ref[:, chunk] for chunk in range(lanes // TS)], axis=-1)


def blend_kernel(plan, a0_ref, a1_ref, a2_ref, a3_ref, near_ref, far_ref, grow1_ref, grow2_ref, grow3_ref,
                 natural_ref, out_ref, g1_ref, g2_ref, g3_ref, e2_ref, e1_ref, e0_ref, strip_ref, sems):
    bands = plan.bands
    planes = bands + 1
    w = plan.strip
    row_tile, col_tile = lax.axis_index("tx"), lax.axis_index("ty")
    first, last = row_tile == 0, row_tile == plan.n - 1
    left, right = first & (col_tile > 0), last & (col_tile < plan.m - 1)
    first, last = first & (col_tile == 0), last & (col_tile == plan.m - 1)
    edges = near_ref[...] + far_ref[...].astype(F32)
    start = 0
    for level, (src, dst) in enumerate(((a1_ref, g1_ref), (a2_ref, g2_ref), (a3_ref, g3_ref)), 1):
        lanes = src.shape[-1]
        dst[...] = src[...]
        for f in range(planes):
            edge = edges[EDGE * f : EDGE * (f + 1), start : start + lanes]
            far = w >> level
            dst[f, :EDGE] += jnp.where(left, edge, 0.0)
            dst[f, far : far + EDGE] += jnp.where(right, edge, 0.0)
        start += lanes

    def inside(level, columns):
        column = lax.broadcasted_iota(jnp.int32, (columns, 1), 0) - 1
        keep = ((column >= 0) | ~first) & ((column < (w >> level)) | ~last)
        return keep.astype(F32)

    def grown(level, value, up_ref):
        k, c, r = value.shape
        if level == 0:
            half = w // 2
            x, y, z = value[:, :half], value[:, 1 : half + 1], value[:, 2 : half + 2]
            tall = weave((x + 6.0 * y + z) * 0.125, (y + z) * 0.5, up_ref, w)
            return dot2(tall.reshape(k * w, r), grow1_ref[...]).reshape(k, w, plan.rows)
        grow_ref = (grow2_ref, grow3_ref)[level - 1]
        wide = dot2(value.reshape(k * c, r), grow_ref[...])
        wide = wide.reshape(k, c, wide.shape[-1])
        pairs = min(up8(plan.held[level]) // 2, c - 2)
        return weave(*grow_columns(wide, 2 * pairs), up_ref, plan.size[level])

    e2a_ref, e1a_ref, e0a_ref = (ref.at[pl.ds(0, bands)] for ref in (e2_ref, e1_ref, e0_ref))
    e2b_ref, e1b_ref, e0b_ref = (ref.at[pl.ds(bands, bands)] for ref in (e2_ref, e1_ref, e0_ref))
    inverses = [1.0 / (BACKGROUND + ref[bands]) for ref in (a0_ref, g1_ref, g2_ref, g3_ref)]
    blend = g3_ref[:bands] * inverses[3]
    detail2 = (g2_ref[:bands] - grown(2, g3_ref[:bands], e2a_ref)) * inverses[2]
    blend = (detail2 + grown(2, blend, e2b_ref)) * inside(2, plan.size[2])
    detail1 = (g1_ref[:bands] - grown(1, g2_ref[:bands], e1a_ref)) * inverses[1]
    blend = (detail1 + grown(1, blend, e1b_ref)) * inside(1, plan.size[1])
    detail0 = (a0_ref[:bands] - grown(0, g1_ref[:bands], e0a_ref)) * inverses[0]
    up = grown(0, blend, e0b_ref)
    copies = []
    part = bands // 2
    for f in range(0, bands, part):
        value = detail0[f : f + part] + up[f : f + part]
        value = value.astype(BF).reshape(part * w, plan.rows)
        value = jnp.dot(value, natural_ref[...], preferred_element_type=F32)
        strip_ref[pl.ds(f, part)] = value.astype(BF).reshape(part, w, plan.rows)
        copies.append(
            pltpu.make_async_copy(
                strip_ref.at[pl.ds(f, part)], out_ref.at[pl.ds(f, part)], sems.at[len(copies)]
            )
        )
        copies[-1].start()
    for copy in copies:
        copy.wait()


def on_chip(value):
    return pltpu.with_memory_space_constraint(value, pltpu.VMEM)


def off_chip(value):
    return pltpu.with_memory_space_constraint(value, pltpu.HBM)


def strip_local(scenes, cloud, destination, offset, counts):
    n, m = lax.axis_size("tx"), lax.axis_size("ty")
    bands = scenes.shape[2]
    plan = Plan(n, m, bands)
    planes = bands + 1
    area = BS * BS
    vmem = pl.BlockSpec(memory_space=pltpu.VMEM)
    smem = pl.BlockSpec(memory_space=pltpu.SMEM)
    hbm = pl.BlockSpec(memory_space=pl.ANY)
    blocks = jnp.swapaxes(scenes[0], 0, 1)

    def call(kernel, operands, outputs, scratch=(), flops=0, out_specs=None):
        return pl.pallas_call(
            functools.partial(kernel, plan),
            out_shape=outputs,
            in_specs=[vmem] * len(operands),
            out_specs=out_specs or jax.tree.map(lambda _: vmem, outputs),
            scratch_shapes=list(scratch),
            compiler_params=pltpu.CompilerParams(vmem_limit_bytes=16 << 20),
            cost_estimate=pl.CostEstimate(flops=flops, bytes_accessed=1 << 20, transcendentals=0),
        )(*[on_chip(v) for v in operands])

    shrinks = row_shrinks(plan.rows)
    row1 = shrinks[0].T[plan.row_of]
    row2 = shrinks[1].T[plan.row_of]
    top = plan.rows >> 3
    wide_top = 2 * top
    row23 = np.concatenate([row2, *split_table(shrinks[2].T[plan.row_of])], axis=1)
    grow3 = np.zeros((wide_top, plan.rows >> 2))
    grow3[:top] = grow_grid(top).T
    grow2 = grow_grid(plan.rows >> 2).T
    grow1 = grow_grid(plan.rows >> 1).T[:, plan.row_of]
    natural = np.eye(plan.rows)[plan.row_of]
    constants = [plan.column_tables(), row1, row23, grow1, grow2, grow3, natural]
    constants = [off_chip(jnp.asarray(table.astype(BF))) for table in constants]
    loaded = pl.pallas_call(
        functools.partial(load_kernel, plan),
        out_shape=[pltpu.VMEM(c.shape[k == 0 :], BF) for k, c in enumerate(constants)],
        in_specs=[hbm] * len(constants),
        out_specs=[vmem] * len(constants),
        scratch_shapes=[pltpu.SemaphoreType.DMA((len(constants),))],
        compiler_params=pltpu.CompilerParams(vmem_limit_bytes=4 << 20),
        name="load",
    )(*constants)
    tables, grows = list(loaded[:3]), list(loaded[3:])
    size = plan.size
    shapes = [
        (planes, size[0], plan.rows),
        (planes, size[1], plan.rows >> 1),
        (planes, size[2], plan.rows >> 2),
        (planes, size[3], wide_top),
    ]
    edge_shape = (up8(EDGE * planes), sum(s[-1] for s in shapes[1:]))
    sums_shape = pltpu.VMEM((planes * plan.half, 2 * plan.slots), F32)
    prod_shape = (planes * plan.half, 4 * S_DEV)
    work = 2 * planes * area * plan.slots * 2 * S_DEV

    across = [(i, n - 1 - i) for i in range(n)]
    beside = [(i, i ^ 1) for i in range(n)]
    far = lax.ppermute(blocks, "tx", across)
    near = lax.ppermute(blocks, "tx", beside)
    pack, note = pl.pallas_call(
        functools.partial(pack_kernel, plan),
        out_shape=[
            pltpu.VMEM((plan.code_at + CODE_ROWS, 2 * S_DEV), BF),
            pltpu.VMEM((plan.half + CODE_ROWS, 2 * S_DEV), BF),
        ],
        in_specs=[smem] + [hbm] * 4,
        out_specs=[vmem] * 2,
        scratch_shapes=[
            pltpu.VMEM((planes, S_DEV, area), BF),
            pltpu.VMEM(destination.shape, jnp.int32),
            pltpu.VMEM(offset.shape, jnp.int32),
            pltpu.SemaphoreType.DMA((4,)),
        ],
        compiler_params=pltpu.CompilerParams(vmem_limit_bytes=4 << 20),
        name="pack",
    )(counts, *[off_chip(v) for v in (blocks, cloud[0], destination, offset)])

    far_note = lax.ppermute(note, "tx", across)
    near_note = lax.ppermute(note, "tx", beside)
    edge_work = [
        pltpu.VMEM((planes * plan.half, TS), F32),
        pltpu.VMEM((2, 2 * plan.near, plan.rows), BF),
        pltpu.VMEM((planes, 8, plan.rows), F32),
        pltpu.VMEM((planes, 16, plan.rows), F32),
    ]
    sums, edge_far = call(
        own_kernel,
        [pack] + tables,
        [sums_shape, pltpu.VMEM(edge_shape, BF)],
        [pltpu.VMEM(prod_shape, BF)] + edge_work,
        flops=work,
    )

    def over(value, shift):
        pairs = []
        for t in range(n):
            for j in range(m):
                target = t ^ shift
                pairs.append((t * m + j, target * m + (j + 1 if 2 * target < n else j - 1) % m))
        return lax.ppermute(value, ("tx", "ty"), pairs)

    edge_far = over(edge_far, n // 2)
    late = lax.ppermute(far, "tx", beside)
    late_note = lax.ppermute(far_note, "tx", beside)
    sums, edge_near = call(
        first_kernel,
        [far, far_note, near, near_note, sums] + tables,
        [sums_shape, pltpu.VMEM(edge_shape, F32)],
        [pltpu.VMEM((2, *prod_shape), BF)] + edge_work,
        flops=4 * work,
    )
    edge_near = over(edge_near, 0)
    levels = call(
        place_kernel,
        [late, late_note, sums] + tables,
        [pltpu.VMEM(s, F32) for s in shapes],
        [
            pltpu.VMEM(prod_shape, BF),
            pltpu.VMEM(sums_shape.shape, F32),
            pltpu.VMEM((2, 2 * TS, plan.rows), BF),
            pltpu.VMEM((planes, size[1], plan.rows), F32),
            pltpu.VMEM((planes, size[2] + size[3], plan.rows), F32),
        ],
        flops=4 * work,
    )
    out = call(
        blend_kernel,
        [*levels, edge_near, edge_far, *grows],
        jax.ShapeDtypeStruct((bands, size[0], plan.rows), BF),
        [
            pltpu.VMEM(shapes[1], F32),
            pltpu.VMEM(shapes[2], F32),
            pltpu.VMEM(shapes[3], F32),
            pltpu.VMEM((2 * bands, (plan.rows >> 2) // TS, size[2], TS), F32),
            pltpu.VMEM((2 * bands, (plan.rows >> 1) // TS, size[1], TS), F32),
            pltpu.VMEM((2 * bands, (plan.rows >> 1) // TS, size[0], TS), F32),
            pltpu.VMEM((bands, size[0], plan.rows), BF),
            pltpu.SemaphoreType.DMA((2,)),
        ],
        flops=4 * work,
        out_specs=hbm,
    )
    return out[:, None]


def strip_step(*arguments):
    return strip_local(*arguments)


def use_strips(n, m):
    spread = max(2, 2 * S_DEV // n)
    return n == 4 and TS // n >= 32 and m >= 2 and S_DEV <= 2 * spread


def solution(mesh):
    placed = (
        P(("region", "ty"), "tx", "band", None),
        P(("region", "ty"), "tx", None),
        P(("region", "ty"), "tx"),
        P(("region", "ty"), "tx"),
        P(("region", "ty"), "tx"),
    )
    strips = use_strips(mesh.shape["tx"], mesh.shape["ty"])
    return jax.shard_map(
        strip_step if strips else local,
        mesh=mesh,
        in_specs=placed,
        out_specs=P("band", ("region", "ty"), "tx", None),
        check_vma=False,
    )
```
